256 devices in a mesh: inst: 8 (over y_hi, x), space: 32 (over z, y_lo, core).
Axes of the slice: x: 4, y: 4 (y_hi: 2, y_lo: 2; y = y_hi * 2 + y_lo), z: 8, core: 2. Of those that a mesh axis runs over, the one named last changes fastest.
Arguments:
- psi_start: float32 [5, 8, 256, 1024], P(None, 'inst', 'space'), may hold values from -6 to 6
- density: float32 [8, 256, 1024], P('inst', 'space'), may hold values from 0.8 to 1.25
- velocity: float32 [3, 8, 256, 1024], P(None, 'inst', 'space'), may hold values from -0.6 to 0.6
- pressure: float32 [8, 256, 1024], P('inst', 'space'), may hold values from 0.5 to 1
- obs_pos: float32 [3, 512], P(None, 'space'), may hold values from -16 to 16, as said below
- obs_weight: float32 [2, 512], P(None, 'space'), may hold values from -0.6 to 0.6
- obs_harmonic: int32 [512], P('space'), may hold values from 1 to 3
- panel_pos: float32 [3, 65536], replicated, may hold values from -1 to 1
- panel_normal: float32 [3, 65536], P(None, 'space'), may hold values from -5 to 5
- panel_cell: int32 [65536], P('space'), may hold values from 0 to 8191
- plane_nbr: int32 [4, 1024], replicated, may hold values from 0 to 1023
Outputs:
- adjoint: float32 [5, 8, 256, 1024], P(None, 'inst', 'space')
The draws below stay inside these ranges and needn't reach their ends.
Inputs may be any that keep to these rules, and one draw needn't show every extreme that they name: `obs_pos`: observers lie between 8 and 16 from the anchor, outside the panels' cube. panel_cell[q] is an index into the 8 x 1024 cells of the slot's owner, layer panel_cell[q] // 1024.
All inputs are finite; a program needn't handle non-finite values.
Results may differ from the reference program's by a relative error of at most 0.0001.
Values sent between devices are 32-bit elements; how exact they have to be, the bound alone decides.
A program may use at most 64 MiB of HBM per device.

```python
import math
import jax
import jax.numpy as jnp
from jax import lax

CA = 8
CB = 1024
PROW_DEV = 16
ITERS = 3
INST = 8
NXG = 256
SURFACE_PANELS = 65536
OBS = 512


def draw_obs_pos(key, part):
    first, second, third = jax.random.split(jax.random.fold_in(key, 11), 3)
    polar = jax.random.uniform(first, (OBS,), jnp.float32, 0.3, 2.8)
    azimuth = jax.random.uniform(second, (OBS,), jnp.float32, -math.pi, math.pi)
    radius = jax.random.uniform(third, (OBS,), jnp.float32, 8.0, 16.0)
    return jnp.stack([radius * jnp.sin(polar) * jnp.cos(azimuth), radius * jnp.sin(polar) * jnp.sin(azimuth), radius * jnp.cos(polar)]).astype(jnp.float32)


def set_ends(array, rng, least, largest):
    place = [jax.random.randint(jax.random.fold_in(rng, axis), (), 0, length) for axis, length in enumerate(array.shape)]
    longest = array.shape.index(max(array.shape))
    next_to = place[:longest] + [(place[longest] + 1) % array.shape[longest]] + place[longest + 1:]
    return array.at[tuple(place)].set(least).at[tuple(next_to)].set(largest)


def level_of(key, shape, pieces, least, largest):
    factor_of, own = 1.0, jax.random.fold_in(key, 6)
    for axis_at, parts in pieces:
        heights = jnp.exp(jax.random.uniform(jax.random.fold_in(own, axis_at), (parts,), jnp.float32, least / len(pieces), largest / len(pieces)))
        factor_of = factor_of * jnp.repeat(heights, shape[axis_at] // parts).reshape([-1 if axis == axis_at else 1 for axis in range(len(shape))])
    return factor_of


def scatter_about(stream_key, shape, scale, limit, pieces=(), kind=jnp.bfloat16):
    level = level_of(stream_key, shape, pieces, -0.22, 0.18) if pieces else 1.0
    values = jax.random.normal(stream_key, shape, jnp.float32) * scale * level
    return jnp.minimum(jnp.maximum(values, -limit), limit).astype(kind)


def setup_inputs(seed: int = 0) -> dict:
    keys = jax.random.split(jax.random.key(seed), 12)
    return {
        "psi_start": scatter_about(keys[0], (5, INST, NXG, CB), 1.0, 6.0, ((1, 8), (2, 32)), jnp.float32),
        "density": jnp.clip(0.8 + 0.45 * jax.random.uniform(keys[1], (INST, NXG, CB), jnp.float32) ** level_of(keys[1], (INST, NXG, CB), ((0, 8), (1, 32)), -0.2, 0.2), 0.8, 1.25),
        "velocity": jnp.clip(jax.random.uniform(keys[2], (3, INST, NXG, CB), jnp.float32, -0.6, 0.6) * level_of(keys[2], (3, INST, NXG, CB), ((1, 8), (2, 32)), -0.4, 0.0), -0.6, 0.6),
        "pressure": jnp.clip(0.5 + 0.5 * jax.random.uniform(keys[3], (INST, NXG, CB), jnp.float32) ** level_of(keys[3], (INST, NXG, CB), ((0, 8), (1, 32)), -0.2, 0.2), 0.5, 1.0),
        "obs_pos": draw_obs_pos(jax.random.fold_in(keys[11], 71), 0),
        "obs_weight": scatter_about(keys[5], (2, OBS), 0.1, 0.6, ((1, 32),), jnp.float32),
        "obs_harmonic": set_ends(jax.random.randint(keys[6], (OBS,), 1, 4), jax.random.fold_in(keys[6], 1), 1, 3).astype(jnp.int32),
        "panel_pos": jnp.clip(jax.random.uniform(keys[7], (3, SURFACE_PANELS), jnp.float32, -1.0, 1.0), -1.0, 1.0),
        "panel_normal": scatter_about(keys[8], (3, SURFACE_PANELS), 1.0, 5.0, ((1, 32),), jnp.float32),
        "panel_cell": set_ends(jax.random.randint(keys[9], (SURFACE_PANELS,), 0, CA * CB), jax.random.fold_in(keys[9], 1), 0, (CA * CB) - 1).astype(jnp.int32),
        "plane_nbr": set_ends(jax.random.randint(keys[10], (4, CB), 0, CB), jax.random.fold_in(keys[10], 1), 0, CB - 1).astype(jnp.int32),
    }


GAMMA = 1.4
KWAVE = 0.7
RADIUS = 10.0
TAU = 0.05
DISSIP = 0.25
OMEGA = 1.5
VISCO = 0.5

def panel_block(observers, panels, time_now):
    delta = panels[:, None, :] - observers[:3, :, None]
    dist2 = lax.optimization_barrier(jnp.sum(delta * delta, axis=0))
    dist = jnp.sqrt(dist2)
    harm = observers[5][:, None]
    phase = harm * (time_now - KWAVE * dist)
    amp = (observers[3][:, None] * jnp.cos(phase) + observers[4][:, None] * jnp.sin(phase)) * (RADIUS * RADIUS) / (dist2 * dist)
    return lax.optimization_barrier(jnp.sum(amp[None] * delta, axis=1))

def sensitivity(observers, panels, time_now):
    count = panels.shape[1]
    obs_count = observers.shape[1]
    block = math.gcd(count, max(128, 262144 // obs_count))
    split = panels.reshape(3, count // block, block).transpose(1, 0, 2)
    out = lax.map(lambda piece: panel_block(observers, piece, time_now), split)
    return out.transpose(1, 0, 2).reshape(3, count)

def conserved(density, velocity, pressure):
    moment = density[None] * velocity
    energy = pressure / (GAMMA - 1.0) + 0.5 * density * lax.optimization_barrier(jnp.sum(velocity * velocity, axis=0))
    return jnp.concatenate([density[None], moment, energy[None]], axis=0)

def fluxes(state):
    dens = state[0]
    moment = state[1:4]
    energy = state[4]
    vel = moment / dens
    press = (GAMMA - 1.0) * (energy - 0.5 * lax.optimization_barrier(jnp.sum(moment * vel, axis=0)))
    result = []
    for axis_d in range(3):
        comps = [moment[axis_d]]
        for axis_e in range(3):
            term = moment[axis_e] * vel[axis_d]
            if axis_e == axis_d:
                term = term + press
            comps.append(term)
        comps.append((energy + press) * vel[axis_d])
        result.append(jnp.stack(comps))
    return tuple(result)

def spectral_coeff(offset, count):
    safe = jnp.where(offset == 0, 1.0, offset)
    angle = math.pi * safe / count
    even_odd_flag = 1.0 - 2.0 * jnp.mod(safe, 2.0)
    other = -(OMEGA / 2.0) * even_odd_flag * jnp.cos(angle) / jnp.sin(angle) + VISCO * (OMEGA * OMEGA / 2.0) * even_odd_flag / jnp.sin(angle) ** 2
    return jnp.where(offset == 0, VISCO * OMEGA * OMEGA * (count * count + 2.0) / 12.0, other)

def reference(psi_start, density, velocity, pressure, obs_pos, obs_weight, obs_harmonic, panel_pos, panel_normal, panel_cell, plane_nbr):
    observers = jnp.concatenate([obs_pos, obs_weight, obs_harmonic[None].astype(jnp.float32)], axis=0)
    owners = jnp.arange(SURFACE_PANELS, dtype=jnp.int32) // (PROW_DEV * 128)
    flat = owners * (CA * CB) + panel_cell
    walls = []
    for inst_id in range(INST):
        time_now = 2.0 * math.pi * inst_id / INST
        sens = sensitivity(observers, panel_pos, time_now)
        weight = lax.optimization_barrier(jnp.sum(sens * panel_normal, axis=0))
        walls.append(jax.ops.segment_sum(weight, flat, num_segments=NXG * CB).reshape(NXG, CB))
    wall = jnp.stack(walls)
    state = conserved(density, velocity, pressure)
    slope = jnp.concatenate([0.5 * lax.optimization_barrier(jnp.sum(velocity * velocity, axis=0))[None], -velocity, jnp.ones_like(density)[None]], axis=0) * (GAMMA - 1.0)
    source = slope * wall[None]
    _, pull = jax.vjp(fluxes, state)
    rows = jnp.arange(INST)[:, None]
    cols = jnp.arange(INST)[None, :]
    coupling = spectral_coeff(jnp.mod(rows - cols, INST).astype(jnp.float32), float(INST))
    psi = psi_start
    for step in range(ITERS):
        minus_a = jnp.roll(psi, 1, axis=2)
        plus_a = jnp.roll(psi, -1, axis=2)
        plus_y = jnp.take(psi, plane_nbr[0], axis=3)
        minus_y = jnp.take(psi, plane_nbr[1], axis=3)
        plus_z = jnp.take(psi, plane_nbr[2], axis=3)
        minus_z = jnp.take(psi, plane_nbr[3], axis=3)
        middle_point = pull((0.5 * (minus_a - plus_a), 0.5 * (minus_y - plus_y), 0.5 * (minus_z - plus_z)))[0]
        spread = 6.0 * psi - (minus_a + plus_a + plus_y + minus_y + plus_z + minus_z)
        spectral_operator = jnp.einsum('ij,vjab->viab', coupling, psi, precision=lax.Precision.HIGHEST)
        psi = psi - TAU * (middle_point + DISSIP * spread + spectral_operator + source)
    return psi
```

```python
import math

import jax
import jax.numpy as jnp
from jax import lax
from jax.sharding import PartitionSpec as P

ITERS = 3


GAMMA = 1.4
KWAVE = 0.7
RADIUS = 10.0
TAU = 0.05
DISSIP = 0.25
OMEGA = 1.5
VISCO = 0.5


def padded_2(cells, sides, width):
    for axis, dim in sides:
        count = lax.axis_size(axis)
        head = lax.slice_in_dim(cells, 0, width, axis=dim)
        tail = lax.slice_in_dim(cells, cells.shape[dim] - width, cells.shape[dim], axis=dim)
        cells = jnp.concatenate(
            [
                lax.ppermute(tail, axis, [(i, (i + 1) % count) for i in range(count)]),
                cells,
                lax.ppermute(head, axis, [((i + 1) % count, i) for i in range(count)]),
            ],
            axis=dim,
        )
    return cells


def panel_block(observers, panels, time_now):
    delta = panels[:, None, :] - observers[:3, :, None]
    dist2 = jnp.sum(delta * delta, axis=0)
    dist = jnp.sqrt(dist2)
    harm = observers[5][:, None]
    phase = harm * (time_now - KWAVE * dist)
    amp = (
        (observers[3][:, None] * jnp.cos(phase) + observers[4][:, None] * jnp.sin(phase))
        * (RADIUS * RADIUS)
        / (dist2 * dist)
    )
    return jnp.sum(amp[None] * delta, axis=1)


def sensitivity(observers, panels, time_now):
    count = panels.shape[1]
    obs_count = observers.shape[1]
    block = math.gcd(count, max(128, 262144 // obs_count))
    split = panels.reshape(3, count // block, block).transpose(1, 0, 2)
    out = lax.map(lambda piece: panel_block(observers, piece, time_now), split)
    return out.transpose(1, 0, 2).reshape(3, count)


def conserved(density, velocity, pressure):
    moment = density[None] * velocity
    energy = pressure / (GAMMA - 1.0) + 0.5 * density * jnp.sum(velocity * velocity, axis=0)
    return jnp.concatenate([density[None], moment, energy[None]], axis=0)


def fluxes(state):
    dens = state[0]
    moment = state[1:4]
    energy = state[4]
    vel = moment / dens
    press = (GAMMA - 1.0) * (energy - 0.5 * jnp.sum(moment * vel, axis=0))
    result = []
    for axis_d in range(3):
        comps = [moment[axis_d]]
        for axis_e in range(3):
            term = moment[axis_e] * vel[axis_d]
            if axis_e == axis_d:
                term = term + press
            comps.append(term)
        comps.append((energy + press) * vel[axis_d])
        result.append(jnp.stack(comps))
    return tuple(result)


def spectral_coeff(offset, count):
    safe = jnp.where(offset == 0, 1.0, offset)
    angle = math.pi * safe / count
    even_odd_flag = 1.0 - 2.0 * jnp.mod(safe, 2.0)
    other = (
        -(OMEGA / 2.0) * even_odd_flag * jnp.cos(angle) / jnp.sin(angle)
        + VISCO * (OMEGA * OMEGA / 2.0) * even_odd_flag / jnp.sin(angle) ** 2
    )
    return jnp.where(offset == 0, VISCO * OMEGA * OMEGA * (count * count + 2.0) / 12.0, other)


def split_three(values):
    high = lax.reduce_precision(values, exponent_bits=8, mantissa_bits=7)
    rest = values - high
    middle = lax.reduce_precision(rest, exponent_bits=8, mantissa_bits=7)
    low = rest - middle
    return jnp.stack([high, middle, low]).astype(jnp.bfloat16)


def plane_gather(psi, onehot):
    comps, layers, plane = psi.shape
    parts = split_three(psi.reshape(comps * layers, plane))
    picked = jnp.einsum("pra,kba->kprb", parts, onehot,
                        preferred_element_type=jnp.float32)
    picked = (picked[:, 0] + picked[:, 1]) + picked[:, 2]
    return picked.reshape(onehot.shape[0], comps, layers, plane)


def shards(
    psi_start,
    density,
    velocity,
    pressure,
    obs_pos,
    obs_weight,
    obs_harmonic,
    panel_pos,
    panel_normal,
    panel_cell,
    plane_nbr,
):
    inst_count = lax.axis_size("inst")
    inst_id = lax.axis_index("inst")
    space_id = lax.axis_index("space")
    times = jnp.array([2.0 * math.pi * i / inst_count for i in range(inst_count)], jnp.float32)
    time_now = times[inst_id]
    local_obs = jnp.concatenate(
        [obs_pos, obs_weight, obs_harmonic[None].astype(jnp.float32)], axis=0
    )
    observers = lax.all_gather(local_obs, "space", axis=1, tiled=True)
    owned_count = panel_normal.shape[1]
    mine = lax.dynamic_slice_in_dim(panel_pos, space_id * owned_count, owned_count, 1)
    delta = mine[:, None, :] - observers[:3, :, None]
    dist2 = jnp.sum(delta * delta, axis=0)
    dist = jnp.sqrt(dist2)
    phase = observers[5][:, None] * (time_now - KWAVE * dist)
    amp = (
        (observers[3][:, None] * jnp.cos(phase) + observers[4][:, None] * jnp.sin(phase))
        * (RADIUS * RADIUS)
        / (dist2 * dist)
    )
    along = jnp.sum(delta * panel_normal[:, None, :], axis=0)
    weight = jnp.sum(amp * along, axis=0)
    layers = psi_start.shape[2]
    plane = psi_start.shape[3]
    wall = jax.ops.segment_sum(weight, panel_cell, num_segments=layers * plane).reshape(
        layers, plane
    )
    dens = density[0]
    vel = velocity[:, 0]
    state = conserved(dens, vel, pressure[0])
    slope = jnp.concatenate(
        [0.5 * jnp.sum(vel * vel, axis=0)[None], -vel, jnp.ones_like(dens)[None]], axis=0
    ) * (GAMMA - 1.0)
    source = slope * wall[None]
    _, pull = jax.vjp(fluxes, state)
    onehot = (plane_nbr[:, :, None] == jnp.arange(plane, dtype=jnp.int32)[None, None, :]).astype(
        jnp.bfloat16
    )
    others = jnp.arange(inst_count, dtype=jnp.int32)
    row_entry = spectral_coeff(
        jnp.mod(inst_id - others, inst_count).astype(jnp.float32), float(inst_count)
    )
    psi = psi_start[:, 0]
    for step in range(ITERS):
        padded = padded_2(psi, (("space", 1),), 1)
        minus_a = padded[:, :-2]
        plus_a = padded[:, 2:]
        plus_y, minus_y, plus_z, minus_z = plane_gather(psi, onehot)
        middle_point = pull(
            (0.5 * (minus_a - plus_a), 0.5 * (minus_y - plus_y), 0.5 * (minus_z - plus_z))
        )[0]
        spread = 6.0 * psi - (minus_a + plus_a + plus_y + minus_y + plus_z + minus_z)
        every_instant = lax.all_gather(psi[:, None], "inst", axis=1, tiled=True)
        spectral_operator = jnp.einsum(
            "c,kcyo->kyo", row_entry, every_instant, precision=lax.Precision.HIGHEST
        )
        psi = psi - TAU * (middle_point + DISSIP * spread + spectral_operator + source)
    return psi[:, None]


def solution(mesh):
    placed = (
        P(None, "inst", "space", None),
        P("inst", "space", None),
        P(None, "inst", "space", None),
        P("inst", "space", None),
        P(None, "space"),
        P(None, "space"),
        P("space"),
        P(),
        P(None, "space"),
        P("space"),
        P(),
    )
    return jax.shard_map(
        shards,
        mesh=mesh,
        in_specs=placed,
        out_specs=P(None, "inst", "space", None),
        check_vma=False,
    )
```

```python
import math

import jax
import jax.numpy as jnp
from jax import lax
from jax.sharding import PartitionSpec as P

ITERS = 3


GAMMA = 1.4
KWAVE = 0.7
RADIUS = 10.0
TAU = 0.05
DISSIP = 0.25
OMEGA = 1.5
VISCO = 0.5


def padded_2(cells, sides, width):
    for axis, dim in sides:
        count = lax.axis_size(axis)
        head = lax.slice_in_dim(cells, 0, width, axis=dim)
        tail = lax.slice_in_dim(cells, cells.shape[dim] - width, cells.shape[dim], axis=dim)
        cells = jnp.concatenate(
            [
                lax.ppermute(tail, axis, [(i, (i + 1) % count) for i in range(count)]),
                cells,
                lax.ppermute(head, axis, [((i + 1) % count, i) for i in range(count)]),
            ],
            axis=dim,
        )
    return cells


def panel_block(observers, panels, time_now):
    delta = panels[:, None, :] - observers[:3, :, None]
    dist2 = jnp.sum(delta * delta, axis=0)
    dist = jnp.sqrt(dist2)
    harm = observers[5][:, None]
    phase = harm * (time_now - KWAVE * dist)
    amp = (
        (observers[3][:, None] * jnp.cos(phase) + observers[4][:, None] * jnp.sin(phase))
        * (RADIUS * RADIUS)
        / (dist2 * dist)
    )
    return jnp.sum(amp[None] * delta, axis=1)


def sensitivity(observers, panels, time_now):
    count = panels.shape[1]
    obs_count = observers.shape[1]
    block = math.gcd(count, max(128, 262144 // obs_count))
    split = panels.reshape(3, count // block, block).transpose(1, 0, 2)
    out = lax.map(lambda piece: panel_block(observers, piece, time_now), split)
    return out.transpose(1, 0, 2).reshape(3, count)


def conserved(density, velocity, pressure):
    moment = density[None] * velocity
    energy = pressure / (GAMMA - 1.0) + 0.5 * density * jnp.sum(velocity * velocity, axis=0)
    return jnp.concatenate([density[None], moment, energy[None]], axis=0)


def fluxes(state):
    dens = state[0]
    moment = state[1:4]
    energy = state[4]
    vel = moment / dens
    press = (GAMMA - 1.0) * (energy - 0.5 * jnp.sum(moment * vel, axis=0))
    result = []
    for axis_d in range(3):
        comps = [moment[axis_d]]
        for axis_e in range(3):
            term = moment[axis_e] * vel[axis_d]
            if axis_e == axis_d:
                term = term + press
            comps.append(term)
        comps.append((energy + press) * vel[axis_d])
        result.append(jnp.stack(comps))
    return tuple(result)


def spectral_coeff(offset, count):
    safe = jnp.where(offset == 0, 1.0, offset)
    angle = math.pi * safe / count
    even_odd_flag = 1.0 - 2.0 * jnp.mod(safe, 2.0)
    other = (
        -(OMEGA / 2.0) * even_odd_flag * jnp.cos(angle) / jnp.sin(angle)
        + VISCO * (OMEGA * OMEGA / 2.0) * even_odd_flag / jnp.sin(angle) ** 2
    )
    return jnp.where(offset == 0, VISCO * OMEGA * OMEGA * (count * count + 2.0) / 12.0, other)


def split_three(values):
    high = lax.reduce_precision(values, exponent_bits=8, mantissa_bits=7)
    rest = values - high
    middle = lax.reduce_precision(rest, exponent_bits=8, mantissa_bits=7)
    low = rest - middle
    return jnp.stack([high, middle, low]).astype(jnp.bfloat16)


def plane_gather(psi, onehot):
    comps, layers, plane = psi.shape
    parts = split_three(psi.reshape(comps * layers, plane))
    picked = jnp.einsum("pra,kba->kprb", parts, onehot,
                        preferred_element_type=jnp.float32)
    picked = (picked[:, 0] + picked[:, 1]) + picked[:, 2]
    return picked.reshape(onehot.shape[0], comps, layers, plane)


def cell_sum(weight, cell, layers, plane):
    by_layer = (cell // plane)[None, :] == jnp.arange(layers, dtype=jnp.int32)[:, None]
    spread = jnp.where(by_layer, weight[None, :], 0.0)
    picks = ((cell % plane)[:, None] == jnp.arange(plane, dtype=jnp.int32)[None, :]).astype(
        jnp.bfloat16
    )
    parts = split_three(spread)
    summed = jnp.einsum("plq,qb->plb", parts, picks, preferred_element_type=jnp.float32)
    return (summed[0] + summed[1]) + summed[2]


def instance_coupling(psi, row_entry):
    count = lax.axis_size("inst")
    me = lax.axis_index("inst")
    inner = 4 if count % 4 == 0 else count
    outer = count // inner
    me_hi, me_lo = me // inner, me % inner
    total = row_entry[0] * psi
    for hi in range(outer):
        for lo in range(inner):
            if hi == 0 and lo == 0:
                continue
            pairs = [
                (a * inner + b, ((a + hi) % outer) * inner + (b + lo) % inner)
                for a in range(outer)
                for b in range(inner)
            ]
            got = lax.ppermute(psi, "inst", pairs)
            source = ((me_hi - hi) % outer) * inner + (me_lo - lo) % inner
            total = total + row_entry[(me - source) % count] * got
    return total


def shards(
    psi_start,
    density,
    velocity,
    pressure,
    obs_pos,
    obs_weight,
    obs_harmonic,
    panel_pos,
    panel_normal,
    panel_cell,
    plane_nbr,
):
    inst_count = lax.axis_size("inst")
    inst_id = lax.axis_index("inst")
    space_id = lax.axis_index("space")
    times = jnp.array([2.0 * math.pi * i / inst_count for i in range(inst_count)], jnp.float32)
    time_now = times[inst_id]
    local_obs = jnp.concatenate(
        [obs_pos, obs_weight, obs_harmonic[None].astype(jnp.float32)], axis=0
    )
    observers = lax.all_gather(local_obs, "space", axis=1, tiled=True)
    owned_count = panel_normal.shape[1]
    mine = lax.dynamic_slice_in_dim(panel_pos, space_id * owned_count, owned_count, 1)
    delta = mine[:, None, :] - observers[:3, :, None]
    dist2 = jnp.sum(delta * delta, axis=0)
    dist = jnp.sqrt(dist2)
    phase = observers[5][:, None] * (time_now - KWAVE * dist)
    amp = (
        (observers[3][:, None] * jnp.cos(phase) + observers[4][:, None] * jnp.sin(phase))
        * (RADIUS * RADIUS)
        / (dist2 * dist)
    )
    along = jnp.sum(delta * panel_normal[:, None, :], axis=0)
    weight = jnp.sum(amp * along, axis=0)
    layers = psi_start.shape[2]
    plane = psi_start.shape[3]
    wall = cell_sum(weight, panel_cell, layers, plane)
    dens = density[0]
    vel = velocity[:, 0]
    state = conserved(dens, vel, pressure[0])
    slope = jnp.concatenate(
        [0.5 * jnp.sum(vel * vel, axis=0)[None], -vel, jnp.ones_like(dens)[None]], axis=0
    ) * (GAMMA - 1.0)
    source = slope * wall[None]
    _, pull = jax.vjp(fluxes, state)
    onehot = (plane_nbr[:, :, None] == jnp.arange(plane, dtype=jnp.int32)[None, None, :]).astype(
        jnp.bfloat16
    )
    row_entry = spectral_coeff(
        jnp.arange(inst_count, dtype=jnp.int32).astype(jnp.float32), float(inst_count)
    )
    psi = psi_start[:, 0]
    for step in range(ITERS):
        padded = padded_2(psi, (("space", 1),), 1)
        minus_a = padded[:, :-2]
        plus_a = padded[:, 2:]
        plus_y, minus_y, plus_z, minus_z = plane_gather(psi, onehot)
        middle_point = pull(
            (0.5 * (minus_a - plus_a), 0.5 * (minus_y - plus_y), 0.5 * (minus_z - plus_z))
        )[0]
        spread = 6.0 * psi - (minus_a + plus_a + plus_y + minus_y + plus_z + minus_z)
        spectral_operator = instance_coupling(psi, row_entry)
        psi = psi - TAU * (middle_point + DISSIP * spread + spectral_operator + source)
    return psi[:, None]


def solution(mesh):
    placed = (
        P(None, "inst", "space", None),
        P("inst", "space", None),
        P(None, "inst", "space", None),
        P("inst", "space", None),
        P(None, "space"),
        P(None, "space"),
        P("space"),
        P(),
        P(None, "space"),
        P("space"),
        P(),
    )
    return jax.shard_map(
        shards,
        mesh=mesh,
        in_specs=placed,
        out_specs=P(None, "inst", "space", None),
        check_vma=False,
    )
```

```python
import functools
import math

import jax
import jax.numpy as jnp
from jax import lax
from jax.sharding import PartitionSpec as P
from jax.experimental import pallas as pl
from jax.experimental.pallas import tpu as pltpu

ITERS = 3


GAMMA = 1.4
KWAVE = 0.7
RADIUS = 10.0
TAU = 0.05
DISSIP = 0.25
OMEGA = 1.5
VISCO = 0.5


def padded_2(cells, sides, width):
    for axis, dim in sides:
        count = lax.axis_size(axis)
        head = lax.slice_in_dim(cells, 0, width, axis=dim)
        tail = lax.slice_in_dim(cells, cells.shape[dim] - width, cells.shape[dim], axis=dim)
        cells = jnp.concatenate(
            [
                lax.ppermute(tail, axis, [(i, (i + 1) % count) for i in range(count)]),
                cells,
                lax.ppermute(head, axis, [((i + 1) % count, i) for i in range(count)]),
            ],
            axis=dim,
        )
    return cells


def panel_block(observers, panels, time_now):
    delta = panels[:, None, :] - observers[:3, :, None]
    dist2 = jnp.sum(delta * delta, axis=0)
    dist = jnp.sqrt(dist2)
    harm = observers[5][:, None]
    phase = harm * (time_now - KWAVE * dist)
    amp = (
        (observers[3][:, None] * jnp.cos(phase) + observers[4][:, None] * jnp.sin(phase))
        * (RADIUS * RADIUS)
        / (dist2 * dist)
    )
    return jnp.sum(amp[None] * delta, axis=1)


def sensitivity(observers, panels, time_now):
    count = panels.shape[1]
    obs_count = observers.shape[1]
    block = math.gcd(count, max(128, 262144 // obs_count))
    split = panels.reshape(3, count // block, block).transpose(1, 0, 2)
    out = lax.map(lambda piece: panel_block(observers, piece, time_now), split)
    return out.transpose(1, 0, 2).reshape(3, count)


def conserved(density, velocity, pressure):
    moment = density[None] * velocity
    energy = pressure / (GAMMA - 1.0) + 0.5 * density * jnp.sum(velocity * velocity, axis=0)
    return jnp.concatenate([density[None], moment, energy[None]], axis=0)


def fluxes(state):
    dens = state[0]
    moment = state[1:4]
    energy = state[4]
    vel = moment / dens
    press = (GAMMA - 1.0) * (energy - 0.5 * jnp.sum(moment * vel, axis=0))
    result = []
    for axis_d in range(3):
        comps = [moment[axis_d]]
        for axis_e in range(3):
            term = moment[axis_e] * vel[axis_d]
            if axis_e == axis_d:
                term = term + press
            comps.append(term)
        comps.append((energy + press) * vel[axis_d])
        result.append(jnp.stack(comps))
    return tuple(result)


def spectral_coeff(offset, count):
    safe = jnp.where(offset == 0, 1.0, offset)
    angle = math.pi * safe / count
    even_odd_flag = 1.0 - 2.0 * jnp.mod(safe, 2.0)
    other = (
        -(OMEGA / 2.0) * even_odd_flag * jnp.cos(angle) / jnp.sin(angle)
        + VISCO * (OMEGA * OMEGA / 2.0) * even_odd_flag / jnp.sin(angle) ** 2
    )
    return jnp.where(offset == 0, VISCO * OMEGA * OMEGA * (count * count + 2.0) / 12.0, other)


def split_three(values):
    high = lax.reduce_precision(values, exponent_bits=8, mantissa_bits=7)
    rest = values - high
    middle = lax.reduce_precision(rest, exponent_bits=8, mantissa_bits=7)
    low = rest - middle
    return jnp.stack([high, middle, low]).astype(jnp.bfloat16)


def plane_gather(psi, onehot):
    comps, layers, plane = psi.shape
    parts = split_three(psi.reshape(comps * layers, plane))
    picked = jnp.einsum("pra,kba->kprb", parts, onehot,
                        preferred_element_type=jnp.float32)
    picked = (picked[:, 0] + picked[:, 1]) + picked[:, 2]
    return picked.reshape(onehot.shape[0], comps, layers, plane)


def cell_sum(weight, cell, layers, plane):
    by_layer = (cell // plane)[None, :] == jnp.arange(layers, dtype=jnp.int32)[:, None]
    spread = jnp.where(by_layer, weight[None, :], 0.0)
    picks = ((cell % plane)[:, None] == jnp.arange(plane, dtype=jnp.int32)[None, :]).astype(
        jnp.bfloat16
    )
    parts = split_three(spread)
    summed = jnp.einsum("plq,qb->plb", parts, picks, preferred_element_type=jnp.float32)
    return (summed[0] + summed[1]) + summed[2]


def instance_peers(count, inner, me, sign):
    outer = count // inner
    me_hi, me_lo = me // inner, me % inner
    peers = []
    for slot in range(1, count):
        hi, lo = slot // inner, slot % inner
        peers.append(((me_hi + sign * hi) % outer) * inner + (me_lo + sign * lo) % inner)
    return peers


def coupling_kernel(count, inner, psi_ref, coef_ref, out_ref, held, send_sem, recv_sem):
    me = lax.axis_index("inst")
    targets = instance_peers(count, inner, me, 1)
    barrier = pltpu.get_barrier_semaphore()
    for peer in targets:
        pl.semaphore_signal(barrier, inc=1, device_id={"inst": peer},
                            device_id_type=pl.DeviceIdType.MESH)
    pl.semaphore_wait(barrier, count - 1)
    copies = []
    for slot, peer in enumerate(targets):
        copy = pltpu.make_async_remote_copy(
            src_ref=psi_ref,
            dst_ref=held.at[slot],
            send_sem=send_sem.at[slot],
            recv_sem=recv_sem.at[slot],
            device_id={"inst": peer},
            device_id_type=pl.DeviceIdType.MESH,
        )
        copy.start()
        copies.append(copy)
    total = coef_ref[0] * psi_ref[...]
    for slot, copy in enumerate(copies):
        copy.wait()
        total = total + coef_ref[slot + 1] * held[slot]
    out_ref[...] = total


def instance_coupling(psi, row_entry, step):
    count = lax.axis_size("inst")
    me = lax.axis_index("inst")
    inner = 4 if count % 4 == 0 else count
    sources = instance_peers(count, inner, me, -1)
    coef = jnp.stack([row_entry[0]] + [row_entry[(me - s) % count] for s in sources])
    return pl.pallas_call(
        functools.partial(coupling_kernel, count, inner),
        out_shape=jax.ShapeDtypeStruct(psi.shape, psi.dtype),
        in_specs=[
            pl.BlockSpec(memory_space=pltpu.VMEM),
            pl.BlockSpec(memory_space=pltpu.SMEM),
        ],
        out_specs=pl.BlockSpec(memory_space=pltpu.VMEM),
        scratch_shapes=[
            pltpu.VMEM((count - 1, *psi.shape), psi.dtype),
            pltpu.SemaphoreType.DMA((count - 1,)),
            pltpu.SemaphoreType.DMA((count - 1,)),
        ],
        compiler_params=pltpu.CompilerParams(collective_id=step, has_side_effects=True),
        name=f"instance_coupling_{step}",
    )(psi, coef)


def shards(
    psi_start,
    density,
    velocity,
    pressure,
    obs_pos,
    obs_weight,
    obs_harmonic,
    panel_pos,
    panel_normal,
    panel_cell,
    plane_nbr,
):
    inst_count = lax.axis_size("inst")
    inst_id = lax.axis_index("inst")
    space_id = lax.axis_index("space")
    times = jnp.array([2.0 * math.pi * i / inst_count for i in range(inst_count)], jnp.float32)
    time_now = times[inst_id]
    local_obs = jnp.concatenate(
        [obs_pos, obs_weight, obs_harmonic[None].astype(jnp.float32)], axis=0
    )
    observers = lax.all_gather(local_obs, "space", axis=1, tiled=True)
    owned_count = panel_normal.shape[1]
    mine = lax.dynamic_slice_in_dim(panel_pos, space_id * owned_count, owned_count, 1)
    delta = mine[:, None, :] - observers[:3, :, None]
    dist2 = jnp.sum(delta * delta, axis=0)
    dist = jnp.sqrt(dist2)
    phase = observers[5][:, None] * (time_now - KWAVE * dist)
    amp = (
        (observers[3][:, None] * jnp.cos(phase) + observers[4][:, None] * jnp.sin(phase))
        * (RADIUS * RADIUS)
        / (dist2 * dist)
    )
    along = jnp.sum(delta * panel_normal[:, None, :], axis=0)
    weight = jnp.sum(amp * along, axis=0)
    layers = psi_start.shape[2]
    plane = psi_start.shape[3]
    wall = cell_sum(weight, panel_cell, layers, plane)
    dens = density[0]
    vel = velocity[:, 0]
    state = conserved(dens, vel, pressure[0])
    slope = jnp.concatenate(
        [0.5 * jnp.sum(vel * vel, axis=0)[None], -vel, jnp.ones_like(dens)[None]], axis=0
    ) * (GAMMA - 1.0)
    source = slope * wall[None]
    _, pull = jax.vjp(fluxes, state)
    onehot = (plane_nbr[:, :, None] == jnp.arange(plane, dtype=jnp.int32)[None, None, :]).astype(
        jnp.bfloat16
    )
    row_entry = spectral_coeff(
        jnp.arange(inst_count, dtype=jnp.int32).astype(jnp.float32), float(inst_count)
    )
    psi = psi_start[:, 0]
    for step in range(ITERS):
        padded = padded_2(psi, (("space", 1),), 1)
        minus_a = padded[:, :-2]
        plus_a = padded[:, 2:]
        plus_y, minus_y, plus_z, minus_z = plane_gather(psi, onehot)
        middle_point = pull(
            (0.5 * (minus_a - plus_a), 0.5 * (minus_y - plus_y), 0.5 * (minus_z - plus_z))
        )[0]
        spread = 6.0 * psi - (minus_a + plus_a + plus_y + minus_y + plus_z + minus_z)
        spectral_operator = instance_coupling(psi, row_entry, step)
        psi = psi - TAU * (middle_point + DISSIP * spread + spectral_operator + source)
    return psi[:, None]


def solution(mesh):
    placed = (
        P(None, "inst", "space", None),
        P("inst", "space", None),
        P(None, "inst", "space", None),
        P("inst", "space", None),
        P(None, "space"),
        P(None, "space"),
        P("space"),
        P(),
        P(None, "space"),
        P("space"),
        P(),
    )
    return jax.shard_map(
        shards,
        mesh=mesh,
        in_specs=placed,
        out_specs=P(None, "inst", "space", None),
        check_vma=False,
    )
```

```python
import functools
import math

import jax
import jax.numpy as jnp
from jax import lax
from jax.sharding import PartitionSpec as P
from jax.experimental import pallas as pl
from jax.experimental.pallas import tpu as pltpu

ITERS = 3


GAMMA = 1.4
KWAVE = 0.7
RADIUS = 10.0
TAU = 0.05
DISSIP = 0.25
OMEGA = 1.5
VISCO = 0.5


def padded_2(cells, sides, width):
    for axis, dim in sides:
        count = lax.axis_size(axis)
        head = lax.slice_in_dim(cells, 0, width, axis=dim)
        tail = lax.slice_in_dim(cells, cells.shape[dim] - width, cells.shape[dim], axis=dim)
        cells = jnp.concatenate(
            [
                lax.ppermute(tail, axis, [(i, (i + 1) % count) for i in range(count)]),
                cells,
                lax.ppermute(head, axis, [((i + 1) % count, i) for i in range(count)]),
            ],
            axis=dim,
        )
    return cells


def panel_block(observers, panels, time_now):
    delta = panels[:, None, :] - observers[:3, :, None]
    dist2 = jnp.sum(delta * delta, axis=0)
    dist = jnp.sqrt(dist2)
    harm = observers[5][:, None]
    phase = harm * (time_now - KWAVE * dist)
    amp = (
        (observers[3][:, None] * jnp.cos(phase) + observers[4][:, None] * jnp.sin(phase))
        * (RADIUS * RADIUS)
        / (dist2 * dist)
    )
    return jnp.sum(amp[None] * delta, axis=1)


def sensitivity(observers, panels, time_now):
    count = panels.shape[1]
    obs_count = observers.shape[1]
    block = math.gcd(count, max(128, 262144 // obs_count))
    split = panels.reshape(3, count // block, block).transpose(1, 0, 2)
    out = lax.map(lambda piece: panel_block(observers, piece, time_now), split)
    return out.transpose(1, 0, 2).reshape(3, count)


def conserved(density, velocity, pressure):
    moment = density[None] * velocity
    energy = pressure / (GAMMA - 1.0) + 0.5 * density * jnp.sum(velocity * velocity, axis=0)
    return jnp.concatenate([density[None], moment, energy[None]], axis=0)


def fluxes(state):
    dens = state[0]
    moment = state[1:4]
    energy = state[4]
    vel = moment / dens
    press = (GAMMA - 1.0) * (energy - 0.5 * jnp.sum(moment * vel, axis=0))
    result = []
    for axis_d in range(3):
        comps = [moment[axis_d]]
        for axis_e in range(3):
            term = moment[axis_e] * vel[axis_d]
            if axis_e == axis_d:
                term = term + press
            comps.append(term)
        comps.append((energy + press) * vel[axis_d])
        result.append(jnp.stack(comps))
    return tuple(result)


def spectral_coeff(offset, count):
    safe = jnp.where(offset == 0, 1.0, offset)
    angle = math.pi * safe / count
    even_odd_flag = 1.0 - 2.0 * jnp.mod(safe, 2.0)
    other = (
        -(OMEGA / 2.0) * even_odd_flag * jnp.cos(angle) / jnp.sin(angle)
        + VISCO * (OMEGA * OMEGA / 2.0) * even_odd_flag / jnp.sin(angle) ** 2
    )
    return jnp.where(offset == 0, VISCO * OMEGA * OMEGA * (count * count + 2.0) / 12.0, other)


def split_three(values):
    high = lax.reduce_precision(values, exponent_bits=8, mantissa_bits=7)
    rest = values - high
    middle = lax.reduce_precision(rest, exponent_bits=8, mantissa_bits=7)
    low = rest - middle
    return jnp.stack([high, middle, low]).astype(jnp.bfloat16)


def plane_gather(psi, onehot):
    comps, layers, plane = psi.shape
    parts = split_three(psi.reshape(comps * layers, plane))
    picked = jnp.einsum("pra,kba->kprb", parts, onehot,
                        preferred_element_type=jnp.float32)
    picked = (picked[:, 0] + picked[:, 1]) + picked[:, 2]
    return picked.reshape(onehot.shape[0], comps, layers, plane)


def cell_sum(weight, cell, layers, plane):
    by_layer = (cell // plane)[None, :] == jnp.arange(layers, dtype=jnp.int32)[:, None]
    spread = jnp.where(by_layer, weight[None, :], 0.0)
    picks = ((cell % plane)[:, None] == jnp.arange(plane, dtype=jnp.int32)[None, :]).astype(
        jnp.bfloat16
    )
    parts = split_three(spread)
    summed = jnp.einsum("plq,qb->plb", parts, picks, preferred_element_type=jnp.float32)
    return (summed[0] + summed[1]) + summed[2]


def greet(axis, peers):
    barrier = pltpu.get_barrier_semaphore()
    for peer in peers:
        pl.semaphore_signal(barrier, inc=1, device_id={axis: peer},
                            device_id_type=pl.DeviceIdType.MESH)
    pl.semaphore_wait(barrier, len(peers))


def coupling_kernel(count, inner, psi_ref, table_ref, out_ref, held, outbox, inbox,
                    ring_send, ring_recv, cross_send, cross_recv):
    outer = count // inner
    me = lax.axis_index("inst")
    me_hi, me_lo = me // inner, me % inner
    ring = [me_hi * inner + (me_lo + d) % inner for d in range(1, inner)]
    ring_from = [me_hi * inner + (me_lo - d) % inner for d in range(1, inner)]
    partners = [((me_hi + h) % outer) * inner + me_lo for h in range(1, outer)]
    greet("inst", ring + partners)

    def coef(row, col):
        return table_ref[(row - col) % count]

    copies = []
    for slot, peer in enumerate(ring):
        copy = pltpu.make_async_remote_copy(
            src_ref=psi_ref, dst_ref=held.at[slot], send_sem=ring_send.at[slot],
            recv_sem=ring_recv.at[slot], device_id={"inst": peer},
            device_id_type=pl.DeviceIdType.MESH)
        copy.start()
        copies.append(copy)
    for copy in copies:
        copy.wait()
    cross = []
    for slot, partner in enumerate(partners):
        part = coef(partner, me) * psi_ref[...]
        for d, source in enumerate(ring_from):
            part = part + coef(partner, source) * held[d]
        outbox[slot] = part
        copy = pltpu.make_async_remote_copy(
            src_ref=outbox.at[slot], dst_ref=inbox.at[slot], send_sem=cross_send.at[slot],
            recv_sem=cross_recv.at[slot], device_id={"inst": partner},
            device_id_type=pl.DeviceIdType.MESH)
        copy.start()
        cross.append(copy)
    total = coef(me, me) * psi_ref[...]
    for d, source in enumerate(ring_from):
        total = total + coef(me, source) * held[d]
    for slot, copy in enumerate(cross):
        copy.wait()
        total = total + inbox[slot]
    out_ref[...] = total


def instance_coupling(psi, table, step):
    count = lax.axis_size("inst")
    inner = 4 if count % 4 == 0 else count
    outer = count // inner
    return pl.pallas_call(
        functools.partial(coupling_kernel, count, inner),
        out_shape=jax.ShapeDtypeStruct(psi.shape, psi.dtype),
        in_specs=[
            pl.BlockSpec(memory_space=pltpu.VMEM),
            pl.BlockSpec(memory_space=pltpu.SMEM),
        ],
        out_specs=pl.BlockSpec(memory_space=pltpu.VMEM),
        scratch_shapes=[
            pltpu.VMEM((inner - 1, *psi.shape), psi.dtype),
            pltpu.VMEM((max(outer - 1, 1), *psi.shape), psi.dtype),
            pltpu.VMEM((max(outer - 1, 1), *psi.shape), psi.dtype),
            pltpu.SemaphoreType.DMA((inner - 1,)),
            pltpu.SemaphoreType.DMA((inner - 1,)),
            pltpu.SemaphoreType.DMA((max(outer - 1, 1),)),
            pltpu.SemaphoreType.DMA((max(outer - 1, 1),)),
        ],
        compiler_params=pltpu.CompilerParams(collective_id=step, has_side_effects=True),
        name=f"instance_coupling_{step}",
    )(psi, table)


def gather_kernel(count, block_ref, out_ref, held, send_sem, recv_sem):
    me = lax.axis_index("space")
    peers = [(me + d) % count for d in range(1, count)]
    greet("space", peers)
    copies = []
    for slot, peer in enumerate(peers):
        copy = pltpu.make_async_remote_copy(
            src_ref=block_ref, dst_ref=held.at[me], send_sem=send_sem.at[slot],
            recv_sem=recv_sem.at[slot], device_id={"space": peer},
            device_id_type=pl.DeviceIdType.MESH)
        copy.start()
        copies.append(copy)
    for copy in copies:
        copy.wait()
    held[me] = block_ref[...]
    out_ref[...] = held[...]


def space_gather(block, collective):
    count = lax.axis_size("space")
    return pl.pallas_call(
        functools.partial(gather_kernel, count),
        out_shape=jax.ShapeDtypeStruct((count, *block.shape), block.dtype),
        in_specs=[pl.BlockSpec(memory_space=pltpu.VMEM)],
        out_specs=pl.BlockSpec(memory_space=pltpu.VMEM),
        scratch_shapes=[
            pltpu.VMEM((count, *block.shape), block.dtype),
            pltpu.SemaphoreType.DMA((count - 1,)),
            pltpu.SemaphoreType.DMA((count - 1,)),
        ],
        compiler_params=pltpu.CompilerParams(collective_id=collective, has_side_effects=True),
        name="space_gather",
    )(block)


def shards(
    psi_start,
    density,
    velocity,
    pressure,
    obs_pos,
    obs_weight,
    obs_harmonic,
    panel_pos,
    panel_normal,
    panel_cell,
    plane_nbr,
):
    inst_count = lax.axis_size("inst")
    inst_id = lax.axis_index("inst")
    space_id = lax.axis_index("space")
    times = jnp.array([2.0 * math.pi * i / inst_count for i in range(inst_count)], jnp.float32)
    time_now = times[inst_id]
    local_obs = jnp.concatenate(
        [obs_pos, obs_weight, obs_harmonic[None].astype(jnp.float32)], axis=0
    )
    rows, per = local_obs.shape
    assert rows <= 8 and per <= 128
    packed = jnp.zeros((8, 128), jnp.float32).at[:rows, :per].set(local_obs)
    stacked = space_gather(packed, ITERS)
    observers = stacked[:, :rows, :per].transpose(1, 0, 2).reshape(rows, -1)
    owned_count = panel_normal.shape[1]
    mine = lax.dynamic_slice_in_dim(panel_pos, space_id * owned_count, owned_count, 1)
    delta = mine[:, None, :] - observers[:3, :, None]
    dist2 = jnp.sum(delta * delta, axis=0)
    dist = jnp.sqrt(dist2)
    phase = observers[5][:, None] * (time_now - KWAVE * dist)
    amp = (
        (observers[3][:, None] * jnp.cos(phase) + observers[4][:, None] * jnp.sin(phase))
        * (RADIUS * RADIUS)
        / (dist2 * dist)
    )
    along = jnp.sum(delta * panel_normal[:, None, :], axis=0)
    weight = jnp.sum(amp * along, axis=0)
    layers = psi_start.shape[2]
    plane = psi_start.shape[3]
    wall = cell_sum(weight, panel_cell, layers, plane)
    dens = density[0]
    vel = velocity[:, 0]
    state = conserved(dens, vel, pressure[0])
    slope = jnp.concatenate(
        [0.5 * jnp.sum(vel * vel, axis=0)[None], -vel, jnp.ones_like(dens)[None]], axis=0
    ) * (GAMMA - 1.0)
    source = slope * wall[None]
    _, pull = jax.vjp(fluxes, state)
    onehot = (plane_nbr[:, :, None] == jnp.arange(plane, dtype=jnp.int32)[None, None, :]).astype(
        jnp.bfloat16
    )
    row_entry = spectral_coeff(
        jnp.arange(inst_count, dtype=jnp.int32).astype(jnp.float32), float(inst_count)
    )
    psi = psi_start[:, 0]
    for step in range(ITERS):
        padded = padded_2(psi, (("space", 1),), 1)
        minus_a = padded[:, :-2]
        plus_a = padded[:, 2:]
        plus_y, minus_y, plus_z, minus_z = plane_gather(psi, onehot)
        middle_point = pull(
            (0.5 * (minus_a - plus_a), 0.5 * (minus_y - plus_y), 0.5 * (minus_z - plus_z))
        )[0]
        spread = 6.0 * psi - (minus_a + plus_a + plus_y + minus_y + plus_z + minus_z)
        spectral_operator = instance_coupling(psi, row_entry, step)
        psi = psi - TAU * (middle_point + DISSIP * spread + spectral_operator + source)
    return psi[:, None]


def solution(mesh):
    placed = (
        P(None, "inst", "space", None),
        P("inst", "space", None),
        P(None, "inst", "space", None),
        P("inst", "space", None),
        P(None, "space"),
        P(None, "space"),
        P("space"),
        P(),
        P(None, "space"),
        P("space"),
        P(),
    )
    return jax.shard_map(
        shards,
        mesh=mesh,
        in_specs=placed,
        out_specs=P(None, "inst", "space", None),
        check_vma=False,
    )
```

```python
import functools
import math

import jax
import jax.numpy as jnp
from jax import lax
from jax.sharding import PartitionSpec as P
from jax.experimental import pallas as pl
from jax.experimental.pallas import tpu as pltpu

ITERS = 3


GAMMA = 1.4
KWAVE = 0.7
RADIUS = 10.0
TAU = 0.05
DISSIP = 0.25
OMEGA = 1.5
VISCO = 0.5


def padded_2(cells, sides, width):
    for axis, dim in sides:
        count = lax.axis_size(axis)
        head = lax.slice_in_dim(cells, 0, width, axis=dim)
        tail = lax.slice_in_dim(cells, cells.shape[dim] - width, cells.shape[dim], axis=dim)
        cells = jnp.concatenate(
            [
                lax.ppermute(tail, axis, [(i, (i + 1) % count) for i in range(count)]),
                cells,
                lax.ppermute(head, axis, [((i + 1) % count, i) for i in range(count)]),
            ],
            axis=dim,
        )
    return cells


def panel_block(observers, panels, time_now):
    delta = panels[:, None, :] - observers[:3, :, None]
    dist2 = jnp.sum(delta * delta, axis=0)
    dist = jnp.sqrt(dist2)
    harm = observers[5][:, None]
    phase = harm * (time_now - KWAVE * dist)
    amp = (
        (observers[3][:, None] * jnp.cos(phase) + observers[4][:, None] * jnp.sin(phase))
        * (RADIUS * RADIUS)
        / (dist2 * dist)
    )
    return jnp.sum(amp[None] * delta, axis=1)


def sensitivity(observers, panels, time_now):
    count = panels.shape[1]
    obs_count = observers.shape[1]
    block = math.gcd(count, max(128, 262144 // obs_count))
    split = panels.reshape(3, count // block, block).transpose(1, 0, 2)
    out = lax.map(lambda piece: panel_block(observers, piece, time_now), split)
    return out.transpose(1, 0, 2).reshape(3, count)


def conserved(density, velocity, pressure):
    moment = density[None] * velocity
    energy = pressure / (GAMMA - 1.0) + 0.5 * density * jnp.sum(velocity * velocity, axis=0)
    return jnp.concatenate([density[None], moment, energy[None]], axis=0)


def fluxes(state):
    dens = state[0]
    moment = state[1:4]
    energy = state[4]
    vel = moment / dens
    press = (GAMMA - 1.0) * (energy - 0.5 * jnp.sum(moment * vel, axis=0))
    result = []
    for axis_d in range(3):
        comps = [moment[axis_d]]
        for axis_e in range(3):
            term = moment[axis_e] * vel[axis_d]
            if axis_e == axis_d:
                term = term + press
            comps.append(term)
        comps.append((energy + press) * vel[axis_d])
        result.append(jnp.stack(comps))
    return tuple(result)


def spectral_coeff(offset, count):
    safe = jnp.where(offset == 0, 1.0, offset)
    angle = math.pi * safe / count
    even_odd_flag = 1.0 - 2.0 * jnp.mod(safe, 2.0)
    other = (
        -(OMEGA / 2.0) * even_odd_flag * jnp.cos(angle) / jnp.sin(angle)
        + VISCO * (OMEGA * OMEGA / 2.0) * even_odd_flag / jnp.sin(angle) ** 2
    )
    return jnp.where(offset == 0, VISCO * OMEGA * OMEGA * (count * count + 2.0) / 12.0, other)


def split_three(values):
    high = lax.reduce_precision(values, exponent_bits=8, mantissa_bits=7)
    rest = values - high
    middle = lax.reduce_precision(rest, exponent_bits=8, mantissa_bits=7)
    low = rest - middle
    return jnp.stack([high, middle, low]).astype(jnp.bfloat16)


def plane_gather(psi, onehot):
    comps, layers, plane = psi.shape
    parts = split_three(psi.reshape(comps * layers, plane))
    picked = jnp.einsum("pra,kba->kprb", parts, onehot,
                        preferred_element_type=jnp.float32)
    picked = (picked[:, 0] + picked[:, 1]) + picked[:, 2]
    return picked.reshape(onehot.shape[0], comps, layers, plane)


def cell_sum(weight, cell, layers, plane):
    by_layer = (cell // plane)[None, :] == jnp.arange(layers, dtype=jnp.int32)[:, None]
    spread = jnp.where(by_layer, weight[None, :], 0.0)
    picks = ((cell % plane)[:, None] == jnp.arange(plane, dtype=jnp.int32)[None, :]).astype(
        jnp.bfloat16
    )
    parts = split_three(spread)
    summed = jnp.einsum("plq,qb->plb", parts, picks, preferred_element_type=jnp.float32)
    return (summed[0] + summed[1]) + summed[2]


def greet(axis, peers):
    barrier = pltpu.get_barrier_semaphore()
    for peer in peers:
        pl.semaphore_signal(barrier, inc=1, device_id={axis: peer},
                            device_id_type=pl.DeviceIdType.MESH)
    pl.semaphore_wait(barrier, len(peers))


def coupling_kernel(count, inner, psi_ref, table_ref, out_ref, held, outbox, inbox,
                    ring_send, ring_recv, cross_send, cross_recv):
    outer = count // inner
    me = lax.axis_index("inst")
    me_hi, me_lo = me // inner, me % inner
    ring = [me_hi * inner + (me_lo + d) % inner for d in range(1, inner)]
    ring_from = [me_hi * inner + (me_lo - d) % inner for d in range(1, inner)]
    partners = [((me_hi + h) % outer) * inner + me_lo for h in range(1, outer)]
    greet("inst", ring + partners)

    def coef(row, col):
        return table_ref[(row - col) % count]

    copies = []
    for slot, peer in enumerate(ring):
        copy = pltpu.make_async_remote_copy(
            src_ref=psi_ref, dst_ref=held.at[slot], send_sem=ring_send.at[slot],
            recv_sem=ring_recv.at[slot], device_id={"inst": peer},
            device_id_type=pl.DeviceIdType.MESH)
        copy.start()
        copies.append(copy)
    for copy in copies:
        copy.wait()
    cross = []
    for slot, partner in enumerate(partners):
        part = coef(partner, me) * psi_ref[...]
        for d, source in enumerate(ring_from):
            part = part + coef(partner, source) * held[d]
        outbox[slot] = part
        copy = pltpu.make_async_remote_copy(
            src_ref=outbox.at[slot], dst_ref=inbox.at[slot], send_sem=cross_send.at[slot],
            recv_sem=cross_recv.at[slot], device_id={"inst": partner},
            device_id_type=pl.DeviceIdType.MESH)
        copy.start()
        cross.append(copy)
    total = coef(me, me) * psi_ref[...]
    for d, source in enumerate(ring_from):
        total = total + coef(me, source) * held[d]
    for slot, copy in enumerate(cross):
        copy.wait()
        total = total + inbox[slot]
    out_ref[...] = total


def instance_coupling(psi, table, step):
    count = lax.axis_size("inst")
    inner = 4 if count % 4 == 0 else count
    outer = count // inner
    return pl.pallas_call(
        functools.partial(coupling_kernel, count, inner),
        out_shape=jax.ShapeDtypeStruct(psi.shape, psi.dtype),
        in_specs=[
            pl.BlockSpec(memory_space=pltpu.VMEM),
            pl.BlockSpec(memory_space=pltpu.SMEM),
        ],
        out_specs=pl.BlockSpec(memory_space=pltpu.VMEM),
        scratch_shapes=[
            pltpu.VMEM((inner - 1, *psi.shape), psi.dtype),
            pltpu.VMEM((max(outer - 1, 1), *psi.shape), psi.dtype),
            pltpu.VMEM((max(outer - 1, 1), *psi.shape), psi.dtype),
            pltpu.SemaphoreType.DMA((inner - 1,)),
            pltpu.SemaphoreType.DMA((inner - 1,)),
            pltpu.SemaphoreType.DMA((max(outer - 1, 1),)),
            pltpu.SemaphoreType.DMA((max(outer - 1, 1),)),
        ],
        compiler_params=pltpu.CompilerParams(collective_id=step, has_side_effects=True),
        name=f"instance_coupling_{step}",
    )(psi, table)


def gather_kernel(count, block_ref, out_ref, held, send_sem, recv_sem):
    me = lax.axis_index("space")
    peers = [(me + d) % count for d in range(1, count)]
    greet("space", peers)
    copies = []
    for slot, peer in enumerate(peers):
        copy = pltpu.make_async_remote_copy(
            src_ref=block_ref, dst_ref=held.at[me], send_sem=send_sem.at[slot],
            recv_sem=recv_sem.at[slot], device_id={"space": peer},
            device_id_type=pl.DeviceIdType.MESH)
        copy.start()
        copies.append(copy)
    for copy in copies:
        copy.wait()
    held[me] = block_ref[...]
    out_ref[...] = held[...]


def space_gather(block, collective):
    count = lax.axis_size("space")
    return pl.pallas_call(
        functools.partial(gather_kernel, count),
        out_shape=jax.ShapeDtypeStruct((count, *block.shape), block.dtype),
        in_specs=[pl.BlockSpec(memory_space=pltpu.VMEM)],
        out_specs=pl.BlockSpec(memory_space=pltpu.VMEM),
        scratch_shapes=[
            pltpu.VMEM((count, *block.shape), block.dtype),
            pltpu.SemaphoreType.DMA((count - 1,)),
            pltpu.SemaphoreType.DMA((count - 1,)),
        ],
        compiler_params=pltpu.CompilerParams(collective_id=collective, has_side_effects=True),
        name="space_gather",
    )(block)


def route_kernel(count, rows_ref, out_ref, held, send_sem, recv_sem):
    me = lax.axis_index("inst")
    peers = [(me + d) % count for d in range(1, count)]
    greet("inst", peers)
    copies = []
    for slot, peer in enumerate(peers):
        copy = pltpu.make_async_remote_copy(
            src_ref=rows_ref.at[peer], dst_ref=held.at[me], send_sem=send_sem.at[slot],
            recv_sem=recv_sem.at[slot], device_id={"inst": peer},
            device_id_type=pl.DeviceIdType.MESH)
        copy.start()
        copies.append(copy)
    for copy in copies:
        copy.wait()
    held[me] = rows_ref[me]
    out_ref[...] = held[...]


def inst_route(rows, collective):
    count = lax.axis_size("inst")
    return pl.pallas_call(
        functools.partial(route_kernel, count),
        out_shape=jax.ShapeDtypeStruct(rows.shape, rows.dtype),
        in_specs=[pl.BlockSpec(memory_space=pltpu.VMEM)],
        out_specs=pl.BlockSpec(memory_space=pltpu.VMEM),
        scratch_shapes=[
            pltpu.VMEM(rows.shape, rows.dtype),
            pltpu.SemaphoreType.DMA((count - 1,)),
            pltpu.SemaphoreType.DMA((count - 1,)),
        ],
        compiler_params=pltpu.CompilerParams(collective_id=collective, has_side_effects=True),
        name="inst_route",
    )(rows)


def shards(
    psi_start,
    density,
    velocity,
    pressure,
    obs_pos,
    obs_weight,
    obs_harmonic,
    panel_pos,
    panel_normal,
    panel_cell,
    plane_nbr,
):
    inst_count = lax.axis_size("inst")
    inst_id = lax.axis_index("inst")
    space_id = lax.axis_index("space")
    times = jnp.array([2.0 * math.pi * i / inst_count for i in range(inst_count)], jnp.float32)
    local_obs = jnp.concatenate(
        [obs_pos, obs_weight, obs_harmonic[None].astype(jnp.float32)], axis=0
    )
    rows, per = local_obs.shape
    assert rows <= 8 and per <= 128
    packed = jnp.zeros((8, 128), jnp.float32).at[:rows, :per].set(local_obs)
    stacked = space_gather(packed, ITERS)
    observers = stacked[:, :rows, :per].transpose(1, 0, 2).reshape(rows, -1)
    owned_count = panel_normal.shape[1]
    piece = owned_count // inst_count
    assert piece * inst_count == owned_count and piece % 128 == 0
    mine = lax.dynamic_slice_in_dim(
        panel_pos, space_id * owned_count + inst_id * piece, piece, 1
    )
    normal = lax.dynamic_slice_in_dim(panel_normal, inst_id * piece, piece, 1)
    delta = mine[:, None, :] - observers[:3, :, None]
    dist2 = jnp.sum(delta * delta, axis=0)
    dist = jnp.sqrt(dist2)
    harm = observers[5]
    lag = harm[:, None] * (KWAVE * dist)
    along = jnp.sum(delta * normal[:, None, :], axis=0) * (RADIUS * RADIUS) / (dist2 * dist)
    pairs = jnp.concatenate([along * jnp.cos(lag), along * jnp.sin(lag)], axis=0)
    beat = times[:, None] * harm[None, :]
    cos_beat, sin_beat = jnp.cos(beat), jnp.sin(beat)
    real, imag = observers[3][None, :], observers[4][None, :]
    mixes = jnp.concatenate(
        [real * cos_beat + imag * sin_beat, real * sin_beat - imag * cos_beat], axis=1
    )
    partial = jnp.dot(mixes, pairs, precision=lax.Precision.HIGHEST)
    routed = inst_route(partial.reshape(inst_count, piece // 128, 128), ITERS + 1)
    weight = routed.reshape(owned_count)
    layers = psi_start.shape[2]
    plane = psi_start.shape[3]
    wall = cell_sum(weight, panel_cell, layers, plane)
    dens = density[0]
    vel = velocity[:, 0]
    state = conserved(dens, vel, pressure[0])
    slope = jnp.concatenate(
        [0.5 * jnp.sum(vel * vel, axis=0)[None], -vel, jnp.ones_like(dens)[None]], axis=0
    ) * (GAMMA - 1.0)
    source = slope * wall[None]
    _, pull = jax.vjp(fluxes, state)
    onehot = (plane_nbr[:, :, None] == jnp.arange(plane, dtype=jnp.int32)[None, None, :]).astype(
        jnp.bfloat16
    )
    row_entry = spectral_coeff(
        jnp.arange(inst_count, dtype=jnp.int32).astype(jnp.float32), float(inst_count)
    )
    psi = psi_start[:, 0]
    for step in range(ITERS):
        padded = padded_2(psi, (("space", 1),), 1)
        minus_a = padded[:, :-2]
        plus_a = padded[:, 2:]
        plus_y, minus_y, plus_z, minus_z = plane_gather(psi, onehot)
        middle_point = pull(
            (0.5 * (minus_a - plus_a), 0.5 * (minus_y - plus_y), 0.5 * (minus_z - plus_z))
        )[0]
        spread = 6.0 * psi - (minus_a + plus_a + plus_y + minus_y + plus_z + minus_z)
        spectral_operator = instance_coupling(psi, row_entry, step)
        psi = psi - TAU * (middle_point + DISSIP * spread + spectral_operator + source)
    return psi[:, None]


def solution(mesh):
    placed = (
        P(None, "inst", "space", None),
        P("inst", "space", None),
        P(None, "inst", "space", None),
        P("inst", "space", None),
        P(None, "space"),
        P(None, "space"),
        P("space"),
        P(),
        P(None, "space"),
        P("space"),
        P(),
    )
    return jax.shard_map(
        shards,
        mesh=mesh,
        in_specs=placed,
        out_specs=P(None, "inst", "space", None),
        check_vma=False,
    )
```

```python
import functools
import math

import jax
import jax.numpy as jnp
from jax import lax
from jax.sharding import PartitionSpec as P
from jax.experimental import pallas as pl
from jax.experimental.pallas import tpu as pltpu

ITERS = 3


GAMMA = 1.4
KWAVE = 0.7
RADIUS = 10.0
TAU = 0.05
DISSIP = 0.25
OMEGA = 1.5
VISCO = 0.5


def padded_2(cells, sides, width):
    for axis, dim in sides:
        count = lax.axis_size(axis)
        head = lax.slice_in_dim(cells, 0, width, axis=dim)
        tail = lax.slice_in_dim(cells, cells.shape[dim] - width, cells.shape[dim], axis=dim)
        cells = jnp.concatenate(
            [
                lax.ppermute(tail, axis, [(i, (i + 1) % count) for i in range(count)]),
                cells,
                lax.ppermute(head, axis, [((i + 1) % count, i) for i in range(count)]),
            ],
            axis=dim,
        )
    return cells


def panel_block(observers, panels, time_now):
    delta = panels[:, None, :] - observers[:3, :, None]
    dist2 = jnp.sum(delta * delta, axis=0)
    dist = jnp.sqrt(dist2)
    harm = observers[5][:, None]
    phase = harm * (time_now - KWAVE * dist)
    amp = (
        (observers[3][:, None] * jnp.cos(phase) + observers[4][:, None] * jnp.sin(phase))
        * (RADIUS * RADIUS)
        / (dist2 * dist)
    )
    return jnp.sum(amp[None] * delta, axis=1)


def sensitivity(observers, panels, time_now):
    count = panels.shape[1]
    obs_count = observers.shape[1]
    block = math.gcd(count, max(128, 262144 // obs_count))
    split = panels.reshape(3, count // block, block).transpose(1, 0, 2)
    out = lax.map(lambda piece: panel_block(observers, piece, time_now), split)
    return out.transpose(1, 0, 2).reshape(3, count)


def conserved(density, velocity, pressure):
    moment = density[None] * velocity
    energy = pressure / (GAMMA - 1.0) + 0.5 * density * jnp.sum(velocity * velocity, axis=0)
    return jnp.concatenate([density[None], moment, energy[None]], axis=0)


def fluxes(state):
    dens = state[0]
    moment = state[1:4]
    energy = state[4]
    vel = moment / dens
    press = (GAMMA - 1.0) * (energy - 0.5 * jnp.sum(moment * vel, axis=0))
    result = []
    for axis_d in range(3):
        comps = [moment[axis_d]]
        for axis_e in range(3):
            term = moment[axis_e] * vel[axis_d]
            if axis_e == axis_d:
                term = term + press
            comps.append(term)
        comps.append((energy + press) * vel[axis_d])
        result.append(jnp.stack(comps))
    return tuple(result)


def spectral_coeff(offset, count):
    safe = jnp.where(offset == 0, 1.0, offset)
    angle = math.pi * safe / count
    even_odd_flag = 1.0 - 2.0 * jnp.mod(safe, 2.0)
    other = (
        -(OMEGA / 2.0) * even_odd_flag * jnp.cos(angle) / jnp.sin(angle)
        + VISCO * (OMEGA * OMEGA / 2.0) * even_odd_flag / jnp.sin(angle) ** 2
    )
    return jnp.where(offset == 0, VISCO * OMEGA * OMEGA * (count * count + 2.0) / 12.0, other)


def split_three(values):
    high = lax.reduce_precision(values, exponent_bits=8, mantissa_bits=7)
    rest = values - high
    middle = lax.reduce_precision(rest, exponent_bits=8, mantissa_bits=7)
    low = rest - middle
    return jnp.stack([high, middle, low]).astype(jnp.bfloat16)


def plane_gather(psi, onehot):
    comps, layers, plane = psi.shape
    parts = split_three(psi.reshape(comps * layers, plane))
    picked = jnp.einsum("pra,kba->kprb", parts, onehot,
                        preferred_element_type=jnp.float32)
    picked = (picked[:, 0] + picked[:, 1]) + picked[:, 2]
    return picked.reshape(onehot.shape[0], comps, layers, plane)


def cell_sum(weight, cell, layers, plane):
    by_layer = (cell // plane)[None, :] == jnp.arange(layers, dtype=jnp.int32)[:, None]
    spread = jnp.where(by_layer, weight[None, :], 0.0)
    picks = ((cell % plane)[:, None] == jnp.arange(plane, dtype=jnp.int32)[None, :]).astype(
        jnp.bfloat16
    )
    parts = split_three(spread)
    summed = jnp.einsum("plq,qb->plb", parts, picks, preferred_element_type=jnp.float32)
    return (summed[0] + summed[1]) + summed[2]


def greet(axis, peers):
    greet_all([{axis: peer} for peer in peers])


def greet_all(devices):
    barrier = pltpu.get_barrier_semaphore()
    for device in devices:
        pl.semaphore_signal(barrier, inc=1, device_id=device,
                            device_id_type=pl.DeviceIdType.MESH)
    pl.semaphore_wait(barrier, len(devices))


def coupling_kernel(count, inner, psi_ref, table_ref, out_ref, below_ref, above_ref, held,
                    outbox, inbox, below, above, ring_send, ring_recv, cross_send, cross_recv,
                    edge_send, edge_recv):
    outer = count // inner
    me = lax.axis_index("inst")
    me_hi, me_lo = me // inner, me % inner
    ring = [me_hi * inner + (me_lo + d) % inner for d in range(1, inner)]
    ring_from = [me_hi * inner + (me_lo - d) % inner for d in range(1, inner)]
    partners = [((me_hi + h) % outer) * inner + me_lo for h in range(1, outer)]
    slabs = lax.axis_size("space")
    here = lax.axis_index("space")
    up, down = (here + 1) % slabs, (here + slabs - 1) % slabs
    greet_all([{"inst": p} for p in ring + partners] + [{"space": up}, {"space": down}])
    last = psi_ref.shape[1] - 1
    edges = []
    for slot, (peer, layer, land) in enumerate(((up, last, below), (down, 0, above))):
        copy = pltpu.make_async_remote_copy(
            src_ref=psi_ref.at[:, pl.ds(layer, 1), :], dst_ref=land.at[:, pl.ds(layer, 1), :],
            send_sem=edge_send.at[slot], recv_sem=edge_recv.at[slot],
            device_id={"space": peer}, device_id_type=pl.DeviceIdType.MESH)
        copy.start()
        edges.append(copy)

    def coef(row, col):
        return table_ref[(row - col) % count]

    copies = []
    for slot, peer in enumerate(ring):
        copy = pltpu.make_async_remote_copy(
            src_ref=psi_ref, dst_ref=held.at[slot], send_sem=ring_send.at[slot],
            recv_sem=ring_recv.at[slot], device_id={"inst": peer},
            device_id_type=pl.DeviceIdType.MESH)
        copy.start()
        copies.append(copy)
    for copy in copies:
        copy.wait()
    cross = []
    for slot, partner in enumerate(partners):
        part = coef(partner, me) * psi_ref[...]
        for d, source in enumerate(ring_from):
            part = part + coef(partner, source) * held[d]
        outbox[slot] = part
        copy = pltpu.make_async_remote_copy(
            src_ref=outbox.at[slot], dst_ref=inbox.at[slot], send_sem=cross_send.at[slot],
            recv_sem=cross_recv.at[slot], device_id={"inst": partner},
            device_id_type=pl.DeviceIdType.MESH)
        copy.start()
        cross.append(copy)
    total = coef(me, me) * psi_ref[...]
    for d, source in enumerate(ring_from):
        total = total + coef(me, source) * held[d]
    for slot, copy in enumerate(cross):
        copy.wait()
        total = total + inbox[slot]
    out_ref[...] = total
    for copy in edges:
        copy.wait()
    below_ref[...] = below[:, last:, :]
    above_ref[...] = above[:, :1, :]


def instance_coupling(psi, table, step):
    count = lax.axis_size("inst")
    assert lax.axis_size("space") > 1
    inner = 4 if count % 4 == 0 else count
    outer = count // inner
    comps, layers, plane = psi.shape
    edge = jax.ShapeDtypeStruct((comps, 1, plane), psi.dtype)
    return pl.pallas_call(
        functools.partial(coupling_kernel, count, inner),
        out_shape=(jax.ShapeDtypeStruct(psi.shape, psi.dtype), edge, edge),
        in_specs=[
            pl.BlockSpec(memory_space=pltpu.VMEM),
            pl.BlockSpec(memory_space=pltpu.SMEM),
        ],
        out_specs=[pl.BlockSpec(memory_space=pltpu.VMEM)] * 3,
        scratch_shapes=[
            pltpu.VMEM((inner - 1, *psi.shape), psi.dtype),
            pltpu.VMEM((max(outer - 1, 1), *psi.shape), psi.dtype),
            pltpu.VMEM((max(outer - 1, 1), *psi.shape), psi.dtype),
            pltpu.VMEM(psi.shape, psi.dtype),
            pltpu.VMEM(psi.shape, psi.dtype),
            pltpu.SemaphoreType.DMA((inner - 1,)),
            pltpu.SemaphoreType.DMA((inner - 1,)),
            pltpu.SemaphoreType.DMA((max(outer - 1, 1),)),
            pltpu.SemaphoreType.DMA((max(outer - 1, 1),)),
            pltpu.SemaphoreType.DMA((2,)),
            pltpu.SemaphoreType.DMA((2,)),
        ],
        compiler_params=pltpu.CompilerParams(collective_id=step, has_side_effects=True),
        name=f"instance_coupling_{step}",
    )(psi, table)


def gather_kernel(count, block_ref, out_ref, held, send_sem, recv_sem):
    me = lax.axis_index("space")
    peers = [(me + d) % count for d in range(1, count)]
    greet("space", peers)
    copies = []
    for slot, peer in enumerate(peers):
        copy = pltpu.make_async_remote_copy(
            src_ref=block_ref, dst_ref=held.at[me], send_sem=send_sem.at[slot],
            recv_sem=recv_sem.at[slot], device_id={"space": peer},
            device_id_type=pl.DeviceIdType.MESH)
        copy.start()
        copies.append(copy)
    for copy in copies:
        copy.wait()
    held[me] = block_ref[...]
    out_ref[...] = held[...]


def space_gather(block, collective):
    count = lax.axis_size("space")
    return pl.pallas_call(
        functools.partial(gather_kernel, count),
        out_shape=jax.ShapeDtypeStruct((count, *block.shape), block.dtype),
        in_specs=[pl.BlockSpec(memory_space=pltpu.VMEM)],
        out_specs=pl.BlockSpec(memory_space=pltpu.VMEM),
        scratch_shapes=[
            pltpu.VMEM((count, *block.shape), block.dtype),
            pltpu.SemaphoreType.DMA((count - 1,)),
            pltpu.SemaphoreType.DMA((count - 1,)),
        ],
        compiler_params=pltpu.CompilerParams(collective_id=collective, has_side_effects=True),
        name="space_gather",
    )(block)


def route_kernel(count, rows_ref, out_ref, held, send_sem, recv_sem):
    me = lax.axis_index("inst")
    peers = [(me + d) % count for d in range(1, count)]
    greet("inst", peers)
    copies = []
    for slot, peer in enumerate(peers):
        copy = pltpu.make_async_remote_copy(
            src_ref=rows_ref.at[peer], dst_ref=held.at[me], send_sem=send_sem.at[slot],
            recv_sem=recv_sem.at[slot], device_id={"inst": peer},
            device_id_type=pl.DeviceIdType.MESH)
        copy.start()
        copies.append(copy)
    for copy in copies:
        copy.wait()
    held[me] = rows_ref[me]
    out_ref[...] = held[...]


def inst_route(rows, collective):
    count = lax.axis_size("inst")
    return pl.pallas_call(
        functools.partial(route_kernel, count),
        out_shape=jax.ShapeDtypeStruct(rows.shape, rows.dtype),
        in_specs=[pl.BlockSpec(memory_space=pltpu.VMEM)],
        out_specs=pl.BlockSpec(memory_space=pltpu.VMEM),
        scratch_shapes=[
            pltpu.VMEM(rows.shape, rows.dtype),
            pltpu.SemaphoreType.DMA((count - 1,)),
            pltpu.SemaphoreType.DMA((count - 1,)),
        ],
        compiler_params=pltpu.CompilerParams(collective_id=collective, has_side_effects=True),
        name="inst_route",
    )(rows)


def shards(
    psi_start,
    density,
    velocity,
    pressure,
    obs_pos,
    obs_weight,
    obs_harmonic,
    panel_pos,
    panel_normal,
    panel_cell,
    plane_nbr,
):
    inst_count = lax.axis_size("inst")
    inst_id = lax.axis_index("inst")
    space_id = lax.axis_index("space")
    times = jnp.array([2.0 * math.pi * i / inst_count for i in range(inst_count)], jnp.float32)
    local_obs = jnp.concatenate(
        [obs_pos, obs_weight, obs_harmonic[None].astype(jnp.float32)], axis=0
    )
    rows, per = local_obs.shape
    assert rows <= 8 and per <= 128
    packed = jnp.zeros((8, 128), jnp.float32).at[:rows, :per].set(local_obs)
    stacked = space_gather(packed, ITERS)
    observers = stacked[:, :rows, :per].transpose(1, 0, 2).reshape(rows, -1)
    owned_count = panel_normal.shape[1]
    piece = owned_count // inst_count
    assert piece * inst_count == owned_count and piece % 128 == 0
    mine = lax.dynamic_slice_in_dim(
        panel_pos, space_id * owned_count + inst_id * piece, piece, 1
    )
    normal = lax.dynamic_slice_in_dim(panel_normal, inst_id * piece, piece, 1)
    delta = mine[:, None, :] - observers[:3, :, None]
    dist2 = jnp.sum(delta * delta, axis=0)
    dist = jnp.sqrt(dist2)
    harm = observers[5]
    lag = harm[:, None] * (KWAVE * dist)
    along = jnp.sum(delta * normal[:, None, :], axis=0) * (RADIUS * RADIUS) / (dist2 * dist)
    pairs = jnp.concatenate([along * jnp.cos(lag), along * jnp.sin(lag)], axis=0)
    beat = times[:, None] * harm[None, :]
    cos_beat, sin_beat = jnp.cos(beat), jnp.sin(beat)
    real, imag = observers[3][None, :], observers[4][None, :]
    mixes = jnp.concatenate(
        [real * cos_beat + imag * sin_beat, real * sin_beat - imag * cos_beat], axis=1
    )
    partial = jnp.dot(mixes, pairs, precision=lax.Precision.HIGHEST)
    routed = inst_route(partial.reshape(inst_count, piece // 128, 128), ITERS + 1)
    weight = routed.reshape(owned_count)
    layers = psi_start.shape[2]
    plane = psi_start.shape[3]
    wall = cell_sum(weight, panel_cell, layers, plane)
    dens = density[0]
    vel = velocity[:, 0]
    state = conserved(dens, vel, pressure[0])
    slope = jnp.concatenate(
        [0.5 * jnp.sum(vel * vel, axis=0)[None], -vel, jnp.ones_like(dens)[None]], axis=0
    ) * (GAMMA - 1.0)
    source = slope * wall[None]
    _, pull = jax.vjp(fluxes, state)
    onehot = (plane_nbr[:, :, None] == jnp.arange(plane, dtype=jnp.int32)[None, None, :]).astype(
        jnp.bfloat16
    )
    row_entry = spectral_coeff(
        jnp.arange(inst_count, dtype=jnp.int32).astype(jnp.float32), float(inst_count)
    )
    psi = psi_start[:, 0]
    for step in range(ITERS):
        spectral_operator, below, above = instance_coupling(psi, row_entry, step)
        minus_a = jnp.concatenate([below, psi[:, :-1]], axis=1)
        plus_a = jnp.concatenate([psi[:, 1:], above], axis=1)
        plus_y, minus_y, plus_z, minus_z = plane_gather(psi, onehot)
        middle_point = pull(
            (0.5 * (minus_a - plus_a), 0.5 * (minus_y - plus_y), 0.5 * (minus_z - plus_z))
        )[0]
        spread = 6.0 * psi - (minus_a + plus_a + plus_y + minus_y + plus_z + minus_z)
        psi = psi - TAU * (middle_point + DISSIP * spread + spectral_operator + source)
    return psi[:, None]


def solution(mesh):
    placed = (
        P(None, "inst", "space", None),
        P("inst", "space", None),
        P(None, "inst", "space", None),
        P("inst", "space", None),
        P(None, "space"),
        P(None, "space"),
        P("space"),
        P(),
        P(None, "space"),
        P("space"),
        P(),
    )
    return jax.shard_map(
        shards,
        mesh=mesh,
        in_specs=placed,
        out_specs=P(None, "inst", "space", None),
        check_vma=False,
    )
```

```python
import functools
import math

import jax
import jax.numpy as jnp
from jax import lax
from jax.sharding import PartitionSpec as P
from jax.experimental import pallas as pl
from jax.experimental.pallas import tpu as pltpu

ITERS = 3


GAMMA = 1.4
KWAVE = 0.7
RADIUS = 10.0
TAU = 0.05
DISSIP = 0.25
OMEGA = 1.5
VISCO = 0.5


def padded_2(cells, sides, width):
    for axis, dim in sides:
        count = lax.axis_size(axis)
        head = lax.slice_in_dim(cells, 0, width, axis=dim)
        tail = lax.slice_in_dim(cells, cells.shape[dim] - width, cells.shape[dim], axis=dim)
        cells = jnp.concatenate(
            [
                lax.ppermute(tail, axis, [(i, (i + 1) % count) for i in range(count)]),
                cells,
                lax.ppermute(head, axis, [((i + 1) % count, i) for i in range(count)]),
            ],
            axis=dim,
        )
    return cells


def panel_block(observers, panels, time_now):
    delta = panels[:, None, :] - observers[:3, :, None]
    dist2 = jnp.sum(delta * delta, axis=0)
    dist = jnp.sqrt(dist2)
    harm = observers[5][:, None]
    phase = harm * (time_now - KWAVE * dist)
    amp = (
        (observers[3][:, None] * jnp.cos(phase) + observers[4][:, None] * jnp.sin(phase))
        * (RADIUS * RADIUS)
        / (dist2 * dist)
    )
    return jnp.sum(amp[None] * delta, axis=1)


def sensitivity(observers, panels, time_now):
    count = panels.shape[1]
    obs_count = observers.shape[1]
    block = math.gcd(count, max(128, 262144 // obs_count))
    split = panels.reshape(3, count // block, block).transpose(1, 0, 2)
    out = lax.map(lambda piece: panel_block(observers, piece, time_now), split)
    return out.transpose(1, 0, 2).reshape(3, count)


def conserved(density, velocity, pressure):
    moment = density[None] * velocity
    energy = pressure / (GAMMA - 1.0) + 0.5 * density * jnp.sum(velocity * velocity, axis=0)
    return jnp.concatenate([density[None], moment, energy[None]], axis=0)


def fluxes(state):
    dens = state[0]
    moment = state[1:4]
    energy = state[4]
    vel = moment / dens
    press = (GAMMA - 1.0) * (energy - 0.5 * jnp.sum(moment * vel, axis=0))
    result = []
    for axis_d in range(3):
        comps = [moment[axis_d]]
        for axis_e in range(3):
            term = moment[axis_e] * vel[axis_d]
            if axis_e == axis_d:
                term = term + press
            comps.append(term)
        comps.append((energy + press) * vel[axis_d])
        result.append(jnp.stack(comps))
    return tuple(result)


def spectral_coeff(offset, count):
    safe = jnp.where(offset == 0, 1.0, offset)
    angle = math.pi * safe / count
    even_odd_flag = 1.0 - 2.0 * jnp.mod(safe, 2.0)
    other = (
        -(OMEGA / 2.0) * even_odd_flag * jnp.cos(angle) / jnp.sin(angle)
        + VISCO * (OMEGA * OMEGA / 2.0) * even_odd_flag / jnp.sin(angle) ** 2
    )
    return jnp.where(offset == 0, VISCO * OMEGA * OMEGA * (count * count + 2.0) / 12.0, other)


def split_three(values):
    high = lax.reduce_precision(values, exponent_bits=8, mantissa_bits=7)
    rest = values - high
    middle = lax.reduce_precision(rest, exponent_bits=8, mantissa_bits=7)
    low = rest - middle
    return jnp.stack([high, middle, low]).astype(jnp.bfloat16)


def plane_gather(psi, onehot):
    comps, layers, plane = psi.shape
    parts = split_three(psi.reshape(comps * layers, plane))
    picked = jnp.einsum("pra,kba->kprb", parts, onehot,
                        preferred_element_type=jnp.float32)
    picked = (picked[:, 0] + picked[:, 1]) + picked[:, 2]
    return picked.reshape(onehot.shape[0], comps, layers, plane)


def cell_sum(weight, cell, layers, plane):
    by_layer = (cell // plane)[None, :] == jnp.arange(layers, dtype=jnp.int32)[:, None]
    spread = jnp.where(by_layer, weight[None, :], 0.0)
    picks = ((cell % plane)[:, None] == jnp.arange(plane, dtype=jnp.int32)[None, :]).astype(
        jnp.bfloat16
    )
    parts = split_three(spread)
    summed = jnp.einsum("plq,qb->plb", parts, picks, preferred_element_type=jnp.float32)
    return (summed[0] + summed[1]) + summed[2]


def greet(axis, peers):
    greet_all([{axis: peer} for peer in peers])


def greet_all(devices):
    barrier = pltpu.get_barrier_semaphore()
    for device in devices:
        pl.semaphore_signal(barrier, inc=1, device_id=device,
                            device_id_type=pl.DeviceIdType.MESH)
    pl.semaphore_wait(barrier, len(devices))


def coupling_kernel(count, inner, gather, psi_ref, table_ref, *refs):
    if gather:
        (block_ref, out_ref, below_ref, above_ref, stacked_ref, held, outbox, inbox, below, above,
         ring_send, ring_recv, cross_send, cross_recv, edge_send, edge_recv, gheld, gsend,
         grecv) = refs
    else:
        (out_ref, below_ref, above_ref, held, outbox, inbox, below, above, ring_send, ring_recv,
         cross_send, cross_recv, edge_send, edge_recv) = refs
    outer = count // inner
    me = lax.axis_index("inst")
    me_hi, me_lo = me // inner, me % inner
    ring = [me_hi * inner + (me_lo + d) % inner for d in range(1, inner)]
    ring_from = [me_hi * inner + (me_lo - d) % inner for d in range(1, inner)]
    partners = [((me_hi + h) % outer) * inner + me_lo for h in range(1, outer)]
    slabs = lax.axis_size("space")
    here = lax.axis_index("space")
    up, down = (here + 1) % slabs, (here + slabs - 1) % slabs
    if gather:
        others = [(here + d) % slabs for d in range(1, slabs)]
        greet_all([{"inst": p} for p in ring + partners] + [{"space": s} for s in others])
        gathered = []
        for slot, peer in enumerate(others):
            copy = pltpu.make_async_remote_copy(
                src_ref=block_ref, dst_ref=gheld.at[here], send_sem=gsend.at[slot],
                recv_sem=grecv.at[slot], device_id={"space": peer},
                device_id_type=pl.DeviceIdType.MESH)
            copy.start()
            gathered.append(copy)
    else:
        greet_all([{"inst": p} for p in ring + partners] + [{"space": up}, {"space": down}])
    last = psi_ref.shape[1] - 1
    edges = []
    for slot, (peer, layer, land) in enumerate(((up, last, below), (down, 0, above))):
        copy = pltpu.make_async_remote_copy(
            src_ref=psi_ref.at[:, pl.ds(layer, 1), :], dst_ref=land.at[:, pl.ds(layer, 1), :],
            send_sem=edge_send.at[slot], recv_sem=edge_recv.at[slot],
            device_id={"space": peer}, device_id_type=pl.DeviceIdType.MESH)
        copy.start()
        edges.append(copy)

    def coef(row, col):
        return table_ref[(row - col) % count]

    copies = []
    for slot, peer in enumerate(ring):
        copy = pltpu.make_async_remote_copy(
            src_ref=psi_ref, dst_ref=held.at[slot], send_sem=ring_send.at[slot],
            recv_sem=ring_recv.at[slot], device_id={"inst": peer},
            device_id_type=pl.DeviceIdType.MESH)
        copy.start()
        copies.append(copy)
    for copy in copies:
        copy.wait()
    cross = []
    for slot, partner in enumerate(partners):
        part = coef(partner, me) * psi_ref[...]
        for d, source in enumerate(ring_from):
            part = part + coef(partner, source) * held[d]
        outbox[slot] = part
        copy = pltpu.make_async_remote_copy(
            src_ref=outbox.at[slot], dst_ref=inbox.at[slot], send_sem=cross_send.at[slot],
            recv_sem=cross_recv.at[slot], device_id={"inst": partner},
            device_id_type=pl.DeviceIdType.MESH)
        copy.start()
        cross.append(copy)
    total = coef(me, me) * psi_ref[...]
    for d, source in enumerate(ring_from):
        total = total + coef(me, source) * held[d]
    for slot, copy in enumerate(cross):
        copy.wait()
        total = total + inbox[slot]
    out_ref[...] = total
    for copy in edges:
        copy.wait()
    below_ref[...] = below[:, last:, :]
    above_ref[...] = above[:, :1, :]
    if gather:
        for copy in gathered:
            copy.wait()
        gheld[here] = block_ref[...]
        stacked_ref[...] = gheld[...]


def instance_coupling(psi, table, step, block=None):
    count = lax.axis_size("inst")
    slabs = lax.axis_size("space")
    assert slabs > 2
    gather = block is not None
    inner = 4 if count % 4 == 0 else count
    outer = count // inner
    comps, layers, plane = psi.shape
    edge = jax.ShapeDtypeStruct((comps, 1, plane), psi.dtype)
    extra_out, extra_scratch, operands = (), [], (psi, table)
    if gather:
        extra_out = (jax.ShapeDtypeStruct((slabs, *block.shape), block.dtype),)
        extra_scratch = [
            pltpu.VMEM((slabs, *block.shape), block.dtype),
            pltpu.SemaphoreType.DMA((slabs - 1,)),
            pltpu.SemaphoreType.DMA((slabs - 1,)),
        ]
        operands = (psi, table, block)
    return pl.pallas_call(
        functools.partial(coupling_kernel, count, inner, gather),
        out_shape=(jax.ShapeDtypeStruct(psi.shape, psi.dtype), edge, edge) + extra_out,
        in_specs=[
            pl.BlockSpec(memory_space=pltpu.VMEM),
            pl.BlockSpec(memory_space=pltpu.SMEM),
        ] + [pl.BlockSpec(memory_space=pltpu.VMEM)] * gather,
        out_specs=[pl.BlockSpec(memory_space=pltpu.VMEM)] * (3 + gather),
        scratch_shapes=[
            pltpu.VMEM((inner - 1, *psi.shape), psi.dtype),
            pltpu.VMEM((max(outer - 1, 1), *psi.shape), psi.dtype),
            pltpu.VMEM((max(outer - 1, 1), *psi.shape), psi.dtype),
            pltpu.VMEM(psi.shape, psi.dtype),
            pltpu.VMEM(psi.shape, psi.dtype),
            pltpu.SemaphoreType.DMA((inner - 1,)),
            pltpu.SemaphoreType.DMA((inner - 1,)),
            pltpu.SemaphoreType.DMA((max(outer - 1, 1),)),
            pltpu.SemaphoreType.DMA((max(outer - 1, 1),)),
            pltpu.SemaphoreType.DMA((2,)),
            pltpu.SemaphoreType.DMA((2,)),
        ] + extra_scratch,
        compiler_params=pltpu.CompilerParams(collective_id=step, has_side_effects=True),
        name=f"instance_coupling_{step}",
    )(*operands)


def gather_kernel(count, block_ref, out_ref, held, send_sem, recv_sem):
    me = lax.axis_index("space")
    peers = [(me + d) % count for d in range(1, count)]
    greet("space", peers)
    copies = []
    for slot, peer in enumerate(peers):
        copy = pltpu.make_async_remote_copy(
            src_ref=block_ref, dst_ref=held.at[me], send_sem=send_sem.at[slot],
            recv_sem=recv_sem.at[slot], device_id={"space": peer},
            device_id_type=pl.DeviceIdType.MESH)
        copy.start()
        copies.append(copy)
    for copy in copies:
        copy.wait()
    held[me] = block_ref[...]
    out_ref[...] = held[...]


def space_gather(block, collective):
    count = lax.axis_size("space")
    return pl.pallas_call(
        functools.partial(gather_kernel, count),
        out_shape=jax.ShapeDtypeStruct((count, *block.shape), block.dtype),
        in_specs=[pl.BlockSpec(memory_space=pltpu.VMEM)],
        out_specs=pl.BlockSpec(memory_space=pltpu.VMEM),
        scratch_shapes=[
            pltpu.VMEM((count, *block.shape), block.dtype),
            pltpu.SemaphoreType.DMA((count - 1,)),
            pltpu.SemaphoreType.DMA((count - 1,)),
        ],
        compiler_params=pltpu.CompilerParams(collective_id=collective, has_side_effects=True),
        name="space_gather",
    )(block)


def route_kernel(count, rows_ref, out_ref, held, send_sem, recv_sem):
    me = lax.axis_index("inst")
    peers = [(me + d) % count for d in range(1, count)]
    greet("inst", peers)
    copies = []
    for slot, peer in enumerate(peers):
        copy = pltpu.make_async_remote_copy(
            src_ref=rows_ref.at[peer], dst_ref=held.at[me], send_sem=send_sem.at[slot],
            recv_sem=recv_sem.at[slot], device_id={"inst": peer},
            device_id_type=pl.DeviceIdType.MESH)
        copy.start()
        copies.append(copy)
    for copy in copies:
        copy.wait()
    held[me] = rows_ref[me]
    out_ref[...] = held[...]


def inst_route(rows, collective):
    count = lax.axis_size("inst")
    return pl.pallas_call(
        functools.partial(route_kernel, count),
        out_shape=jax.ShapeDtypeStruct(rows.shape, rows.dtype),
        in_specs=[pl.BlockSpec(memory_space=pltpu.VMEM)],
        out_specs=pl.BlockSpec(memory_space=pltpu.VMEM),
        scratch_shapes=[
            pltpu.VMEM(rows.shape, rows.dtype),
            pltpu.SemaphoreType.DMA((count - 1,)),
            pltpu.SemaphoreType.DMA((count - 1,)),
        ],
        compiler_params=pltpu.CompilerParams(collective_id=collective, has_side_effects=True),
        name="inst_route",
    )(rows)


def shards(
    psi_start,
    density,
    velocity,
    pressure,
    obs_pos,
    obs_weight,
    obs_harmonic,
    panel_pos,
    panel_normal,
    panel_cell,
    plane_nbr,
):
    inst_count = lax.axis_size("inst")
    inst_id = lax.axis_index("inst")
    space_id = lax.axis_index("space")
    times = jnp.array([2.0 * math.pi * i / inst_count for i in range(inst_count)], jnp.float32)
    local_obs = jnp.concatenate(
        [obs_pos, obs_weight, obs_harmonic[None].astype(jnp.float32)], axis=0
    )
    rows, per = local_obs.shape
    assert rows <= 8 and per <= 128
    packed = jnp.zeros((8, 128), jnp.float32).at[:rows, :per].set(local_obs)
    psi = psi_start[:, 0]
    row_entry = spectral_coeff(
        jnp.arange(inst_count, dtype=jnp.int32).astype(jnp.float32), float(inst_count)
    )
    first = instance_coupling(psi, row_entry, 0, packed)
    stacked = first[3]
    observers = stacked[:, :rows, :per].transpose(1, 0, 2).reshape(rows, -1)
    owned_count = panel_normal.shape[1]
    piece = owned_count // inst_count
    assert piece * inst_count == owned_count and piece % 128 == 0
    mine = lax.dynamic_slice_in_dim(
        panel_pos, space_id * owned_count + inst_id * piece, piece, 1
    )
    normal = lax.dynamic_slice_in_dim(panel_normal, inst_id * piece, piece, 1)
    delta = mine[:, None, :] - observers[:3, :, None]
    dist2 = jnp.sum(delta * delta, axis=0)
    dist = jnp.sqrt(dist2)
    harm = observers[5]
    lag = harm[:, None] * (KWAVE * dist)
    along = jnp.sum(delta * normal[:, None, :], axis=0) * (RADIUS * RADIUS) / (dist2 * dist)
    pairs = jnp.concatenate([along * jnp.cos(lag), along * jnp.sin(lag)], axis=0)
    beat = times[:, None] * harm[None, :]
    cos_beat, sin_beat = jnp.cos(beat), jnp.sin(beat)
    real, imag = observers[3][None, :], observers[4][None, :]
    mixes = jnp.concatenate(
        [real * cos_beat + imag * sin_beat, real * sin_beat - imag * cos_beat], axis=1
    )
    partial = jnp.dot(mixes, pairs, precision=lax.Precision.HIGHEST)
    routed = inst_route(partial.reshape(inst_count, piece // 128, 128), ITERS + 1)
    weight = routed.reshape(owned_count)
    layers = psi_start.shape[2]
    plane = psi_start.shape[3]
    wall = cell_sum(weight, panel_cell, layers, plane)
    dens = density[0]
    vel = velocity[:, 0]
    state = conserved(dens, vel, pressure[0])
    slope = jnp.concatenate(
        [0.5 * jnp.sum(vel * vel, axis=0)[None], -vel, jnp.ones_like(dens)[None]], axis=0
    ) * (GAMMA - 1.0)
    source = slope * wall[None]
    _, pull = jax.vjp(fluxes, state)
    onehot = (plane_nbr[:, :, None] == jnp.arange(plane, dtype=jnp.int32)[None, None, :]).astype(
        jnp.bfloat16
    )
    for step in range(ITERS):
        if step == 0:
            spectral_operator, below, above = first[:3]
        else:
            spectral_operator, below, above = instance_coupling(psi, row_entry, step)
        minus_a = jnp.concatenate([below, psi[:, :-1]], axis=1)
        plus_a = jnp.concatenate([psi[:, 1:], above], axis=1)
        plus_y, minus_y, plus_z, minus_z = plane_gather(psi, onehot)
        middle_point = pull(
            (0.5 * (minus_a - plus_a), 0.5 * (minus_y - plus_y), 0.5 * (minus_z - plus_z))
        )[0]
        spread = 6.0 * psi - (minus_a + plus_a + plus_y + minus_y + plus_z + minus_z)
        psi = psi - TAU * (middle_point + DISSIP * spread + spectral_operator + source)
    return psi[:, None]


def solution(mesh):
    placed = (
        P(None, "inst", "space", None),
        P("inst", "space", None),
        P(None, "inst", "space", None),
        P("inst", "space", None),
        P(None, "space"),
        P(None, "space"),
        P("space"),
        P(),
        P(None, "space"),
        P("space"),
        P(),
    )
    return jax.shard_map(
        shards,
        mesh=mesh,
        in_specs=placed,
        out_specs=P(None, "inst", "space", None),
        check_vma=False,
    )
```

```python
import functools
import math

import jax
import jax.numpy as jnp
from jax import lax
from jax.sharding import PartitionSpec as P
from jax.experimental import pallas as pl
from jax.experimental.pallas import tpu as pltpu

ITERS = 3


GAMMA = 1.4
KWAVE = 0.7
RADIUS = 10.0
TAU = 0.05
DISSIP = 0.25
OMEGA = 1.5
VISCO = 0.5


def padded_2(cells, sides, width):
    for axis, dim in sides:
        count = lax.axis_size(axis)
        head = lax.slice_in_dim(cells, 0, width, axis=dim)
        tail = lax.slice_in_dim(cells, cells.shape[dim] - width, cells.shape[dim], axis=dim)
        cells = jnp.concatenate(
            [
                lax.ppermute(tail, axis, [(i, (i + 1) % count) for i in range(count)]),
                cells,
                lax.ppermute(head, axis, [((i + 1) % count, i) for i in range(count)]),
            ],
            axis=dim,
        )
    return cells


def panel_block(observers, panels, time_now):
    delta = panels[:, None, :] - observers[:3, :, None]
    dist2 = jnp.sum(delta * delta, axis=0)
    dist = jnp.sqrt(dist2)
    harm = observers[5][:, None]
    phase = harm * (time_now - KWAVE * dist)
    amp = (
        (observers[3][:, None] * jnp.cos(phase) + observers[4][:, None] * jnp.sin(phase))
        * (RADIUS * RADIUS)
        / (dist2 * dist)
    )
    return jnp.sum(amp[None] * delta, axis=1)


def sensitivity(observers, panels, time_now):
    count = panels.shape[1]
    obs_count = observers.shape[1]
    block = math.gcd(count, max(128, 262144 // obs_count))
    split = panels.reshape(3, count // block, block).transpose(1, 0, 2)
    out = lax.map(lambda piece: panel_block(observers, piece, time_now), split)
    return out.transpose(1, 0, 2).reshape(3, count)


def conserved(density, velocity, pressure):
    moment = density[None] * velocity
    energy = pressure / (GAMMA - 1.0) + 0.5 * density * jnp.sum(velocity * velocity, axis=0)
    return jnp.concatenate([density[None], moment, energy[None]], axis=0)


def fluxes(state):
    dens = state[0]
    moment = state[1:4]
    energy = state[4]
    vel = moment / dens
    press = (GAMMA - 1.0) * (energy - 0.5 * jnp.sum(moment * vel, axis=0))
    result = []
    for axis_d in range(3):
        comps = [moment[axis_d]]
        for axis_e in range(3):
            term = moment[axis_e] * vel[axis_d]
            if axis_e == axis_d:
                term = term + press
            comps.append(term)
        comps.append((energy + press) * vel[axis_d])
        result.append(jnp.stack(comps))
    return tuple(result)


def spectral_coeff(offset, count):
    safe = jnp.where(offset == 0, 1.0, offset)
    angle = math.pi * safe / count
    even_odd_flag = 1.0 - 2.0 * jnp.mod(safe, 2.0)
    other = (
        -(OMEGA / 2.0) * even_odd_flag * jnp.cos(angle) / jnp.sin(angle)
        + VISCO * (OMEGA * OMEGA / 2.0) * even_odd_flag / jnp.sin(angle) ** 2
    )
    return jnp.where(offset == 0, VISCO * OMEGA * OMEGA * (count * count + 2.0) / 12.0, other)


def split_three(values):
    high = lax.reduce_precision(values, exponent_bits=8, mantissa_bits=7)
    rest = values - high
    middle = lax.reduce_precision(rest, exponent_bits=8, mantissa_bits=7)
    low = rest - middle
    return jnp.stack([high, middle, low]).astype(jnp.bfloat16)


def plane_gather(psi, onehot):
    comps, layers, plane = psi.shape
    parts = split_three(psi.reshape(comps * layers, plane))
    picked = jnp.einsum("pra,kba->kprb", parts, onehot,
                        preferred_element_type=jnp.float32)
    picked = (picked[:, 0] + picked[:, 1]) + picked[:, 2]
    return picked.reshape(onehot.shape[0], comps, layers, plane)


def cell_sum(weight, cell, layers, plane):
    by_layer = (cell // plane)[None, :] == jnp.arange(layers, dtype=jnp.int32)[:, None]
    spread = jnp.where(by_layer, weight[None, :], 0.0)
    picks = ((cell % plane)[:, None] == jnp.arange(plane, dtype=jnp.int32)[None, :]).astype(
        jnp.bfloat16
    )
    parts = split_three(spread)
    summed = jnp.einsum("plq,qb->plb", parts, picks, preferred_element_type=jnp.float32)
    return (summed[0] + summed[1]) + summed[2]


def greet(axis, peers):
    greet_all([{axis: peer} for peer in peers])


def greet_all(devices):
    barrier = pltpu.get_barrier_semaphore()
    for device in devices:
        pl.semaphore_signal(barrier, inc=1, device_id=device,
                            device_id_type=pl.DeviceIdType.MESH)
    pl.semaphore_wait(barrier, len(devices))


def coupling_kernel(count, inner, gather, psi_ref, table_ref, *refs):
    if gather:
        (block_ref, out_ref, below_ref, above_ref, stacked_ref, held, outbox, inbox, below, above,
         ring_send, ring_recv, cross_send, cross_recv, edge_send, edge_recv, gheld, gsend,
         grecv) = refs
    else:
        (out_ref, below_ref, above_ref, held, outbox, inbox, below, above, ring_send, ring_recv,
         cross_send, cross_recv, edge_send, edge_recv) = refs
    outer = count // inner
    me = lax.axis_index("inst")
    me_hi, me_lo = me // inner, me % inner
    ring = [me_hi * inner + (me_lo + d) % inner for d in range(1, inner)]
    ring_from = [me_hi * inner + (me_lo - d) % inner for d in range(1, inner)]
    partners = [((me_hi + h) % outer) * inner + me_lo for h in range(1, outer)]
    slabs = lax.axis_size("space")
    here = lax.axis_index("space")
    up, down = (here + 1) % slabs, (here + slabs - 1) % slabs
    if gather:
        others = [(here + d) % slabs for d in range(1, slabs)]
        greet_all([{"inst": p} for p in ring + partners] + [{"space": s} for s in others])
        gathered = []
        for slot, peer in enumerate(others):
            copy = pltpu.make_async_remote_copy(
                src_ref=block_ref, dst_ref=gheld.at[here], send_sem=gsend.at[slot],
                recv_sem=grecv.at[slot], device_id={"space": peer},
                device_id_type=pl.DeviceIdType.MESH)
            copy.start()
            gathered.append(copy)
    else:
        greet_all([{"inst": p} for p in ring + partners] + [{"space": up}, {"space": down}])
    last = psi_ref.shape[1] - 1
    edges = []
    for slot, (peer, layer, land) in enumerate(((up, last, below), (down, 0, above))):
        copy = pltpu.make_async_remote_copy(
            src_ref=psi_ref.at[:, pl.ds(layer, 1), :], dst_ref=land.at[:, pl.ds(layer, 1), :],
            send_sem=edge_send.at[slot], recv_sem=edge_recv.at[slot],
            device_id={"space": peer}, device_id_type=pl.DeviceIdType.MESH)
        copy.start()
        edges.append(copy)

    def coef(row, col):
        return table_ref[(row - col) % count]

    halves = 2
    width = psi_ref.shape[2] // halves
    spans = [pl.ds(h * width, width) for h in range(halves)]
    copies = []
    for h, cols in enumerate(spans):
        row = []
        for slot, peer in enumerate(ring):
            at = h * len(ring) + slot
            copy = pltpu.make_async_remote_copy(
                src_ref=psi_ref.at[:, :, cols], dst_ref=held.at[slot, :, :, cols],
                send_sem=ring_send.at[at], recv_sem=ring_recv.at[at],
                device_id={"inst": peer}, device_id_type=pl.DeviceIdType.MESH)
            copy.start()
            row.append(copy)
        copies.append(row)
    cross = []
    for h, cols in enumerate(spans):
        for copy in copies[h]:
            copy.wait()
        for slot, partner in enumerate(partners):
            at = h * len(partners) + slot
            part = coef(partner, me) * psi_ref[:, :, cols]
            for d, source in enumerate(ring_from):
                part = part + coef(partner, source) * held[d, :, :, cols]
            outbox[slot, :, :, cols] = part
            copy = pltpu.make_async_remote_copy(
                src_ref=outbox.at[slot, :, :, cols], dst_ref=inbox.at[slot, :, :, cols],
                send_sem=cross_send.at[at], recv_sem=cross_recv.at[at],
                device_id={"inst": partner}, device_id_type=pl.DeviceIdType.MESH)
            copy.start()
            cross.append((h, slot, copy))
    for h, cols in enumerate(spans):
        total = coef(me, me) * psi_ref[:, :, cols]
        for d, source in enumerate(ring_from):
            total = total + coef(me, source) * held[d, :, :, cols]
        out_ref[:, :, cols] = total
    for h, slot, copy in cross:
        copy.wait()
        out_ref[:, :, spans[h]] = out_ref[:, :, spans[h]] + inbox[slot, :, :, spans[h]]
    for copy in edges:
        copy.wait()
    below_ref[...] = below[:, last:, :]
    above_ref[...] = above[:, :1, :]
    if gather:
        for copy in gathered:
            copy.wait()
        gheld[here] = block_ref[...]
        stacked_ref[...] = gheld[...]


def instance_coupling(psi, table, step, block=None):
    count = lax.axis_size("inst")
    slabs = lax.axis_size("space")
    assert slabs > 2
    gather = block is not None
    inner = 4 if count % 4 == 0 else count
    outer = count // inner
    comps, layers, plane = psi.shape
    edge = jax.ShapeDtypeStruct((comps, 1, plane), psi.dtype)
    extra_out, extra_scratch, operands = (), [], (psi, table)
    if gather:
        extra_out = (jax.ShapeDtypeStruct((slabs, *block.shape), block.dtype),)
        extra_scratch = [
            pltpu.VMEM((slabs, *block.shape), block.dtype),
            pltpu.SemaphoreType.DMA((slabs - 1,)),
            pltpu.SemaphoreType.DMA((slabs - 1,)),
        ]
        operands = (psi, table, block)
    return pl.pallas_call(
        functools.partial(coupling_kernel, count, inner, gather),
        out_shape=(jax.ShapeDtypeStruct(psi.shape, psi.dtype), edge, edge) + extra_out,
        in_specs=[
            pl.BlockSpec(memory_space=pltpu.VMEM),
            pl.BlockSpec(memory_space=pltpu.SMEM),
        ] + [pl.BlockSpec(memory_space=pltpu.VMEM)] * gather,
        out_specs=[pl.BlockSpec(memory_space=pltpu.VMEM)] * (3 + gather),
        scratch_shapes=[
            pltpu.VMEM((inner - 1, *psi.shape), psi.dtype),
            pltpu.VMEM((max(outer - 1, 1), *psi.shape), psi.dtype),
            pltpu.VMEM((max(outer - 1, 1), *psi.shape), psi.dtype),
            pltpu.VMEM(psi.shape, psi.dtype),
            pltpu.VMEM(psi.shape, psi.dtype),
            pltpu.SemaphoreType.DMA((2 * (inner - 1),)),
            pltpu.SemaphoreType.DMA((2 * (inner - 1),)),
            pltpu.SemaphoreType.DMA((2 * max(outer - 1, 1),)),
            pltpu.SemaphoreType.DMA((2 * max(outer - 1, 1),)),
            pltpu.SemaphoreType.DMA((2,)),
            pltpu.SemaphoreType.DMA((2,)),
        ] + extra_scratch,
        compiler_params=pltpu.CompilerParams(collective_id=step, has_side_effects=True),
        name=f"instance_coupling_{step}",
    )(*operands)


def gather_kernel(count, block_ref, out_ref, held, send_sem, recv_sem):
    me = lax.axis_index("space")
    peers = [(me + d) % count for d in range(1, count)]
    greet("space", peers)
    copies = []
    for slot, peer in enumerate(peers):
        copy = pltpu.make_async_remote_copy(
            src_ref=block_ref, dst_ref=held.at[me], send_sem=send_sem.at[slot],
            recv_sem=recv_sem.at[slot], device_id={"space": peer},
            device_id_type=pl.DeviceIdType.MESH)
        copy.start()
        copies.append(copy)
    for copy in copies:
        copy.wait()
    held[me] = block_ref[...]
    out_ref[...] = held[...]


def space_gather(block, collective):
    count = lax.axis_size("space")
    return pl.pallas_call(
        functools.partial(gather_kernel, count),
        out_shape=jax.ShapeDtypeStruct((count, *block.shape), block.dtype),
        in_specs=[pl.BlockSpec(memory_space=pltpu.VMEM)],
        out_specs=pl.BlockSpec(memory_space=pltpu.VMEM),
        scratch_shapes=[
            pltpu.VMEM((count, *block.shape), block.dtype),
            pltpu.SemaphoreType.DMA((count - 1,)),
            pltpu.SemaphoreType.DMA((count - 1,)),
        ],
        compiler_params=pltpu.CompilerParams(collective_id=collective, has_side_effects=True),
        name="space_gather",
    )(block)


def route_kernel(count, rows_ref, out_ref, held, send_sem, recv_sem):
    me = lax.axis_index("inst")
    peers = [(me + d) % count for d in range(1, count)]
    greet("inst", peers)
    copies = []
    for slot, peer in enumerate(peers):
        copy = pltpu.make_async_remote_copy(
            src_ref=rows_ref.at[peer], dst_ref=held.at[me], send_sem=send_sem.at[slot],
            recv_sem=recv_sem.at[slot], device_id={"inst": peer},
            device_id_type=pl.DeviceIdType.MESH)
        copy.start()
        copies.append(copy)
    for copy in copies:
        copy.wait()
    held[me] = rows_ref[me]
    out_ref[...] = held[...]


def inst_route(rows, collective):
    count = lax.axis_size("inst")
    return pl.pallas_call(
        functools.partial(route_kernel, count),
        out_shape=jax.ShapeDtypeStruct(rows.shape, rows.dtype),
        in_specs=[pl.BlockSpec(memory_space=pltpu.VMEM)],
        out_specs=pl.BlockSpec(memory_space=pltpu.VMEM),
        scratch_shapes=[
            pltpu.VMEM(rows.shape, rows.dtype),
            pltpu.SemaphoreType.DMA((count - 1,)),
            pltpu.SemaphoreType.DMA((count - 1,)),
        ],
        compiler_params=pltpu.CompilerParams(collective_id=collective, has_side_effects=True),
        name="inst_route",
    )(rows)


def shards(
    psi_start,
    density,
    velocity,
    pressure,
    obs_pos,
    obs_weight,
    obs_harmonic,
    panel_pos,
    panel_normal,
    panel_cell,
    plane_nbr,
):
    inst_count = lax.axis_size("inst")
    inst_id = lax.axis_index("inst")
    space_id = lax.axis_index("space")
    times = jnp.array([2.0 * math.pi * i / inst_count for i in range(inst_count)], jnp.float32)
    local_obs = jnp.concatenate(
        [obs_pos, obs_weight, obs_harmonic[None].astype(jnp.float32)], axis=0
    )
    rows, per = local_obs.shape
    assert rows <= 8 and per <= 128
    packed = jnp.zeros((8, 128), jnp.float32).at[:rows, :per].set(local_obs)
    psi = psi_start[:, 0]
    row_entry = spectral_coeff(
        jnp.arange(inst_count, dtype=jnp.int32).astype(jnp.float32), float(inst_count)
    )
    first = instance_coupling(psi, row_entry, 0, packed)
    stacked = first[3]
    observers = stacked[:, :rows, :per].transpose(1, 0, 2).reshape(rows, -1)
    owned_count = panel_normal.shape[1]
    piece = owned_count // inst_count
    assert piece * inst_count == owned_count and piece % 128 == 0
    mine = lax.dynamic_slice_in_dim(
        panel_pos, space_id * owned_count + inst_id * piece, piece, 1
    )
    normal = lax.dynamic_slice_in_dim(panel_normal, inst_id * piece, piece, 1)
    delta = mine[:, None, :] - observers[:3, :, None]
    dist2 = jnp.sum(delta * delta, axis=0)
    dist = jnp.sqrt(dist2)
    harm = observers[5]
    lag = harm[:, None] * (KWAVE * dist)
    along = jnp.sum(delta * normal[:, None, :], axis=0) * (RADIUS * RADIUS) / (dist2 * dist)
    pairs = jnp.concatenate([along * jnp.cos(lag), along * jnp.sin(lag)], axis=0)
    beat = times[:, None] * harm[None, :]
    cos_beat, sin_beat = jnp.cos(beat), jnp.sin(beat)
    real, imag = observers[3][None, :], observers[4][None, :]
    mixes = jnp.concatenate(
        [real * cos_beat + imag * sin_beat, real * sin_beat - imag * cos_beat], axis=1
    )
    partial = jnp.dot(mixes, pairs, precision=lax.Precision.HIGHEST)
    routed = inst_route(partial.reshape(inst_count, piece // 128, 128), ITERS + 1)
    weight = routed.reshape(owned_count)
    layers = psi_start.shape[2]
    plane = psi_start.shape[3]
    wall = cell_sum(weight, panel_cell, layers, plane)
    dens = density[0]
    vel = velocity[:, 0]
    state = conserved(dens, vel, pressure[0])
    slope = jnp.concatenate(
        [0.5 * jnp.sum(vel * vel, axis=0)[None], -vel, jnp.ones_like(dens)[None]], axis=0
    ) * (GAMMA - 1.0)
    source = slope * wall[None]
    _, pull = jax.vjp(fluxes, state)
    onehot = (plane_nbr[:, :, None] == jnp.arange(plane, dtype=jnp.int32)[None, None, :]).astype(
        jnp.bfloat16
    )
    for step in range(ITERS):
        if step == 0:
            spectral_operator, below, above = first[:3]
        else:
            spectral_operator, below, above = instance_coupling(psi, row_entry, step)
        minus_a = jnp.concatenate([below, psi[:, :-1]], axis=1)
        plus_a = jnp.concatenate([psi[:, 1:], above], axis=1)
        plus_y, minus_y, plus_z, minus_z = plane_gather(psi, onehot)
        middle_point = pull(
            (0.5 * (minus_a - plus_a), 0.5 * (minus_y - plus_y), 0.5 * (minus_z - plus_z))
        )[0]
        spread = 6.0 * psi - (minus_a + plus_a + plus_y + minus_y + plus_z + minus_z)
        psi = psi - TAU * (middle_point + DISSIP * spread + spectral_operator + source)
    return psi[:, None]


def solution(mesh):
    placed = (
        P(None, "inst", "space", None),
        P("inst", "space", None),
        P(None, "inst", "space", None),
        P("inst", "space", None),
        P(None, "space"),
        P(None, "space"),
        P("space"),
        P(),
        P(None, "space"),
        P("space"),
        P(),
    )
    return jax.shard_map(
        shards,
        mesh=mesh,
        in_specs=placed,
        out_specs=P(None, "inst", "space", None),
        check_vma=False,
    )
```

```python
import functools
import math

import jax
import jax.numpy as jnp
from jax import lax
from jax.sharding import PartitionSpec as P
from jax.experimental import pallas as pl
from jax.experimental.pallas import tpu as pltpu

ITERS = 3
PIECES = 4


GAMMA = 1.4
KWAVE = 0.7
RADIUS = 10.0
TAU = 0.05
DISSIP = 0.25
OMEGA = 1.5
VISCO = 0.5


def padded_2(cells, sides, width):
    for axis, dim in sides:
        count = lax.axis_size(axis)
        head = lax.slice_in_dim(cells, 0, width, axis=dim)
        tail = lax.slice_in_dim(cells, cells.shape[dim] - width, cells.shape[dim], axis=dim)
        cells = jnp.concatenate(
            [
                lax.ppermute(tail, axis, [(i, (i + 1) % count) for i in range(count)]),
                cells,
                lax.ppermute(head, axis, [((i + 1) % count, i) for i in range(count)]),
            ],
            axis=dim,
        )
    return cells


def panel_block(observers, panels, time_now):
    delta = panels[:, None, :] - observers[:3, :, None]
    dist2 = jnp.sum(delta * delta, axis=0)
    dist = jnp.sqrt(dist2)
    harm = observers[5][:, None]
    phase = harm * (time_now - KWAVE * dist)
    amp = (
        (observers[3][:, None] * jnp.cos(phase) + observers[4][:, None] * jnp.sin(phase))
        * (RADIUS * RADIUS)
        / (dist2 * dist)
    )
    return jnp.sum(amp[None] * delta, axis=1)


def sensitivity(observers, panels, time_now):
    count = panels.shape[1]
    obs_count = observers.shape[1]
    block = math.gcd(count, max(128, 262144 // obs_count))
    split = panels.reshape(3, count // block, block).transpose(1, 0, 2)
    out = lax.map(lambda piece: panel_block(observers, piece, time_now), split)
    return out.transpose(1, 0, 2).reshape(3, count)


def conserved(density, velocity, pressure):
    moment = density[None] * velocity
    energy = pressure / (GAMMA - 1.0) + 0.5 * density * jnp.sum(velocity * velocity, axis=0)
    return jnp.concatenate([density[None], moment, energy[None]], axis=0)


def fluxes(state):
    dens = state[0]
    moment = state[1:4]
    energy = state[4]
    vel = moment / dens
    press = (GAMMA - 1.0) * (energy - 0.5 * jnp.sum(moment * vel, axis=0))
    result = []
    for axis_d in range(3):
        comps = [moment[axis_d]]
        for axis_e in range(3):
            term = moment[axis_e] * vel[axis_d]
            if axis_e == axis_d:
                term = term + press
            comps.append(term)
        comps.append((energy + press) * vel[axis_d])
        result.append(jnp.stack(comps))
    return tuple(result)


def spectral_coeff(offset, count):
    safe = jnp.where(offset == 0, 1.0, offset)
    angle = math.pi * safe / count
    even_odd_flag = 1.0 - 2.0 * jnp.mod(safe, 2.0)
    other = (
        -(OMEGA / 2.0) * even_odd_flag * jnp.cos(angle) / jnp.sin(angle)
        + VISCO * (OMEGA * OMEGA / 2.0) * even_odd_flag / jnp.sin(angle) ** 2
    )
    return jnp.where(offset == 0, VISCO * OMEGA * OMEGA * (count * count + 2.0) / 12.0, other)


def split_three(values):
    high = lax.reduce_precision(values, exponent_bits=8, mantissa_bits=7)
    rest = values - high
    middle = lax.reduce_precision(rest, exponent_bits=8, mantissa_bits=7)
    low = rest - middle
    return jnp.stack([high, middle, low]).astype(jnp.bfloat16)


def plane_gather(psi, onehot):
    comps, layers, plane = psi.shape
    parts = split_three(psi.reshape(comps * layers, plane))
    picked = jnp.einsum("pra,kba->kprb", parts, onehot,
                        preferred_element_type=jnp.float32)
    picked = (picked[:, 0] + picked[:, 1]) + picked[:, 2]
    return picked.reshape(onehot.shape[0], comps, layers, plane)


def cell_sum(weight, cell, layers, plane):
    by_layer = (cell // plane)[None, :] == jnp.arange(layers, dtype=jnp.int32)[:, None]
    spread = jnp.where(by_layer, weight[None, :], 0.0)
    picks = ((cell % plane)[:, None] == jnp.arange(plane, dtype=jnp.int32)[None, :]).astype(
        jnp.bfloat16
    )
    parts = split_three(spread)
    summed = jnp.einsum("plq,qb->plb", parts, picks, preferred_element_type=jnp.float32)
    return (summed[0] + summed[1]) + summed[2]


def greet(axis, peers):
    greet_all([{axis: peer} for peer in peers])


def greet_all(devices):
    barrier = pltpu.get_barrier_semaphore()
    for device in devices:
        pl.semaphore_signal(barrier, inc=1, device_id=device,
                            device_id_type=pl.DeviceIdType.MESH)
    pl.semaphore_wait(barrier, len(devices))


def coupling_kernel(count, inner, gather, psi_ref, table_ref, *refs):
    if gather:
        (block_ref, out_ref, below_ref, above_ref, stacked_ref, held, outbox, inbox, below, above,
         ring_send, ring_recv, cross_send, cross_recv, edge_send, edge_recv, gheld, gsend,
         grecv) = refs
    else:
        (out_ref, below_ref, above_ref, held, outbox, inbox, below, above, ring_send, ring_recv,
         cross_send, cross_recv, edge_send, edge_recv) = refs
    outer = count // inner
    me = lax.axis_index("inst")
    me_hi, me_lo = me // inner, me % inner
    ring = [me_hi * inner + (me_lo + d) % inner for d in range(1, inner)]
    ring_from = [me_hi * inner + (me_lo - d) % inner for d in range(1, inner)]
    partners = [((me_hi + h) % outer) * inner + me_lo for h in range(1, outer)]
    slabs = lax.axis_size("space")
    here = lax.axis_index("space")
    up, down = (here + 1) % slabs, (here + slabs - 1) % slabs
    if gather:
        others = [(here + d) % slabs for d in range(1, slabs)]
        greet_all([{"inst": p} for p in ring + partners] + [{"space": s} for s in others])
        gathered = []
        for slot, peer in enumerate(others):
            copy = pltpu.make_async_remote_copy(
                src_ref=block_ref, dst_ref=gheld.at[here], send_sem=gsend.at[slot],
                recv_sem=grecv.at[slot], device_id={"space": peer},
                device_id_type=pl.DeviceIdType.MESH)
            copy.start()
            gathered.append(copy)
    else:
        greet_all([{"inst": p} for p in ring + partners] + [{"space": up}, {"space": down}])
    last = psi_ref.shape[1] - 1
    edges = []
    for slot, (peer, layer, land) in enumerate(((up, last, below), (down, 0, above))):
        copy = pltpu.make_async_remote_copy(
            src_ref=psi_ref.at[:, pl.ds(layer, 1), :], dst_ref=land.at[:, pl.ds(layer, 1), :],
            send_sem=edge_send.at[slot], recv_sem=edge_recv.at[slot],
            device_id={"space": peer}, device_id_type=pl.DeviceIdType.MESH)
        copy.start()
        edges.append(copy)

    def coef(row, col):
        return table_ref[(row - col) % count]

    halves = PIECES
    width = psi_ref.shape[2] // halves
    spans = [pl.ds(h * width, width) for h in range(halves)]
    copies = []
    for h, cols in enumerate(spans):
        row = []
        for slot, peer in enumerate(ring):
            at = h * len(ring) + slot
            copy = pltpu.make_async_remote_copy(
                src_ref=psi_ref.at[:, :, cols], dst_ref=held.at[slot, :, :, cols],
                send_sem=ring_send.at[at], recv_sem=ring_recv.at[at],
                device_id={"inst": peer}, device_id_type=pl.DeviceIdType.MESH)
            copy.start()
            row.append(copy)
        copies.append(row)
    cross = []
    for h, cols in enumerate(spans):
        for copy in copies[h]:
            copy.wait()
        for slot, partner in enumerate(partners):
            at = h * len(partners) + slot
            part = coef(partner, me) * psi_ref[:, :, cols]
            for d, source in enumerate(ring_from):
                part = part + coef(partner, source) * held[d, :, :, cols]
            outbox[slot, :, :, cols] = part
            copy = pltpu.make_async_remote_copy(
                src_ref=outbox.at[slot, :, :, cols], dst_ref=inbox.at[slot, :, :, cols],
                send_sem=cross_send.at[at], recv_sem=cross_recv.at[at],
                device_id={"inst": partner}, device_id_type=pl.DeviceIdType.MESH)
            copy.start()
            cross.append((h, slot, copy))
    for h, cols in enumerate(spans):
        total = coef(me, me) * psi_ref[:, :, cols]
        for d, source in enumerate(ring_from):
            total = total + coef(me, source) * held[d, :, :, cols]
        out_ref[:, :, cols] = total
    for h, slot, copy in cross:
        copy.wait()
        out_ref[:, :, spans[h]] = out_ref[:, :, spans[h]] + inbox[slot, :, :, spans[h]]
    for copy in edges:
        copy.wait()
    below_ref[...] = below[:, last:, :]
    above_ref[...] = above[:, :1, :]
    if gather:
        for copy in gathered:
            copy.wait()
        gheld[here] = block_ref[...]
        stacked_ref[...] = gheld[...]


def instance_coupling(psi, table, step, block=None):
    count = lax.axis_size("inst")
    slabs = lax.axis_size("space")
    assert slabs > 2
    gather = block is not None
    inner = 4 if count % 4 == 0 else count
    outer = count // inner
    comps, layers, plane = psi.shape
    edge = jax.ShapeDtypeStruct((comps, 1, plane), psi.dtype)
    extra_out, extra_scratch, operands = (), [], (psi, table)
    if gather:
        extra_out = (jax.ShapeDtypeStruct((slabs, *block.shape), block.dtype),)
        extra_scratch = [
            pltpu.VMEM((slabs, *block.shape), block.dtype),
            pltpu.SemaphoreType.DMA((slabs - 1,)),
            pltpu.SemaphoreType.DMA((slabs - 1,)),
        ]
        operands = (psi, table, block)
    return pl.pallas_call(
        functools.partial(coupling_kernel, count, inner, gather),
        out_shape=(jax.ShapeDtypeStruct(psi.shape, psi.dtype), edge, edge) + extra_out,
        in_specs=[
            pl.BlockSpec(memory_space=pltpu.VMEM),
            pl.BlockSpec(memory_space=pltpu.SMEM),
        ] + [pl.BlockSpec(memory_space=pltpu.VMEM)] * gather,
        out_specs=[pl.BlockSpec(memory_space=pltpu.VMEM)] * (3 + gather),
        scratch_shapes=[
            pltpu.VMEM((inner - 1, *psi.shape), psi.dtype),
            pltpu.VMEM((max(outer - 1, 1), *psi.shape), psi.dtype),
            pltpu.VMEM((max(outer - 1, 1), *psi.shape), psi.dtype),
            pltpu.VMEM(psi.shape, psi.dtype),
            pltpu.VMEM(psi.shape, psi.dtype),
            pltpu.SemaphoreType.DMA((PIECES * (inner - 1),)),
            pltpu.SemaphoreType.DMA((PIECES * (inner - 1),)),
            pltpu.SemaphoreType.DMA((PIECES * max(outer - 1, 1),)),
            pltpu.SemaphoreType.DMA((PIECES * max(outer - 1, 1),)),
            pltpu.SemaphoreType.DMA((2,)),
            pltpu.SemaphoreType.DMA((2,)),
        ] + extra_scratch,
        compiler_params=pltpu.CompilerParams(collective_id=step, has_side_effects=True),
        name=f"instance_coupling_{step}",
    )(*operands)


def gather_kernel(count, block_ref, out_ref, held, send_sem, recv_sem):
    me = lax.axis_index("space")
    peers = [(me + d) % count for d in range(1, count)]
    greet("space", peers)
    copies = []
    for slot, peer in enumerate(peers):
        copy = pltpu.make_async_remote_copy(
            src_ref=block_ref, dst_ref=held.at[me], send_sem=send_sem.at[slot],
            recv_sem=recv_sem.at[slot], device_id={"space": peer},
            device_id_type=pl.DeviceIdType.MESH)
        copy.start()
        copies.append(copy)
    for copy in copies:
        copy.wait()
    held[me] = block_ref[...]
    out_ref[...] = held[...]


def space_gather(block, collective):
    count = lax.axis_size("space")
    return pl.pallas_call(
        functools.partial(gather_kernel, count),
        out_shape=jax.ShapeDtypeStruct((count, *block.shape), block.dtype),
        in_specs=[pl.BlockSpec(memory_space=pltpu.VMEM)],
        out_specs=pl.BlockSpec(memory_space=pltpu.VMEM),
        scratch_shapes=[
            pltpu.VMEM((count, *block.shape), block.dtype),
            pltpu.SemaphoreType.DMA((count - 1,)),
            pltpu.SemaphoreType.DMA((count - 1,)),
        ],
        compiler_params=pltpu.CompilerParams(collective_id=collective, has_side_effects=True),
        name="space_gather",
    )(block)


def route_kernel(count, rows_ref, out_ref, held, send_sem, recv_sem):
    me = lax.axis_index("inst")
    peers = [(me + d) % count for d in range(1, count)]
    greet("inst", peers)
    copies = []
    for slot, peer in enumerate(peers):
        copy = pltpu.make_async_remote_copy(
            src_ref=rows_ref.at[peer], dst_ref=held.at[me], send_sem=send_sem.at[slot],
            recv_sem=recv_sem.at[slot], device_id={"inst": peer},
            device_id_type=pl.DeviceIdType.MESH)
        copy.start()
        copies.append(copy)
    for copy in copies:
        copy.wait()
    held[me] = rows_ref[me]
    out_ref[...] = held[...]


def inst_route(rows, collective):
    count = lax.axis_size("inst")
    return pl.pallas_call(
        functools.partial(route_kernel, count),
        out_shape=jax.ShapeDtypeStruct(rows.shape, rows.dtype),
        in_specs=[pl.BlockSpec(memory_space=pltpu.VMEM)],
        out_specs=pl.BlockSpec(memory_space=pltpu.VMEM),
        scratch_shapes=[
            pltpu.VMEM(rows.shape, rows.dtype),
            pltpu.SemaphoreType.DMA((count - 1,)),
            pltpu.SemaphoreType.DMA((count - 1,)),
        ],
        compiler_params=pltpu.CompilerParams(collective_id=collective, has_side_effects=True),
        name="inst_route",
    )(rows)


def shards(
    psi_start,
    density,
    velocity,
    pressure,
    obs_pos,
    obs_weight,
    obs_harmonic,
    panel_pos,
    panel_normal,
    panel_cell,
    plane_nbr,
):
    inst_count = lax.axis_size("inst")
    inst_id = lax.axis_index("inst")
    space_id = lax.axis_index("space")
    times = jnp.array([2.0 * math.pi * i / inst_count for i in range(inst_count)], jnp.float32)
    local_obs = jnp.concatenate(
        [obs_pos, obs_weight, obs_harmonic[None].astype(jnp.float32)], axis=0
    )
    rows, per = local_obs.shape
    assert rows <= 8 and per <= 128
    packed = jnp.zeros((8, 128), jnp.float32).at[:rows, :per].set(local_obs)
    psi = psi_start[:, 0]
    row_entry = spectral_coeff(
        jnp.arange(inst_count, dtype=jnp.int32).astype(jnp.float32), float(inst_count)
    )
    first = instance_coupling(psi, row_entry, 0, packed)
    stacked = first[3]
    observers = stacked[:, :rows, :per].transpose(1, 0, 2).reshape(rows, -1)
    owned_count = panel_normal.shape[1]
    piece = owned_count // inst_count
    assert piece * inst_count == owned_count and piece % 128 == 0
    mine = lax.dynamic_slice_in_dim(
        panel_pos, space_id * owned_count + inst_id * piece, piece, 1
    )
    normal = lax.dynamic_slice_in_dim(panel_normal, inst_id * piece, piece, 1)
    delta = mine[:, None, :] - observers[:3, :, None]
    dist2 = jnp.sum(delta * delta, axis=0)
    dist = jnp.sqrt(dist2)
    harm = observers[5]
    lag = harm[:, None] * (KWAVE * dist)
    along = jnp.sum(delta * normal[:, None, :], axis=0) * (RADIUS * RADIUS) / (dist2 * dist)
    pairs = jnp.concatenate([along * jnp.cos(lag), along * jnp.sin(lag)], axis=0)
    beat = times[:, None] * harm[None, :]
    cos_beat, sin_beat = jnp.cos(beat), jnp.sin(beat)
    real, imag = observers[3][None, :], observers[4][None, :]
    mixes = jnp.concatenate(
        [real * cos_beat + imag * sin_beat, real * sin_beat - imag * cos_beat], axis=1
    )
    partial = jnp.dot(mixes, pairs, precision=lax.Precision.HIGHEST)
    routed = inst_route(partial.reshape(inst_count, piece // 128, 128), ITERS + 1)
    weight = routed.reshape(owned_count)
    layers = psi_start.shape[2]
    plane = psi_start.shape[3]
    wall = cell_sum(weight, panel_cell, layers, plane)
    dens = density[0]
    vel = velocity[:, 0]
    state = conserved(dens, vel, pressure[0])
    slope = jnp.concatenate(
        [0.5 * jnp.sum(vel * vel, axis=0)[None], -vel, jnp.ones_like(dens)[None]], axis=0
    ) * (GAMMA - 1.0)
    source = slope * wall[None]
    _, pull = jax.vjp(fluxes, state)
    onehot = (plane_nbr[:, :, None] == jnp.arange(plane, dtype=jnp.int32)[None, None, :]).astype(
        jnp.bfloat16
    )
    for step in range(ITERS):
        if step == 0:
            spectral_operator, below, above = first[:3]
        else:
            spectral_operator, below, above = instance_coupling(psi, row_entry, step)
        minus_a = jnp.concatenate([below, psi[:, :-1]], axis=1)
        plus_a = jnp.concatenate([psi[:, 1:], above], axis=1)
        plus_y, minus_y, plus_z, minus_z = plane_gather(psi, onehot)
        middle_point = pull(
            (0.5 * (minus_a - plus_a), 0.5 * (minus_y - plus_y), 0.5 * (minus_z - plus_z))
        )[0]
        spread = 6.0 * psi - (minus_a + plus_a + plus_y + minus_y + plus_z + minus_z)
        psi = psi - TAU * (middle_point + DISSIP * spread + spectral_operator + source)
    return psi[:, None]


def solution(mesh):
    placed = (
        P(None, "inst", "space", None),
        P("inst", "space", None),
        P(None, "inst", "space", None),
        P("inst", "space", None),
        P(None, "space"),
        P(None, "space"),
        P("space"),
        P(),
        P(None, "space"),
        P("space"),
        P(),
    )
    return jax.shard_map(
        shards,
        mesh=mesh,
        in_specs=placed,
        out_specs=P(None, "inst", "space", None),
        check_vma=False,
    )
```

```python
import functools
import math

import jax
import jax.numpy as jnp
from jax import lax
from jax.sharding import PartitionSpec as P
from jax.experimental import pallas as pl
from jax.experimental.pallas import tpu as pltpu

ITERS = 3
PIECES = 8


GAMMA = 1.4
KWAVE = 0.7
RADIUS = 10.0
TAU = 0.05
DISSIP = 0.25
OMEGA = 1.5
VISCO = 0.5


def padded_2(cells, sides, width):
    for axis, dim in sides:
        count = lax.axis_size(axis)
        head = lax.slice_in_dim(cells, 0, width, axis=dim)
        tail = lax.slice_in_dim(cells, cells.shape[dim] - width, cells.shape[dim], axis=dim)
        cells = jnp.concatenate(
            [
                lax.ppermute(tail, axis, [(i, (i + 1) % count) for i in range(count)]),
                cells,
                lax.ppermute(head, axis, [((i + 1) % count, i) for i in range(count)]),
            ],
            axis=dim,
        )
    return cells


def panel_block(observers, panels, time_now):
    delta = panels[:, None, :] - observers[:3, :, None]
    dist2 = jnp.sum(delta * delta, axis=0)
    dist = jnp.sqrt(dist2)
    harm = observers[5][:, None]
    phase = harm * (time_now - KWAVE * dist)
    amp = (
        (observers[3][:, None] * jnp.cos(phase) + observers[4][:, None] * jnp.sin(phase))
        * (RADIUS * RADIUS)
        / (dist2 * dist)
    )
    return jnp.sum(amp[None] * delta, axis=1)


def sensitivity(observers, panels, time_now):
    count = panels.shape[1]
    obs_count = observers.shape[1]
    block = math.gcd(count, max(128, 262144 // obs_count))
    split = panels.reshape(3, count // block, block).transpose(1, 0, 2)
    out = lax.map(lambda piece: panel_block(observers, piece, time_now), split)
    return out.transpose(1, 0, 2).reshape(3, count)


def conserved(density, velocity, pressure):
    moment = density[None] * velocity
    energy = pressure / (GAMMA - 1.0) + 0.5 * density * jnp.sum(velocity * velocity, axis=0)
    return jnp.concatenate([density[None], moment, energy[None]], axis=0)


def fluxes(state):
    dens = state[0]
    moment = state[1:4]
    energy = state[4]
    vel = moment / dens
    press = (GAMMA - 1.0) * (energy - 0.5 * jnp.sum(moment * vel, axis=0))
    result = []
    for axis_d in range(3):
        comps = [moment[axis_d]]
        for axis_e in range(3):
            term = moment[axis_e] * vel[axis_d]
            if axis_e == axis_d:
                term = term + press
            comps.append(term)
        comps.append((energy + press) * vel[axis_d])
        result.append(jnp.stack(comps))
    return tuple(result)


def spectral_coeff(offset, count):
    safe = jnp.where(offset == 0, 1.0, offset)
    angle = math.pi * safe / count
    even_odd_flag = 1.0 - 2.0 * jnp.mod(safe, 2.0)
    other = (
        -(OMEGA / 2.0) * even_odd_flag * jnp.cos(angle) / jnp.sin(angle)
        + VISCO * (OMEGA * OMEGA / 2.0) * even_odd_flag / jnp.sin(angle) ** 2
    )
    return jnp.where(offset == 0, VISCO * OMEGA * OMEGA * (count * count + 2.0) / 12.0, other)


def split_three(values):
    high = lax.reduce_precision(values, exponent_bits=8, mantissa_bits=7)
    rest = values - high
    middle = lax.reduce_precision(rest, exponent_bits=8, mantissa_bits=7)
    low = rest - middle
    return jnp.stack([high, middle, low]).astype(jnp.bfloat16)


def plane_gather(psi, onehot):
    comps, layers, plane = psi.shape
    parts = split_three(psi.reshape(comps * layers, plane))
    picked = jnp.einsum("pra,kba->kprb", parts, onehot,
                        preferred_element_type=jnp.float32)
    picked = (picked[:, 0] + picked[:, 1]) + picked[:, 2]
    return picked.reshape(onehot.shape[0], comps, layers, plane)


def cell_sum(weight, cell, layers, plane):
    by_layer = (cell // plane)[None, :] == jnp.arange(layers, dtype=jnp.int32)[:, None]
    spread = jnp.where(by_layer, weight[None, :], 0.0)
    picks = ((cell % plane)[:, None] == jnp.arange(plane, dtype=jnp.int32)[None, :]).astype(
        jnp.bfloat16
    )
    parts = split_three(spread)
    summed = jnp.einsum("plq,qb->plb", parts, picks, preferred_element_type=jnp.float32)
    return (summed[0] + summed[1]) + summed[2]


def greet(axis, peers):
    greet_all([{axis: peer} for peer in peers])


def greet_all(devices):
    barrier = pltpu.get_barrier_semaphore()
    for device in devices:
        pl.semaphore_signal(barrier, inc=1, device_id=device,
                            device_id_type=pl.DeviceIdType.MESH)
    pl.semaphore_wait(barrier, len(devices))


def coupling_kernel(count, inner, gather, psi_ref, table_ref, *refs):
    if gather:
        (block_ref, out_ref, below_ref, above_ref, stacked_ref, held, outbox, inbox, below, above,
         ring_send, ring_recv, cross_send, cross_recv, edge_send, edge_recv, gheld, gsend,
         grecv) = refs
    else:
        (out_ref, below_ref, above_ref, held, outbox, inbox, below, above, ring_send, ring_recv,
         cross_send, cross_recv, edge_send, edge_recv) = refs
    outer = count // inner
    me = lax.axis_index("inst")
    me_hi, me_lo = me // inner, me % inner
    ring = [me_hi * inner + (me_lo + d) % inner for d in range(1, inner)]
    ring_from = [me_hi * inner + (me_lo - d) % inner for d in range(1, inner)]
    partners = [((me_hi + h) % outer) * inner + me_lo for h in range(1, outer)]
    slabs = lax.axis_size("space")
    here = lax.axis_index("space")
    up, down = (here + 1) % slabs, (here + slabs - 1) % slabs
    if gather:
        others = [(here + d) % slabs for d in range(1, slabs)]
        greet_all([{"inst": p} for p in ring + partners] + [{"space": s} for s in others])
        gathered = []
        for slot, peer in enumerate(others):
            copy = pltpu.make_async_remote_copy(
                src_ref=block_ref, dst_ref=gheld.at[here], send_sem=gsend.at[slot],
                recv_sem=grecv.at[slot], device_id={"space": peer},
                device_id_type=pl.DeviceIdType.MESH)
            copy.start()
            gathered.append(copy)
    else:
        greet_all([{"inst": p} for p in ring + partners] + [{"space": up}, {"space": down}])
    last = psi_ref.shape[1] - 1
    edges = []
    for slot, (peer, layer, land) in enumerate(((up, last, below), (down, 0, above))):
        copy = pltpu.make_async_remote_copy(
            src_ref=psi_ref.at[:, pl.ds(layer, 1), :], dst_ref=land.at[:, pl.ds(layer, 1), :],
            send_sem=edge_send.at[slot], recv_sem=edge_recv.at[slot],
            device_id={"space": peer}, device_id_type=pl.DeviceIdType.MESH)
        copy.start()
        edges.append(copy)

    def coef(row, col):
        return table_ref[(row - col) % count]

    halves = PIECES
    width = psi_ref.shape[2] // halves
    spans = [pl.ds(h * width, width) for h in range(halves)]
    copies = []
    for h, cols in enumerate(spans):
        row = []
        for slot, peer in enumerate(ring):
            at = h * len(ring) + slot
            copy = pltpu.make_async_remote_copy(
                src_ref=psi_ref.at[:, :, cols], dst_ref=held.at[slot, :, :, cols],
                send_sem=ring_send.at[at], recv_sem=ring_recv.at[at],
                device_id={"inst": peer}, device_id_type=pl.DeviceIdType.MESH)
            copy.start()
            row.append(copy)
        copies.append(row)
    cross = []
    for h, cols in enumerate(spans):
        for copy in copies[h]:
            copy.wait()
        for slot, partner in enumerate(partners):
            at = h * len(partners) + slot
            part = coef(partner, me) * psi_ref[:, :, cols]
            for d, source in enumerate(ring_from):
                part = part + coef(partner, source) * held[d, :, :, cols]
            outbox[slot, :, :, cols] = part
            copy = pltpu.make_async_remote_copy(
                src_ref=outbox.at[slot, :, :, cols], dst_ref=inbox.at[slot, :, :, cols],
                send_sem=cross_send.at[at], recv_sem=cross_recv.at[at],
                device_id={"inst": partner}, device_id_type=pl.DeviceIdType.MESH)
            copy.start()
            cross.append((h, slot, copy))
    for h, cols in enumerate(spans):
        total = coef(me, me) * psi_ref[:, :, cols]
        for d, source in enumerate(ring_from):
            total = total + coef(me, source) * held[d, :, :, cols]
        out_ref[:, :, cols] = total
    for h, slot, copy in cross:
        copy.wait()
        out_ref[:, :, spans[h]] = out_ref[:, :, spans[h]] + inbox[slot, :, :, spans[h]]
    for copy in edges:
        copy.wait()
    below_ref[...] = below[:, last:, :]
    above_ref[...] = above[:, :1, :]
    if gather:
        for copy in gathered:
            copy.wait()
        gheld[here] = block_ref[...]
        stacked_ref[...] = gheld[...]


def instance_coupling(psi, table, step, block=None):
    count = lax.axis_size("inst")
    slabs = lax.axis_size("space")
    assert slabs > 2
    gather = block is not None
    inner = 4 if count % 4 == 0 else count
    outer = count // inner
    comps, layers, plane = psi.shape
    edge = jax.ShapeDtypeStruct((comps, 1, plane), psi.dtype)
    extra_out, extra_scratch, operands = (), [], (psi, table)
    if gather:
        extra_out = (jax.ShapeDtypeStruct((slabs, *block.shape), block.dtype),)
        extra_scratch = [
            pltpu.VMEM((slabs, *block.shape), block.dtype),
            pltpu.SemaphoreType.DMA((slabs - 1,)),
            pltpu.SemaphoreType.DMA((slabs - 1,)),
        ]
        operands = (psi, table, block)
    return pl.pallas_call(
        functools.partial(coupling_kernel, count, inner, gather),
        out_shape=(jax.ShapeDtypeStruct(psi.shape, psi.dtype), edge, edge) + extra_out,
        in_specs=[
            pl.BlockSpec(memory_space=pltpu.VMEM),
            pl.BlockSpec(memory_space=pltpu.SMEM),
        ] + [pl.BlockSpec(memory_space=pltpu.VMEM)] * gather,
        out_specs=[pl.BlockSpec(memory_space=pltpu.VMEM)] * (3 + gather),
        scratch_shapes=[
            pltpu.VMEM((inner - 1, *psi.shape), psi.dtype),
            pltpu.VMEM((max(outer - 1, 1), *psi.shape), psi.dtype),
            pltpu.VMEM((max(outer - 1, 1), *psi.shape), psi.dtype),
            pltpu.VMEM(psi.shape, psi.dtype),
            pltpu.VMEM(psi.shape, psi.dtype),
            pltpu.SemaphoreType.DMA((PIECES * (inner - 1),)),
            pltpu.SemaphoreType.DMA((PIECES * (inner - 1),)),
            pltpu.SemaphoreType.DMA((PIECES * max(outer - 1, 1),)),
            pltpu.SemaphoreType.DMA((PIECES * max(outer - 1, 1),)),
            pltpu.SemaphoreType.DMA((2,)),
            pltpu.SemaphoreType.DMA((2,)),
        ] + extra_scratch,
        compiler_params=pltpu.CompilerParams(collective_id=step, has_side_effects=True),
        name=f"instance_coupling_{step}",
    )(*operands)


def gather_kernel(count, block_ref, out_ref, held, send_sem, recv_sem):
    me = lax.axis_index("space")
    peers = [(me + d) % count for d in range(1, count)]
    greet("space", peers)
    copies = []
    for slot, peer in enumerate(peers):
        copy = pltpu.make_async_remote_copy(
            src_ref=block_ref, dst_ref=held.at[me], send_sem=send_sem.at[slot],
            recv_sem=recv_sem.at[slot], device_id={"space": peer},
            device_id_type=pl.DeviceIdType.MESH)
        copy.start()
        copies.append(copy)
    for copy in copies:
        copy.wait()
    held[me] = block_ref[...]
    out_ref[...] = held[...]


def space_gather(block, collective):
    count = lax.axis_size("space")
    return pl.pallas_call(
        functools.partial(gather_kernel, count),
        out_shape=jax.ShapeDtypeStruct((count, *block.shape), block.dtype),
        in_specs=[pl.BlockSpec(memory_space=pltpu.VMEM)],
        out_specs=pl.BlockSpec(memory_space=pltpu.VMEM),
        scratch_shapes=[
            pltpu.VMEM((count, *block.shape), block.dtype),
            pltpu.SemaphoreType.DMA((count - 1,)),
            pltpu.SemaphoreType.DMA((count - 1,)),
        ],
        compiler_params=pltpu.CompilerParams(collective_id=collective, has_side_effects=True),
        name="space_gather",
    )(block)


def route_kernel(count, rows_ref, out_ref, held, send_sem, recv_sem):
    me = lax.axis_index("inst")
    peers = [(me + d) % count for d in range(1, count)]
    greet("inst", peers)
    copies = []
    for slot, peer in enumerate(peers):
        copy = pltpu.make_async_remote_copy(
            src_ref=rows_ref.at[peer], dst_ref=held.at[me], send_sem=send_sem.at[slot],
            recv_sem=recv_sem.at[slot], device_id={"inst": peer},
            device_id_type=pl.DeviceIdType.MESH)
        copy.start()
        copies.append(copy)
    for copy in copies:
        copy.wait()
    held[me] = rows_ref[me]
    out_ref[...] = held[...]


def inst_route(rows, collective):
    count = lax.axis_size("inst")
    return pl.pallas_call(
        functools.partial(route_kernel, count),
        out_shape=jax.ShapeDtypeStruct(rows.shape, rows.dtype),
        in_specs=[pl.BlockSpec(memory_space=pltpu.VMEM)],
        out_specs=pl.BlockSpec(memory_space=pltpu.VMEM),
        scratch_shapes=[
            pltpu.VMEM(rows.shape, rows.dtype),
            pltpu.SemaphoreType.DMA((count - 1,)),
            pltpu.SemaphoreType.DMA((count - 1,)),
        ],
        compiler_params=pltpu.CompilerParams(collective_id=collective, has_side_effects=True),
        name="inst_route",
    )(rows)


def shards(
    psi_start,
    density,
    velocity,
    pressure,
    obs_pos,
    obs_weight,
    obs_harmonic,
    panel_pos,
    panel_normal,
    panel_cell,
    plane_nbr,
):
    inst_count = lax.axis_size("inst")
    inst_id = lax.axis_index("inst")
    space_id = lax.axis_index("space")
    times = jnp.array([2.0 * math.pi * i / inst_count for i in range(inst_count)], jnp.float32)
    local_obs = jnp.concatenate(
        [obs_pos, obs_weight, obs_harmonic[None].astype(jnp.float32)], axis=0
    )
    rows, per = local_obs.shape
    assert rows <= 8 and per <= 128
    packed = jnp.zeros((8, 128), jnp.float32).at[:rows, :per].set(local_obs)
    psi = psi_start[:, 0]
    row_entry = spectral_coeff(
        jnp.arange(inst_count, dtype=jnp.int32).astype(jnp.float32), float(inst_count)
    )
    first = instance_coupling(psi, row_entry, 0, packed)
    stacked = first[3]
    observers = stacked[:, :rows, :per].transpose(1, 0, 2).reshape(rows, -1)
    owned_count = panel_normal.shape[1]
    piece = owned_count // inst_count
    assert piece * inst_count == owned_count and piece % 128 == 0
    mine = lax.dynamic_slice_in_dim(
        panel_pos, space_id * owned_count + inst_id * piece, piece, 1
    )
    normal = lax.dynamic_slice_in_dim(panel_normal, inst_id * piece, piece, 1)
    delta = mine[:, None, :] - observers[:3, :, None]
    dist2 = jnp.sum(delta * delta, axis=0)
    dist = jnp.sqrt(dist2)
    harm = observers[5]
    lag = harm[:, None] * (KWAVE * dist)
    along = jnp.sum(delta * normal[:, None, :], axis=0) * (RADIUS * RADIUS) / (dist2 * dist)
    pairs = jnp.concatenate([along * jnp.cos(lag), along * jnp.sin(lag)], axis=0)
    beat = times[:, None] * harm[None, :]
    cos_beat, sin_beat = jnp.cos(beat), jnp.sin(beat)
    real, imag = observers[3][None, :], observers[4][None, :]
    mixes = jnp.concatenate(
        [real * cos_beat + imag * sin_beat, real * sin_beat - imag * cos_beat], axis=1
    )
    partial = jnp.dot(mixes, pairs, precision=lax.Precision.HIGHEST)
    routed = inst_route(partial.reshape(inst_count, piece // 128, 128), ITERS + 1)
    weight = routed.reshape(owned_count)
    layers = psi_start.shape[2]
    plane = psi_start.shape[3]
    wall = cell_sum(weight, panel_cell, layers, plane)
    dens = density[0]
    vel = velocity[:, 0]
    state = conserved(dens, vel, pressure[0])
    slope = jnp.concatenate(
        [0.5 * jnp.sum(vel * vel, axis=0)[None], -vel, jnp.ones_like(dens)[None]], axis=0
    ) * (GAMMA - 1.0)
    source = slope * wall[None]
    _, pull = jax.vjp(fluxes, state)
    onehot = (plane_nbr[:, :, None] == jnp.arange(plane, dtype=jnp.int32)[None, None, :]).astype(
        jnp.bfloat16
    )
    for step in range(ITERS):
        if step == 0:
            spectral_operator, below, above = first[:3]
        else:
            spectral_operator, below, above = instance_coupling(psi, row_entry, step)
        minus_a = jnp.concatenate([below, psi[:, :-1]], axis=1)
        plus_a = jnp.concatenate([psi[:, 1:], above], axis=1)
        plus_y, minus_y, plus_z, minus_z = plane_gather(psi, onehot)
        middle_point = pull(
            (0.5 * (minus_a - plus_a), 0.5 * (minus_y - plus_y), 0.5 * (minus_z - plus_z))
        )[0]
        spread = 6.0 * psi - (minus_a + plus_a + plus_y + minus_y + plus_z + minus_z)
        psi = psi - TAU * (middle_point + DISSIP * spread + spectral_operator + source)
    return psi[:, None]


def solution(mesh):
    placed = (
        P(None, "inst", "space", None),
        P("inst", "space", None),
        P(None, "inst", "space", None),
        P("inst", "space", None),
        P(None, "space"),
        P(None, "space"),
        P("space"),
        P(),
        P(None, "space"),
        P("space"),
        P(),
    )
    return jax.shard_map(
        shards,
        mesh=mesh,
        in_specs=placed,
        out_specs=P(None, "inst", "space", None),
        check_vma=False,
    )
```

```python
import functools
import math

import jax
import jax.numpy as jnp
from jax import lax
from jax.sharding import PartitionSpec as P
from jax.experimental import pallas as pl
from jax.experimental.pallas import tpu as pltpu

ITERS = 3
PIECES = 4


GAMMA = 1.4
KWAVE = 0.7
RADIUS = 10.0
TAU = 0.05
DISSIP = 0.25
OMEGA = 1.5
VISCO = 0.5


def padded_2(cells, sides, width):
    for axis, dim in sides:
        count = lax.axis_size(axis)
        head = lax.slice_in_dim(cells, 0, width, axis=dim)
        tail = lax.slice_in_dim(cells, cells.shape[dim] - width, cells.shape[dim], axis=dim)
        cells = jnp.concatenate(
            [
                lax.ppermute(tail, axis, [(i, (i + 1) % count) for i in range(count)]),
                cells,
                lax.ppermute(head, axis, [((i + 1) % count, i) for i in range(count)]),
            ],
            axis=dim,
        )
    return cells


def panel_block(observers, panels, time_now):
    delta = panels[:, None, :] - observers[:3, :, None]
    dist2 = jnp.sum(delta * delta, axis=0)
    dist = jnp.sqrt(dist2)
    harm = observers[5][:, None]
    phase = harm * (time_now - KWAVE * dist)
    amp = (
        (observers[3][:, None] * jnp.cos(phase) + observers[4][:, None] * jnp.sin(phase))
        * (RADIUS * RADIUS)
        / (dist2 * dist)
    )
    return jnp.sum(amp[None] * delta, axis=1)


def sensitivity(observers, panels, time_now):
    count = panels.shape[1]
    obs_count = observers.shape[1]
    block = math.gcd(count, max(128, 262144 // obs_count))
    split = panels.reshape(3, count // block, block).transpose(1, 0, 2)
    out = lax.map(lambda piece: panel_block(observers, piece, time_now), split)
    return out.transpose(1, 0, 2).reshape(3, count)


def conserved(density, velocity, pressure):
    moment = density[None] * velocity
    energy = pressure / (GAMMA - 1.0) + 0.5 * density * jnp.sum(velocity * velocity, axis=0)
    return jnp.concatenate([density[None], moment, energy[None]], axis=0)


def fluxes(state):
    dens = state[0]
    moment = state[1:4]
    energy = state[4]
    vel = moment / dens
    press = (GAMMA - 1.0) * (energy - 0.5 * jnp.sum(moment * vel, axis=0))
    result = []
    for axis_d in range(3):
        comps = [moment[axis_d]]
        for axis_e in range(3):
            term = moment[axis_e] * vel[axis_d]
            if axis_e == axis_d:
                term = term + press
            comps.append(term)
        comps.append((energy + press) * vel[axis_d])
        result.append(jnp.stack(comps))
    return tuple(result)


def spectral_coeff(offset, count):
    safe = jnp.where(offset == 0, 1.0, offset)
    angle = math.pi * safe / count
    even_odd_flag = 1.0 - 2.0 * jnp.mod(safe, 2.0)
    other = (
        -(OMEGA / 2.0) * even_odd_flag * jnp.cos(angle) / jnp.sin(angle)
        + VISCO * (OMEGA * OMEGA / 2.0) * even_odd_flag / jnp.sin(angle) ** 2
    )
    return jnp.where(offset == 0, VISCO * OMEGA * OMEGA * (count * count + 2.0) / 12.0, other)


def split_three(values):
    high = lax.reduce_precision(values, exponent_bits=8, mantissa_bits=7)
    rest = values - high
    middle = lax.reduce_precision(rest, exponent_bits=8, mantissa_bits=7)
    low = rest - middle
    return jnp.stack([high, middle, low]).astype(jnp.bfloat16)


def plane_gather(psi, onehot):
    comps, layers, plane = psi.shape
    parts = split_three(psi.reshape(comps * layers, plane))
    picked = jnp.einsum("pra,kba->kprb", parts, onehot,
                        preferred_element_type=jnp.float32)
    picked = (picked[:, 0] + picked[:, 1]) + picked[:, 2]
    return picked.reshape(onehot.shape[0], comps, layers, plane)


def cell_sum(weight, cell, layers, plane):
    by_layer = (cell // plane)[None, :] == jnp.arange(layers, dtype=jnp.int32)[:, None]
    spread = jnp.where(by_layer, weight[None, :], 0.0)
    picks = ((cell % plane)[:, None] == jnp.arange(plane, dtype=jnp.int32)[None, :]).astype(
        jnp.bfloat16
    )
    parts = split_three(spread)
    summed = jnp.einsum("plq,qb->plb", parts, picks, preferred_element_type=jnp.float32)
    return (summed[0] + summed[1]) + summed[2]


def greet(axis, peers):
    greet_all([{axis: peer} for peer in peers])


def greet_all(devices):
    barrier = pltpu.get_barrier_semaphore()
    for device in devices:
        pl.semaphore_signal(barrier, inc=1, device_id=device,
                            device_id_type=pl.DeviceIdType.MESH)
    pl.semaphore_wait(barrier, len(devices))


def coupling_kernel(count, inner, gather, psi_ref, table_ref, *refs):
    if gather:
        (block_ref, out_ref, below_ref, above_ref, stacked_ref, held, outbox, inbox, below, above,
         ring_send, ring_recv, cross_send, cross_recv, edge_send, edge_recv, gheld, gsend,
         grecv) = refs
    else:
        (out_ref, below_ref, above_ref, held, outbox, inbox, below, above, ring_send, ring_recv,
         cross_send, cross_recv, edge_send, edge_recv) = refs
    outer = count // inner
    me = lax.axis_index("inst")
    me_hi, me_lo = me // inner, me % inner
    ring = [me_hi * inner + (me_lo + d) % inner for d in range(1, inner)]
    ring_from = [me_hi * inner + (me_lo - d) % inner for d in range(1, inner)]
    partners = [((me_hi + h) % outer) * inner + me_lo for h in range(1, outer)]
    slabs = lax.axis_size("space")
    here = lax.axis_index("space")
    up, down = (here + 1) % slabs, (here + slabs - 1) % slabs
    if gather:
        others = [(here + d) % slabs for d in range(1, slabs)]
        greet_all([{"inst": p} for p in ring + partners] + [{"space": s} for s in others])
        gathered = []
        for slot, peer in enumerate(others):
            copy = pltpu.make_async_remote_copy(
                src_ref=block_ref, dst_ref=gheld.at[here], send_sem=gsend.at[slot],
                recv_sem=grecv.at[slot], device_id={"space": peer},
                device_id_type=pl.DeviceIdType.MESH)
            copy.start()
            gathered.append(copy)
    else:
        greet_all([{"inst": p} for p in ring + partners] + [{"space": up}, {"space": down}])
    last = psi_ref.shape[1] - 1
    edges = []
    for slot, (peer, layer, land) in enumerate(((up, last, below), (down, 0, above))):
        copy = pltpu.make_async_remote_copy(
            src_ref=psi_ref.at[:, pl.ds(layer, 1), :], dst_ref=land.at[:, pl.ds(layer, 1), :],
            send_sem=edge_send.at[slot], recv_sem=edge_recv.at[slot],
            device_id={"space": peer}, device_id_type=pl.DeviceIdType.MESH)
        copy.start()
        edges.append(copy)

    def coef(row, col):
        return table_ref[(row - col) % count]

    halves = PIECES
    width = psi_ref.shape[2] // halves
    spans = [pl.ds(h * width, width) for h in range(halves)]
    copies = []
    for h, cols in enumerate(spans):
        row = []
        for slot, peer in enumerate(ring):
            at = h * len(ring) + slot
            copy = pltpu.make_async_remote_copy(
                src_ref=psi_ref.at[:, :, cols], dst_ref=held.at[slot, :, :, cols],
                send_sem=ring_send.at[at], recv_sem=ring_recv.at[at],
                device_id={"inst": peer}, device_id_type=pl.DeviceIdType.MESH)
            copy.start()
            row.append(copy)
        copies.append(row)
    cross = []
    for h, cols in enumerate(spans):
        for copy in copies[h]:
            copy.wait()
        for slot, partner in enumerate(partners):
            at = h * len(partners) + slot
            part = coef(partner, me) * psi_ref[:, :, cols]
            for d, source in enumerate(ring_from):
                part = part + coef(partner, source) * held[d, :, :, cols]
            outbox[slot, :, :, cols] = part
            copy = pltpu.make_async_remote_copy(
                src_ref=outbox.at[slot, :, :, cols], dst_ref=inbox.at[slot, :, :, cols],
                send_sem=cross_send.at[at], recv_sem=cross_recv.at[at],
                device_id={"inst": partner}, device_id_type=pl.DeviceIdType.MESH)
            copy.start()
            cross.append((h, slot, copy))
    for h, cols in enumerate(spans):
        total = coef(me, me) * psi_ref[:, :, cols]
        for d, source in enumerate(ring_from):
            total = total + coef(me, source) * held[d, :, :, cols]
        out_ref[:, :, cols] = total
    for h, slot, copy in cross:
        copy.wait()
        out_ref[:, :, spans[h]] = out_ref[:, :, spans[h]] + inbox[slot, :, :, spans[h]]
    for copy in edges:
        copy.wait()
    below_ref[...] = below[:, last:, :]
    above_ref[...] = above[:, :1, :]
    if gather:
        for copy in gathered:
            copy.wait()
        gheld[here] = block_ref[...]
        stacked_ref[...] = gheld[...]


def instance_coupling(psi, table, step, block=None):
    count = lax.axis_size("inst")
    slabs = lax.axis_size("space")
    assert slabs > 2
    gather = block is not None
    inner = 4 if count % 4 == 0 else count
    outer = count // inner
    comps, layers, plane = psi.shape
    edge = jax.ShapeDtypeStruct((comps, 1, plane), psi.dtype)
    extra_out, extra_scratch, operands = (), [], (psi, table)
    if gather:
        extra_out = (jax.ShapeDtypeStruct((slabs, *block.shape), block.dtype),)
        extra_scratch = [
            pltpu.VMEM((slabs, *block.shape), block.dtype),
            pltpu.SemaphoreType.DMA((slabs - 1,)),
            pltpu.SemaphoreType.DMA((slabs - 1,)),
        ]
        operands = (psi, table, block)
    return pl.pallas_call(
        functools.partial(coupling_kernel, count, inner, gather),
        out_shape=(jax.ShapeDtypeStruct(psi.shape, psi.dtype), edge, edge) + extra_out,
        in_specs=[
            pl.BlockSpec(memory_space=pltpu.VMEM),
            pl.BlockSpec(memory_space=pltpu.SMEM),
        ] + [pl.BlockSpec(memory_space=pltpu.VMEM)] * gather,
        out_specs=[pl.BlockSpec(memory_space=pltpu.VMEM)] * (3 + gather),
        scratch_shapes=[
            pltpu.VMEM((inner - 1, *psi.shape), psi.dtype),
            pltpu.VMEM((max(outer - 1, 1), *psi.shape), psi.dtype),
            pltpu.VMEM((max(outer - 1, 1), *psi.shape), psi.dtype),
            pltpu.VMEM(psi.shape, psi.dtype),
            pltpu.VMEM(psi.shape, psi.dtype),
            pltpu.SemaphoreType.DMA((PIECES * (inner - 1),)),
            pltpu.SemaphoreType.DMA((PIECES * (inner - 1),)),
            pltpu.SemaphoreType.DMA((PIECES * max(outer - 1, 1),)),
            pltpu.SemaphoreType.DMA((PIECES * max(outer - 1, 1),)),
            pltpu.SemaphoreType.DMA((2,)),
            pltpu.SemaphoreType.DMA((2,)),
        ] + extra_scratch,
        compiler_params=pltpu.CompilerParams(collective_id=step, has_side_effects=True),
        name=f"instance_coupling_{step}",
    )(*operands)


def gather_kernel(count, block_ref, out_ref, held, send_sem, recv_sem):
    me = lax.axis_index("space")
    peers = [(me + d) % count for d in range(1, count)]
    greet("space", peers)
    copies = []
    for slot, peer in enumerate(peers):
        copy = pltpu.make_async_remote_copy(
            src_ref=block_ref, dst_ref=held.at[me], send_sem=send_sem.at[slot],
            recv_sem=recv_sem.at[slot], device_id={"space": peer},
            device_id_type=pl.DeviceIdType.MESH)
        copy.start()
        copies.append(copy)
    for copy in copies:
        copy.wait()
    held[me] = block_ref[...]
    out_ref[...] = held[...]


def space_gather(block, collective):
    count = lax.axis_size("space")
    return pl.pallas_call(
        functools.partial(gather_kernel, count),
        out_shape=jax.ShapeDtypeStruct((count, *block.shape), block.dtype),
        in_specs=[pl.BlockSpec(memory_space=pltpu.VMEM)],
        out_specs=pl.BlockSpec(memory_space=pltpu.VMEM),
        scratch_shapes=[
            pltpu.VMEM((count, *block.shape), block.dtype),
            pltpu.SemaphoreType.DMA((count - 1,)),
            pltpu.SemaphoreType.DMA((count - 1,)),
        ],
        compiler_params=pltpu.CompilerParams(collective_id=collective, has_side_effects=True),
        name="space_gather",
    )(block)


def route_kernel(count, rows_ref, out_ref, held, send_sem, recv_sem):
    me = lax.axis_index("inst")
    peers = [(me + d) % count for d in range(1, count)]
    greet("inst", peers)
    copies = []
    for slot, peer in enumerate(peers):
        copy = pltpu.make_async_remote_copy(
            src_ref=rows_ref.at[peer], dst_ref=held.at[me], send_sem=send_sem.at[slot],
            recv_sem=recv_sem.at[slot], device_id={"inst": peer},
            device_id_type=pl.DeviceIdType.MESH)
        copy.start()
        copies.append(copy)
    for copy in copies:
        copy.wait()
    held[me] = rows_ref[me]
    out_ref[...] = held[...]


def inst_route(rows, collective):
    count = lax.axis_size("inst")
    return pl.pallas_call(
        functools.partial(route_kernel, count),
        out_shape=jax.ShapeDtypeStruct(rows.shape, rows.dtype),
        in_specs=[pl.BlockSpec(memory_space=pltpu.VMEM)],
        out_specs=pl.BlockSpec(memory_space=pltpu.VMEM),
        scratch_shapes=[
            pltpu.VMEM(rows.shape, rows.dtype),
            pltpu.SemaphoreType.DMA((count - 1,)),
            pltpu.SemaphoreType.DMA((count - 1,)),
        ],
        compiler_params=pltpu.CompilerParams(collective_id=collective, has_side_effects=True),
        name="inst_route",
    )(rows)


def shards(
    psi_start,
    density,
    velocity,
    pressure,
    obs_pos,
    obs_weight,
    obs_harmonic,
    panel_pos,
    panel_normal,
    panel_cell,
    plane_nbr,
):
    inst_count = lax.axis_size("inst")
    inst_id = lax.axis_index("inst")
    space_id = lax.axis_index("space")
    times = jnp.array([2.0 * math.pi * i / inst_count for i in range(inst_count)], jnp.float32)
    local_obs = jnp.concatenate(
        [obs_pos, obs_weight, obs_harmonic[None].astype(jnp.float32)], axis=0
    )
    rows, per = local_obs.shape
    assert rows <= 8 and per <= 128
    packed = jnp.zeros((8, 128), jnp.float32).at[:rows, :per].set(local_obs)
    psi = psi_start[:, 0]
    row_entry = spectral_coeff(
        jnp.arange(inst_count, dtype=jnp.int32).astype(jnp.float32), float(inst_count)
    )
    first = instance_coupling(psi, row_entry, 0, packed)
    stacked = first[3]
    observers = stacked[:, :rows, :per].transpose(1, 0, 2).reshape(rows, -1)
    owned_count = panel_normal.shape[1]
    piece = owned_count // inst_count
    assert piece * inst_count == owned_count and piece % 128 == 0
    mine = lax.dynamic_slice_in_dim(
        panel_pos, space_id * owned_count + inst_id * piece, piece, 1
    )
    normal = lax.dynamic_slice_in_dim(panel_normal, inst_id * piece, piece, 1)
    delta = mine[:, None, :] - observers[:3, :, None]
    dist2 = jnp.sum(delta * delta, axis=0)
    dist = jnp.sqrt(dist2)
    harm = observers[5]
    lag = harm[:, None] * (KWAVE * dist)
    along = jnp.sum(delta * normal[:, None, :], axis=0) * (RADIUS * RADIUS) / (dist2 * dist)
    pairs = jnp.concatenate([along * jnp.cos(lag), along * jnp.sin(lag)], axis=0)
    beat = times[:, None] * harm[None, :]
    cos_beat, sin_beat = jnp.cos(beat), jnp.sin(beat)
    real, imag = observers[3][None, :], observers[4][None, :]
    mixes = jnp.concatenate(
        [real * cos_beat + imag * sin_beat, real * sin_beat - imag * cos_beat], axis=1
    )
    partial = jnp.dot(mixes, pairs, precision=lax.Precision.HIGHEST)
    routed = inst_route(partial.reshape(inst_count, piece // 128, 128), ITERS + 1)
    weight = routed.reshape(owned_count)
    layers = psi_start.shape[2]
    plane = psi_start.shape[3]
    wall = cell_sum(weight, panel_cell, layers, plane)
    dens = density[0]
    vel = velocity[:, 0]
    state = conserved(dens, vel, pressure[0])
    slope = jnp.concatenate(
        [0.5 * jnp.sum(vel * vel, axis=0)[None], -vel, jnp.ones_like(dens)[None]], axis=0
    ) * (GAMMA - 1.0)
    source = slope * wall[None]
    _, pull = jax.vjp(fluxes, state)
    hits = (plane_nbr[:, :, None] == jnp.arange(plane, dtype=jnp.int32)[None, None, :]).astype(
        jnp.float32
    )
    onehot = jnp.stack(
        [hits[0] + hits[1] + hits[2] + hits[3], hits[1] - hits[0], hits[3] - hits[2]]
    ).astype(jnp.bfloat16)
    for step in range(ITERS):
        if step == 0:
            spectral_operator, below, above = first[:3]
        else:
            spectral_operator, below, above = instance_coupling(psi, row_entry, step)
        minus_a = jnp.concatenate([below, psi[:, :-1]], axis=1)
        plus_a = jnp.concatenate([psi[:, 1:], above], axis=1)
        around, across_y, across_z = plane_gather(psi, onehot)
        middle_point = pull((0.5 * (minus_a - plus_a), 0.5 * across_y, 0.5 * across_z))[0]
        spread = 6.0 * psi - (minus_a + plus_a + around)
        psi = psi - TAU * (middle_point + DISSIP * spread + spectral_operator + source)
    return psi[:, None]


def solution(mesh):
    placed = (
        P(None, "inst", "space", None),
        P("inst", "space", None),
        P(None, "inst", "space", None),
        P("inst", "space", None),
        P(None, "space"),
        P(None, "space"),
        P("space"),
        P(),
        P(None, "space"),
        P("space"),
        P(),
    )
    return jax.shard_map(
        shards,
        mesh=mesh,
        in_specs=placed,
        out_specs=P(None, "inst", "space", None),
        check_vma=False,
    )
```

```python
import functools
import math

import jax
import jax.numpy as jnp
from jax import lax
from jax.sharding import PartitionSpec as P
from jax.experimental import pallas as pl
from jax.experimental.pallas import tpu as pltpu

ITERS = 3
PIECES = 4


GAMMA = 1.4
KWAVE = 0.7
RADIUS = 10.0
TAU = 0.05
DISSIP = 0.25
OMEGA = 1.5
VISCO = 0.5


def padded_2(cells, sides, width):
    for axis, dim in sides:
        count = lax.axis_size(axis)
        head = lax.slice_in_dim(cells, 0, width, axis=dim)
        tail = lax.slice_in_dim(cells, cells.shape[dim] - width, cells.shape[dim], axis=dim)
        cells = jnp.concatenate(
            [
                lax.ppermute(tail, axis, [(i, (i + 1) % count) for i in range(count)]),
                cells,
                lax.ppermute(head, axis, [((i + 1) % count, i) for i in range(count)]),
            ],
            axis=dim,
        )
    return cells


def panel_block(observers, panels, time_now):
    delta = panels[:, None, :] - observers[:3, :, None]
    dist2 = jnp.sum(delta * delta, axis=0)
    dist = jnp.sqrt(dist2)
    harm = observers[5][:, None]
    phase = harm * (time_now - KWAVE * dist)
    amp = (
        (observers[3][:, None] * jnp.cos(phase) + observers[4][:, None] * jnp.sin(phase))
        * (RADIUS * RADIUS)
        / (dist2 * dist)
    )
    return jnp.sum(amp[None] * delta, axis=1)


def sensitivity(observers, panels, time_now):
    count = panels.shape[1]
    obs_count = observers.shape[1]
    block = math.gcd(count, max(128, 262144 // obs_count))
    split = panels.reshape(3, count // block, block).transpose(1, 0, 2)
    out = lax.map(lambda piece: panel_block(observers, piece, time_now), split)
    return out.transpose(1, 0, 2).reshape(3, count)


def conserved(density, velocity, pressure):
    moment = density[None] * velocity
    energy = pressure / (GAMMA - 1.0) + 0.5 * density * jnp.sum(velocity * velocity, axis=0)
    return jnp.concatenate([density[None], moment, energy[None]], axis=0)


def fluxes(state):
    dens = state[0]
    moment = state[1:4]
    energy = state[4]
    vel = moment / dens
    press = (GAMMA - 1.0) * (energy - 0.5 * jnp.sum(moment * vel, axis=0))
    result = []
    for axis_d in range(3):
        comps = [moment[axis_d]]
        for axis_e in range(3):
            term = moment[axis_e] * vel[axis_d]
            if axis_e == axis_d:
                term = term + press
            comps.append(term)
        comps.append((energy + press) * vel[axis_d])
        result.append(jnp.stack(comps))
    return tuple(result)


def spectral_coeff(offset, count):
    safe = jnp.where(offset == 0, 1.0, offset)
    angle = math.pi * safe / count
    even_odd_flag = 1.0 - 2.0 * jnp.mod(safe, 2.0)
    other = (
        -(OMEGA / 2.0) * even_odd_flag * jnp.cos(angle) / jnp.sin(angle)
        + VISCO * (OMEGA * OMEGA / 2.0) * even_odd_flag / jnp.sin(angle) ** 2
    )
    return jnp.where(offset == 0, VISCO * OMEGA * OMEGA * (count * count + 2.0) / 12.0, other)


def split_three(values):
    high = lax.reduce_precision(values, exponent_bits=8, mantissa_bits=7)
    rest = values - high
    middle = lax.reduce_precision(rest, exponent_bits=8, mantissa_bits=7)
    low = rest - middle
    return jnp.stack([high, middle, low]).astype(jnp.bfloat16)


def plane_gather(psi, onehot):
    comps, layers, plane = psi.shape
    parts = split_three(psi.reshape(comps * layers, plane))
    picked = jnp.einsum("pra,kba->kprb", parts, onehot,
                        preferred_element_type=jnp.float32)
    picked = (picked[:, 0] + picked[:, 1]) + picked[:, 2]
    return picked.reshape(onehot.shape[0], comps, layers, plane)


def cell_sum(weight, cell, layers, plane):
    by_layer = (cell // plane)[None, :] == jnp.arange(layers, dtype=jnp.int32)[:, None]
    spread = jnp.where(by_layer, weight[None, :], 0.0)
    picks = ((cell % plane)[:, None] == jnp.arange(plane, dtype=jnp.int32)[None, :]).astype(
        jnp.bfloat16
    )
    parts = split_three(spread)
    summed = jnp.einsum("plq,qb->plb", parts, picks, preferred_element_type=jnp.float32)
    return (summed[0] + summed[1]) + summed[2]


def greet(axis, peers):
    greet_all([{axis: peer} for peer in peers])


def greet_all(devices):
    barrier = pltpu.get_barrier_semaphore()
    for device in devices:
        pl.semaphore_signal(barrier, inc=1, device_id=device,
                            device_id_type=pl.DeviceIdType.MESH)
    pl.semaphore_wait(barrier, len(devices))


def coupling_kernel(count, inner, gather, psi_ref, table_ref, *refs):
    if gather:
        (block_ref, out_ref, below_ref, above_ref, stacked_ref, held, outbox, inbox, below, above,
         ring_send, ring_recv, cross_send, cross_recv, edge_send, edge_recv, gheld, gsend,
         grecv) = refs
    else:
        (out_ref, below_ref, above_ref, held, outbox, inbox, below, above, ring_send, ring_recv,
         cross_send, cross_recv, edge_send, edge_recv) = refs
    outer = count // inner
    me = lax.axis_index("inst")
    me_hi, me_lo = me // inner, me % inner
    ring = [me_hi * inner + (me_lo + d) % inner for d in range(1, inner)]
    ring_from = [me_hi * inner + (me_lo - d) % inner for d in range(1, inner)]
    partners = [((me_hi + h) % outer) * inner + me_lo for h in range(1, outer)]
    slabs = lax.axis_size("space")
    here = lax.axis_index("space")
    up, down = (here + 1) % slabs, (here + slabs - 1) % slabs
    if gather:
        everyone = [(me + d) % count for d in range(1, count)]
        greet_all([{"inst": p} for p in everyone] + [{"space": up}, {"space": down}])
        gathered = []
        for slot, peer in enumerate(everyone):
            copy = pltpu.make_async_remote_copy(
                src_ref=block_ref.at[peer], dst_ref=gheld.at[me], send_sem=gsend.at[slot],
                recv_sem=grecv.at[slot], device_id={"inst": peer},
                device_id_type=pl.DeviceIdType.MESH)
            copy.start()
            gathered.append(copy)
    else:
        greet_all([{"inst": p} for p in ring + partners] + [{"space": up}, {"space": down}])
    last = psi_ref.shape[1] - 1
    edges = []
    for slot, (peer, layer, land) in enumerate(((up, last, below), (down, 0, above))):
        copy = pltpu.make_async_remote_copy(
            src_ref=psi_ref.at[:, pl.ds(layer, 1), :], dst_ref=land.at[:, pl.ds(layer, 1), :],
            send_sem=edge_send.at[slot], recv_sem=edge_recv.at[slot],
            device_id={"space": peer}, device_id_type=pl.DeviceIdType.MESH)
        copy.start()
        edges.append(copy)

    def coef(row, col):
        return table_ref[(row - col) % count]

    halves = PIECES
    width = psi_ref.shape[2] // halves
    spans = [pl.ds(h * width, width) for h in range(halves)]
    copies = []
    for h, cols in enumerate(spans):
        row = []
        for slot, peer in enumerate(ring):
            at = h * len(ring) + slot
            copy = pltpu.make_async_remote_copy(
                src_ref=psi_ref.at[:, :, cols], dst_ref=held.at[slot, :, :, cols],
                send_sem=ring_send.at[at], recv_sem=ring_recv.at[at],
                device_id={"inst": peer}, device_id_type=pl.DeviceIdType.MESH)
            copy.start()
            row.append(copy)
        copies.append(row)
    cross = []
    for h, cols in enumerate(spans):
        for copy in copies[h]:
            copy.wait()
        for slot, partner in enumerate(partners):
            at = h * len(partners) + slot
            part = coef(partner, me) * psi_ref[:, :, cols]
            for d, source in enumerate(ring_from):
                part = part + coef(partner, source) * held[d, :, :, cols]
            outbox[slot, :, :, cols] = part
            copy = pltpu.make_async_remote_copy(
                src_ref=outbox.at[slot, :, :, cols], dst_ref=inbox.at[slot, :, :, cols],
                send_sem=cross_send.at[at], recv_sem=cross_recv.at[at],
                device_id={"inst": partner}, device_id_type=pl.DeviceIdType.MESH)
            copy.start()
            cross.append((h, slot, copy))
    for h, cols in enumerate(spans):
        total = coef(me, me) * psi_ref[:, :, cols]
        for d, source in enumerate(ring_from):
            total = total + coef(me, source) * held[d, :, :, cols]
        out_ref[:, :, cols] = total
    for h, slot, copy in cross:
        copy.wait()
        out_ref[:, :, spans[h]] = out_ref[:, :, spans[h]] + inbox[slot, :, :, spans[h]]
    for copy in edges:
        copy.wait()
    below_ref[...] = below[:, last:, :]
    above_ref[...] = above[:, :1, :]
    if gather:
        for copy in gathered:
            copy.wait()
        gheld[me] = block_ref[me]
        stacked_ref[...] = gheld[...]


def instance_coupling(psi, table, step, block=None):
    count = lax.axis_size("inst")
    slabs = lax.axis_size("space")
    assert slabs > 2
    gather = block is not None
    inner = 4 if count % 4 == 0 else count
    outer = count // inner
    comps, layers, plane = psi.shape
    edge = jax.ShapeDtypeStruct((comps, 1, plane), psi.dtype)
    extra_out, extra_scratch, operands = (), [], (psi, table)
    if gather:
        extra_out = (jax.ShapeDtypeStruct(block.shape, block.dtype),)
        extra_scratch = [
            pltpu.VMEM(block.shape, block.dtype),
            pltpu.SemaphoreType.DMA((count - 1,)),
            pltpu.SemaphoreType.DMA((count - 1,)),
        ]
        operands = (psi, table, block)
    return pl.pallas_call(
        functools.partial(coupling_kernel, count, inner, gather),
        out_shape=(jax.ShapeDtypeStruct(psi.shape, psi.dtype), edge, edge) + extra_out,
        in_specs=[
            pl.BlockSpec(memory_space=pltpu.VMEM),
            pl.BlockSpec(memory_space=pltpu.SMEM),
        ] + [pl.BlockSpec(memory_space=pltpu.VMEM)] * gather,
        out_specs=[pl.BlockSpec(memory_space=pltpu.VMEM)] * (3 + gather),
        scratch_shapes=[
            pltpu.VMEM((inner - 1, *psi.shape), psi.dtype),
            pltpu.VMEM((max(outer - 1, 1), *psi.shape), psi.dtype),
            pltpu.VMEM((max(outer - 1, 1), *psi.shape), psi.dtype),
            pltpu.VMEM(psi.shape, psi.dtype),
            pltpu.VMEM(psi.shape, psi.dtype),
            pltpu.SemaphoreType.DMA((PIECES * (inner - 1),)),
            pltpu.SemaphoreType.DMA((PIECES * (inner - 1),)),
            pltpu.SemaphoreType.DMA((PIECES * max(outer - 1, 1),)),
            pltpu.SemaphoreType.DMA((PIECES * max(outer - 1, 1),)),
            pltpu.SemaphoreType.DMA((2,)),
            pltpu.SemaphoreType.DMA((2,)),
        ] + extra_scratch,
        compiler_params=pltpu.CompilerParams(collective_id=step, has_side_effects=True),
        name=f"instance_coupling_{step}",
    )(*operands)


def gather_kernel(count, block_ref, out_ref, held, send_sem, recv_sem):
    me = lax.axis_index("space")
    peers = [(me + d) % count for d in range(1, count)]
    greet("space", peers)
    copies = []
    for slot, peer in enumerate(peers):
        copy = pltpu.make_async_remote_copy(
            src_ref=block_ref, dst_ref=held.at[me], send_sem=send_sem.at[slot],
            recv_sem=recv_sem.at[slot], device_id={"space": peer},
            device_id_type=pl.DeviceIdType.MESH)
        copy.start()
        copies.append(copy)
    for copy in copies:
        copy.wait()
    held[me] = block_ref[...]
    out_ref[...] = held[...]


def space_gather(block, collective):
    count = lax.axis_size("space")
    return pl.pallas_call(
        functools.partial(gather_kernel, count),
        out_shape=jax.ShapeDtypeStruct((count, *block.shape), block.dtype),
        in_specs=[pl.BlockSpec(memory_space=pltpu.VMEM)],
        out_specs=pl.BlockSpec(memory_space=pltpu.VMEM),
        scratch_shapes=[
            pltpu.VMEM((count, *block.shape), block.dtype),
            pltpu.SemaphoreType.DMA((count - 1,)),
            pltpu.SemaphoreType.DMA((count - 1,)),
        ],
        compiler_params=pltpu.CompilerParams(collective_id=collective, has_side_effects=True),
        name="space_gather",
    )(block)


def route_kernel(count, rows_ref, out_ref, held, send_sem, recv_sem):
    me = lax.axis_index("inst")
    peers = [(me + d) % count for d in range(1, count)]
    greet("inst", peers)
    copies = []
    for slot, peer in enumerate(peers):
        copy = pltpu.make_async_remote_copy(
            src_ref=rows_ref.at[peer], dst_ref=held.at[me], send_sem=send_sem.at[slot],
            recv_sem=recv_sem.at[slot], device_id={"inst": peer},
            device_id_type=pl.DeviceIdType.MESH)
        copy.start()
        copies.append(copy)
    for copy in copies:
        copy.wait()
    held[me] = rows_ref[me]
    out_ref[...] = held[...]


def inst_route(rows, collective):
    count = lax.axis_size("inst")
    return pl.pallas_call(
        functools.partial(route_kernel, count),
        out_shape=jax.ShapeDtypeStruct(rows.shape, rows.dtype),
        in_specs=[pl.BlockSpec(memory_space=pltpu.VMEM)],
        out_specs=pl.BlockSpec(memory_space=pltpu.VMEM),
        scratch_shapes=[
            pltpu.VMEM(rows.shape, rows.dtype),
            pltpu.SemaphoreType.DMA((count - 1,)),
            pltpu.SemaphoreType.DMA((count - 1,)),
        ],
        compiler_params=pltpu.CompilerParams(collective_id=collective, has_side_effects=True),
        name="inst_route",
    )(rows)


def shards(
    psi_start,
    density,
    velocity,
    pressure,
    obs_pos,
    obs_weight,
    obs_harmonic,
    panel_pos,
    panel_normal,
    panel_cell,
    plane_nbr,
):
    inst_count = lax.axis_size("inst")
    inst_id = lax.axis_index("inst")
    space_id = lax.axis_index("space")
    times = jnp.array([2.0 * math.pi * i / inst_count for i in range(inst_count)], jnp.float32)
    local_obs = jnp.concatenate(
        [obs_pos, obs_weight, obs_harmonic[None].astype(jnp.float32)], axis=0
    )
    rows, per = local_obs.shape
    assert rows <= 8 and per <= 128
    packed = jnp.zeros((8, 128), jnp.float32).at[:rows, :per].set(local_obs)
    psi = psi_start[:, 0]
    row_entry = spectral_coeff(
        jnp.arange(inst_count, dtype=jnp.int32).astype(jnp.float32), float(inst_count)
    )
    stacked = space_gather(packed, ITERS)
    observers = stacked[:, :rows, :per].transpose(1, 0, 2).reshape(rows, -1)
    owned_count = panel_normal.shape[1]
    piece = owned_count // inst_count
    assert piece * inst_count == owned_count and piece % 128 == 0
    mine = lax.dynamic_slice_in_dim(
        panel_pos, space_id * owned_count + inst_id * piece, piece, 1
    )
    normal = lax.dynamic_slice_in_dim(panel_normal, inst_id * piece, piece, 1)
    delta = mine[:, None, :] - observers[:3, :, None]
    dist2 = jnp.sum(delta * delta, axis=0)
    dist = jnp.sqrt(dist2)
    harm = observers[5]
    lag = harm[:, None] * (KWAVE * dist)
    along = jnp.sum(delta * normal[:, None, :], axis=0) * (RADIUS * RADIUS) / (dist2 * dist)
    pairs = jnp.concatenate([along * jnp.cos(lag), along * jnp.sin(lag)], axis=0)
    beat = times[:, None] * harm[None, :]
    cos_beat, sin_beat = jnp.cos(beat), jnp.sin(beat)
    real, imag = observers[3][None, :], observers[4][None, :]
    mixes = jnp.concatenate(
        [real * cos_beat + imag * sin_beat, real * sin_beat - imag * cos_beat], axis=1
    )
    partial = jnp.dot(mixes, pairs, precision=lax.Precision.HIGHEST)
    first = instance_coupling(psi, row_entry, 0, partial.reshape(inst_count, piece // 128, 128))
    routed = first[3]
    weight = routed.reshape(owned_count)
    layers = psi_start.shape[2]
    plane = psi_start.shape[3]
    wall = cell_sum(weight, panel_cell, layers, plane)
    dens = density[0]
    vel = velocity[:, 0]
    state = conserved(dens, vel, pressure[0])
    slope = jnp.concatenate(
        [0.5 * jnp.sum(vel * vel, axis=0)[None], -vel, jnp.ones_like(dens)[None]], axis=0
    ) * (GAMMA - 1.0)
    source = slope * wall[None]
    _, pull = jax.vjp(fluxes, state)
    onehot = (plane_nbr[:, :, None] == jnp.arange(plane, dtype=jnp.int32)[None, None, :]).astype(
        jnp.bfloat16
    )
    for step in range(ITERS):
        if step == 0:
            spectral_operator, below, above = first[:3]
        else:
            spectral_operator, below, above = instance_coupling(psi, row_entry, step)
        minus_a = jnp.concatenate([below, psi[:, :-1]], axis=1)
        plus_a = jnp.concatenate([psi[:, 1:], above], axis=1)
        plus_y, minus_y, plus_z, minus_z = plane_gather(psi, onehot)
        middle_point = pull(
            (0.5 * (minus_a - plus_a), 0.5 * (minus_y - plus_y), 0.5 * (minus_z - plus_z))
        )[0]
        spread = 6.0 * psi - (minus_a + plus_a + plus_y + minus_y + plus_z + minus_z)
        psi = psi - TAU * (middle_point + DISSIP * spread + spectral_operator + source)
    return psi[:, None]


def solution(mesh):
    placed = (
        P(None, "inst", "space", None),
        P("inst", "space", None),
        P(None, "inst", "space", None),
        P("inst", "space", None),
        P(None, "space"),
        P(None, "space"),
        P("space"),
        P(),
        P(None, "space"),
        P("space"),
        P(),
    )
    return jax.shard_map(
        shards,
        mesh=mesh,
        in_specs=placed,
        out_specs=P(None, "inst", "space", None),
        check_vma=False,
    )
```

```python
import functools
import math

import jax
import jax.numpy as jnp
from jax import lax
from jax.sharding import PartitionSpec as P
from jax.experimental import pallas as pl
from jax.experimental.pallas import tpu as pltpu

ITERS = 3
PIECES = 4


GAMMA = 1.4
KWAVE = 0.7
RADIUS = 10.0
TAU = 0.05
DISSIP = 0.25
OMEGA = 1.5
VISCO = 0.5


def padded_2(cells, sides, width):
    for axis, dim in sides:
        count = lax.axis_size(axis)
        head = lax.slice_in_dim(cells, 0, width, axis=dim)
        tail = lax.slice_in_dim(cells, cells.shape[dim] - width, cells.shape[dim], axis=dim)
        cells = jnp.concatenate(
            [
                lax.ppermute(tail, axis, [(i, (i + 1) % count) for i in range(count)]),
                cells,
                lax.ppermute(head, axis, [((i + 1) % count, i) for i in range(count)]),
            ],
            axis=dim,
        )
    return cells


def panel_block(observers, panels, time_now):
    delta = panels[:, None, :] - observers[:3, :, None]
    dist2 = jnp.sum(delta * delta, axis=0)
    dist = jnp.sqrt(dist2)
    harm = observers[5][:, None]
    phase = harm * (time_now - KWAVE * dist)
    amp = (
        (observers[3][:, None] * jnp.cos(phase) + observers[4][:, None] * jnp.sin(phase))
        * (RADIUS * RADIUS)
        / (dist2 * dist)
    )
    return jnp.sum(amp[None] * delta, axis=1)


def sensitivity(observers, panels, time_now):
    count = panels.shape[1]
    obs_count = observers.shape[1]
    block = math.gcd(count, max(128, 262144 // obs_count))
    split = panels.reshape(3, count // block, block).transpose(1, 0, 2)
    out = lax.map(lambda piece: panel_block(observers, piece, time_now), split)
    return out.transpose(1, 0, 2).reshape(3, count)


def conserved(density, velocity, pressure):
    moment = density[None] * velocity
    energy = pressure / (GAMMA - 1.0) + 0.5 * density * jnp.sum(velocity * velocity, axis=0)
    return jnp.concatenate([density[None], moment, energy[None]], axis=0)


def fluxes(state):
    dens = state[0]
    moment = state[1:4]
    energy = state[4]
    vel = moment / dens
    press = (GAMMA - 1.0) * (energy - 0.5 * jnp.sum(moment * vel, axis=0))
    result = []
    for axis_d in range(3):
        comps = [moment[axis_d]]
        for axis_e in range(3):
            term = moment[axis_e] * vel[axis_d]
            if axis_e == axis_d:
                term = term + press
            comps.append(term)
        comps.append((energy + press) * vel[axis_d])
        result.append(jnp.stack(comps))
    return tuple(result)


def spectral_coeff(offset, count):
    safe = jnp.where(offset == 0, 1.0, offset)
    angle = math.pi * safe / count
    even_odd_flag = 1.0 - 2.0 * jnp.mod(safe, 2.0)
    other = (
        -(OMEGA / 2.0) * even_odd_flag * jnp.cos(angle) / jnp.sin(angle)
        + VISCO * (OMEGA * OMEGA / 2.0) * even_odd_flag / jnp.sin(angle) ** 2
    )
    return jnp.where(offset == 0, VISCO * OMEGA * OMEGA * (count * count + 2.0) / 12.0, other)


def split_three(values):
    high = lax.reduce_precision(values, exponent_bits=8, mantissa_bits=7)
    rest = values - high
    middle = lax.reduce_precision(rest, exponent_bits=8, mantissa_bits=7)
    low = rest - middle
    return jnp.stack([high, middle, low]).astype(jnp.bfloat16)


def plane_gather(psi, onehot):
    comps, layers, plane = psi.shape
    parts = split_three(psi.reshape(comps * layers, plane))
    picked = jnp.einsum("pra,kba->kprb", parts, onehot,
                        preferred_element_type=jnp.float32)
    picked = (picked[:, 0] + picked[:, 1]) + picked[:, 2]
    return picked.reshape(onehot.shape[0], comps, layers, plane)


def cell_sum(weight, cell, layers, plane):
    by_layer = (cell // plane)[None, :] == jnp.arange(layers, dtype=jnp.int32)[:, None]
    spread = jnp.where(by_layer, weight[None, :], 0.0)
    picks = ((cell % plane)[:, None] == jnp.arange(plane, dtype=jnp.int32)[None, :]).astype(
        jnp.bfloat16
    )
    parts = split_three(spread)
    summed = jnp.einsum("plq,qb->plb", parts, picks, preferred_element_type=jnp.float32)
    return (summed[0] + summed[1]) + summed[2]


def greet(axis, peers):
    greet_all([{axis: peer} for peer in peers])


def greet_all(devices):
    barrier = pltpu.get_barrier_semaphore()
    for device in devices:
        pl.semaphore_signal(barrier, inc=1, device_id=device,
                            device_id_type=pl.DeviceIdType.MESH)
    pl.semaphore_wait(barrier, len(devices))


def coupling_kernel(count, inner, gather, psi_ref, table_ref, *refs):
    if gather:
        (block_ref, out_ref, below_ref, above_ref, stacked_ref, held, outbox, inbox, below, above,
         ring_send, ring_recv, cross_send, cross_recv, edge_send, edge_recv, gheld, gsend,
         grecv) = refs
    else:
        (out_ref, below_ref, above_ref, held, outbox, inbox, below, above, ring_send, ring_recv,
         cross_send, cross_recv, edge_send, edge_recv) = refs
    outer = count // inner
    me = lax.axis_index("inst")
    me_hi, me_lo = me // inner, me % inner
    steps = sorted(range(1, inner), key=lambda d: -min(d, inner - d))
    ring = [me_hi * inner + (me_lo + d) % inner for d in steps]
    ring_from = [me_hi * inner + (me_lo - d) % inner for d in steps]
    partners = [((me_hi + h) % outer) * inner + me_lo for h in range(1, outer)]
    slabs = lax.axis_size("space")
    here = lax.axis_index("space")
    up, down = (here + 1) % slabs, (here + slabs - 1) % slabs
    if gather:
        everyone = [(me + d) % count for d in range(1, count)]
        greet_all([{"inst": p} for p in everyone] + [{"space": up}, {"space": down}])
        gathered = []
        for slot, peer in enumerate(everyone):
            copy = pltpu.make_async_remote_copy(
                src_ref=block_ref.at[peer], dst_ref=gheld.at[me], send_sem=gsend.at[slot],
                recv_sem=grecv.at[slot], device_id={"inst": peer},
                device_id_type=pl.DeviceIdType.MESH)
            copy.start()
            gathered.append(copy)
    else:
        greet_all([{"inst": p} for p in ring + partners] + [{"space": up}, {"space": down}])
    last = psi_ref.shape[1] - 1
    edges = []
    for slot, (peer, layer, land) in enumerate(((up, last, below), (down, 0, above))):
        copy = pltpu.make_async_remote_copy(
            src_ref=psi_ref.at[:, pl.ds(layer, 1), :], dst_ref=land.at[:, pl.ds(layer, 1), :],
            send_sem=edge_send.at[slot], recv_sem=edge_recv.at[slot],
            device_id={"space": peer}, device_id_type=pl.DeviceIdType.MESH)
        copy.start()
        edges.append(copy)

    def coef(row, col):
        return table_ref[(row - col) % count]

    halves = PIECES
    width = psi_ref.shape[2] // halves
    spans = [pl.ds(h * width, width) for h in range(halves)]
    copies = []
    for h, cols in enumerate(spans):
        row = []
        for slot, peer in enumerate(ring):
            at = h * len(ring) + slot
            copy = pltpu.make_async_remote_copy(
                src_ref=psi_ref.at[:, :, cols], dst_ref=held.at[slot, :, :, cols],
                send_sem=ring_send.at[at], recv_sem=ring_recv.at[at],
                device_id={"inst": peer}, device_id_type=pl.DeviceIdType.MESH)
            copy.start()
            row.append(copy)
        copies.append(row)
    cross = []
    for h, cols in enumerate(spans):
        for copy in copies[h]:
            copy.wait()
        for slot, partner in enumerate(partners):
            at = h * len(partners) + slot
            part = coef(partner, me) * psi_ref[:, :, cols]
            for d, source in enumerate(ring_from):
                part = part + coef(partner, source) * held[d, :, :, cols]
            outbox[slot, :, :, cols] = part
            copy = pltpu.make_async_remote_copy(
                src_ref=outbox.at[slot, :, :, cols], dst_ref=inbox.at[slot, :, :, cols],
                send_sem=cross_send.at[at], recv_sem=cross_recv.at[at],
                device_id={"inst": partner}, device_id_type=pl.DeviceIdType.MESH)
            copy.start()
            cross.append((h, slot, copy))
    for h, cols in enumerate(spans):
        total = coef(me, me) * psi_ref[:, :, cols]
        for d, source in enumerate(ring_from):
            total = total + coef(me, source) * held[d, :, :, cols]
        out_ref[:, :, cols] = total
    for h, slot, copy in cross:
        copy.wait()
        out_ref[:, :, spans[h]] = out_ref[:, :, spans[h]] + inbox[slot, :, :, spans[h]]
    for copy in edges:
        copy.wait()
    below_ref[...] = below[:, last:, :]
    above_ref[...] = above[:, :1, :]
    if gather:
        for copy in gathered:
            copy.wait()
        gheld[me] = block_ref[me]
        stacked_ref[...] = gheld[...]


def instance_coupling(psi, table, step, block=None):
    count = lax.axis_size("inst")
    slabs = lax.axis_size("space")
    assert slabs > 2
    gather = block is not None
    inner = 4 if count % 4 == 0 else count
    outer = count // inner
    comps, layers, plane = psi.shape
    edge = jax.ShapeDtypeStruct((comps, 1, plane), psi.dtype)
    extra_out, extra_scratch, operands = (), [], (psi, table)
    if gather:
        extra_out = (jax.ShapeDtypeStruct(block.shape, block.dtype),)
        extra_scratch = [
            pltpu.VMEM(block.shape, block.dtype),
            pltpu.SemaphoreType.DMA((count - 1,)),
            pltpu.SemaphoreType.DMA((count - 1,)),
        ]
        operands = (psi, table, block)
    return pl.pallas_call(
        functools.partial(coupling_kernel, count, inner, gather),
        out_shape=(jax.ShapeDtypeStruct(psi.shape, psi.dtype), edge, edge) + extra_out,
        in_specs=[
            pl.BlockSpec(memory_space=pltpu.VMEM),
            pl.BlockSpec(memory_space=pltpu.SMEM),
        ] + [pl.BlockSpec(memory_space=pltpu.VMEM)] * gather,
        out_specs=[pl.BlockSpec(memory_space=pltpu.VMEM)] * (3 + gather),
        scratch_shapes=[
            pltpu.VMEM((inner - 1, *psi.shape), psi.dtype),
            pltpu.VMEM((max(outer - 1, 1), *psi.shape), psi.dtype),
            pltpu.VMEM((max(outer - 1, 1), *psi.shape), psi.dtype),
            pltpu.VMEM(psi.shape, psi.dtype),
            pltpu.VMEM(psi.shape, psi.dtype),
            pltpu.SemaphoreType.DMA((PIECES * (inner - 1),)),
            pltpu.SemaphoreType.DMA((PIECES * (inner - 1),)),
            pltpu.SemaphoreType.DMA((PIECES * max(outer - 1, 1),)),
            pltpu.SemaphoreType.DMA((PIECES * max(outer - 1, 1),)),
            pltpu.SemaphoreType.DMA((2,)),
            pltpu.SemaphoreType.DMA((2,)),
        ] + extra_scratch,
        compiler_params=pltpu.CompilerParams(collective_id=step, has_side_effects=True),
        name=f"instance_coupling_{step}",
    )(*operands)


def gather_kernel(count, block_ref, out_ref, held, send_sem, recv_sem):
    me = lax.axis_index("space")
    peers = [(me + d) % count for d in range(1, count)]
    greet("space", peers)
    copies = []
    for slot, peer in enumerate(peers):
        copy = pltpu.make_async_remote_copy(
            src_ref=block_ref, dst_ref=held.at[me], send_sem=send_sem.at[slot],
            recv_sem=recv_sem.at[slot], device_id={"space": peer},
            device_id_type=pl.DeviceIdType.MESH)
        copy.start()
        copies.append(copy)
    for copy in copies:
        copy.wait()
    held[me] = block_ref[...]
    out_ref[...] = held[...]


def space_gather(block, collective):
    count = lax.axis_size("space")
    return pl.pallas_call(
        functools.partial(gather_kernel, count),
        out_shape=jax.ShapeDtypeStruct((count, *block.shape), block.dtype),
        in_specs=[pl.BlockSpec(memory_space=pltpu.VMEM)],
        out_specs=pl.BlockSpec(memory_space=pltpu.VMEM),
        scratch_shapes=[
            pltpu.VMEM((count, *block.shape), block.dtype),
            pltpu.SemaphoreType.DMA((count - 1,)),
            pltpu.SemaphoreType.DMA((count - 1,)),
        ],
        compiler_params=pltpu.CompilerParams(collective_id=collective, has_side_effects=True),
        name="space_gather",
    )(block)


def route_kernel(count, rows_ref, out_ref, held, send_sem, recv_sem):
    me = lax.axis_index("inst")
    peers = [(me + d) % count for d in range(1, count)]
    greet("inst", peers)
    copies = []
    for slot, peer in enumerate(peers):
        copy = pltpu.make_async_remote_copy(
            src_ref=rows_ref.at[peer], dst_ref=held.at[me], send_sem=send_sem.at[slot],
            recv_sem=recv_sem.at[slot], device_id={"inst": peer},
            device_id_type=pl.DeviceIdType.MESH)
        copy.start()
        copies.append(copy)
    for copy in copies:
        copy.wait()
    held[me] = rows_ref[me]
    out_ref[...] = held[...]


def inst_route(rows, collective):
    count = lax.axis_size("inst")
    return pl.pallas_call(
        functools.partial(route_kernel, count),
        out_shape=jax.ShapeDtypeStruct(rows.shape, rows.dtype),
        in_specs=[pl.BlockSpec(memory_space=pltpu.VMEM)],
        out_specs=pl.BlockSpec(memory_space=pltpu.VMEM),
        scratch_shapes=[
            pltpu.VMEM(rows.shape, rows.dtype),
            pltpu.SemaphoreType.DMA((count - 1,)),
            pltpu.SemaphoreType.DMA((count - 1,)),
        ],
        compiler_params=pltpu.CompilerParams(collective_id=collective, has_side_effects=True),
        name="inst_route",
    )(rows)


def shards(
    psi_start,
    density,
    velocity,
    pressure,
    obs_pos,
    obs_weight,
    obs_harmonic,
    panel_pos,
    panel_normal,
    panel_cell,
    plane_nbr,
):
    inst_count = lax.axis_size("inst")
    inst_id = lax.axis_index("inst")
    space_id = lax.axis_index("space")
    times = jnp.array([2.0 * math.pi * i / inst_count for i in range(inst_count)], jnp.float32)
    local_obs = jnp.concatenate(
        [obs_pos, obs_weight, obs_harmonic[None].astype(jnp.float32)], axis=0
    )
    rows, per = local_obs.shape
    assert rows <= 8 and per <= 128
    packed = jnp.zeros((8, 128), jnp.float32).at[:rows, :per].set(local_obs)
    psi = psi_start[:, 0]
    row_entry = spectral_coeff(
        jnp.arange(inst_count, dtype=jnp.int32).astype(jnp.float32), float(inst_count)
    )
    stacked = space_gather(packed, ITERS)
    observers = stacked[:, :rows, :per].transpose(1, 0, 2).reshape(rows, -1)
    owned_count = panel_normal.shape[1]
    piece = owned_count // inst_count
    assert piece * inst_count == owned_count and piece % 128 == 0
    mine = lax.dynamic_slice_in_dim(
        panel_pos, space_id * owned_count + inst_id * piece, piece, 1
    )
    normal = lax.dynamic_slice_in_dim(panel_normal, inst_id * piece, piece, 1)
    delta = mine[:, None, :] - observers[:3, :, None]
    dist2 = jnp.sum(delta * delta, axis=0)
    dist = jnp.sqrt(dist2)
    harm = observers[5]
    lag = harm[:, None] * (KWAVE * dist)
    along = jnp.sum(delta * normal[:, None, :], axis=0) * (RADIUS * RADIUS) / (dist2 * dist)
    pairs = jnp.concatenate([along * jnp.cos(lag), along * jnp.sin(lag)], axis=0)
    beat = times[:, None] * harm[None, :]
    cos_beat, sin_beat = jnp.cos(beat), jnp.sin(beat)
    real, imag = observers[3][None, :], observers[4][None, :]
    mixes = jnp.concatenate(
        [real * cos_beat + imag * sin_beat, real * sin_beat - imag * cos_beat], axis=1
    )
    partial = jnp.dot(mixes, pairs, precision=lax.Precision.HIGHEST)
    first = instance_coupling(psi, row_entry, 0, partial.reshape(inst_count, piece // 128, 128))
    routed = first[3]
    weight = routed.reshape(owned_count)
    layers = psi_start.shape[2]
    plane = psi_start.shape[3]
    wall = cell_sum(weight, panel_cell, layers, plane)
    dens = density[0]
    vel = velocity[:, 0]
    state = conserved(dens, vel, pressure[0])
    slope = jnp.concatenate(
        [0.5 * jnp.sum(vel * vel, axis=0)[None], -vel, jnp.ones_like(dens)[None]], axis=0
    ) * (GAMMA - 1.0)
    source = slope * wall[None]
    _, pull = jax.vjp(fluxes, state)
    onehot = (plane_nbr[:, :, None] == jnp.arange(plane, dtype=jnp.int32)[None, None, :]).astype(
        jnp.bfloat16
    )
    for step in range(ITERS):
        if step == 0:
            spectral_operator, below, above = first[:3]
        else:
            spectral_operator, below, above = instance_coupling(psi, row_entry, step)
        minus_a = jnp.concatenate([below, psi[:, :-1]], axis=1)
        plus_a = jnp.concatenate([psi[:, 1:], above], axis=1)
        plus_y, minus_y, plus_z, minus_z = plane_gather(psi, onehot)
        middle_point = pull(
            (0.5 * (minus_a - plus_a), 0.5 * (minus_y - plus_y), 0.5 * (minus_z - plus_z))
        )[0]
        spread = 6.0 * psi - (minus_a + plus_a + plus_y + minus_y + plus_z + minus_z)
        psi = psi - TAU * (middle_point + DISSIP * spread + spectral_operator + source)
    return psi[:, None]


def solution(mesh):
    placed = (
        P(None, "inst", "space", None),
        P("inst", "space", None),
        P(None, "inst", "space", None),
        P("inst", "space", None),
        P(None, "space"),
        P(None, "space"),
        P("space"),
        P(),
        P(None, "space"),
        P("space"),
        P(),
    )
    return jax.shard_map(
        shards,
        mesh=mesh,
        in_specs=placed,
        out_specs=P(None, "inst", "space", None),
        check_vma=False,
    )
```

```python
import functools
import math

import jax
import jax.numpy as jnp
from jax import lax
from jax.sharding import PartitionSpec as P
from jax.experimental import pallas as pl
from jax.experimental.pallas import tpu as pltpu

ITERS = 3
PIECES = 4


GAMMA = 1.4
KWAVE = 0.7
RADIUS = 10.0
TAU = 0.05
DISSIP = 0.25
OMEGA = 1.5
VISCO = 0.5


def padded_2(cells, sides, width):
    for axis, dim in sides:
        count = lax.axis_size(axis)
        head = lax.slice_in_dim(cells, 0, width, axis=dim)
        tail = lax.slice_in_dim(cells, cells.shape[dim] - width, cells.shape[dim], axis=dim)
        cells = jnp.concatenate(
            [
                lax.ppermute(tail, axis, [(i, (i + 1) % count) for i in range(count)]),
                cells,
                lax.ppermute(head, axis, [((i + 1) % count, i) for i in range(count)]),
            ],
            axis=dim,
        )
    return cells


def panel_block(observers, panels, time_now):
    delta = panels[:, None, :] - observers[:3, :, None]
    dist2 = jnp.sum(delta * delta, axis=0)
    dist = jnp.sqrt(dist2)
    harm = observers[5][:, None]
    phase = harm * (time_now - KWAVE * dist)
    amp = (
        (observers[3][:, None] * jnp.cos(phase) + observers[4][:, None] * jnp.sin(phase))
        * (RADIUS * RADIUS)
        / (dist2 * dist)
    )
    return jnp.sum(amp[None] * delta, axis=1)


def sensitivity(observers, panels, time_now):
    count = panels.shape[1]
    obs_count = observers.shape[1]
    block = math.gcd(count, max(128, 262144 // obs_count))
    split = panels.reshape(3, count // block, block).transpose(1, 0, 2)
    out = lax.map(lambda piece: panel_block(observers, piece, time_now), split)
    return out.transpose(1, 0, 2).reshape(3, count)


def conserved(density, velocity, pressure):
    moment = density[None] * velocity
    energy = pressure / (GAMMA - 1.0) + 0.5 * density * jnp.sum(velocity * velocity, axis=0)
    return jnp.concatenate([density[None], moment, energy[None]], axis=0)


def fluxes(state):
    dens = state[0]
    moment = state[1:4]
    energy = state[4]
    vel = moment / dens
    press = (GAMMA - 1.0) * (energy - 0.5 * jnp.sum(moment * vel, axis=0))
    result = []
    for axis_d in range(3):
        comps = [moment[axis_d]]
        for axis_e in range(3):
            term = moment[axis_e] * vel[axis_d]
            if axis_e == axis_d:
                term = term + press
            comps.append(term)
        comps.append((energy + press) * vel[axis_d])
        result.append(jnp.stack(comps))
    return tuple(result)


def spectral_coeff(offset, count):
    safe = jnp.where(offset == 0, 1.0, offset)
    angle = math.pi * safe / count
    even_odd_flag = 1.0 - 2.0 * jnp.mod(safe, 2.0)
    other = (
        -(OMEGA / 2.0) * even_odd_flag * jnp.cos(angle) / jnp.sin(angle)
        + VISCO * (OMEGA * OMEGA / 2.0) * even_odd_flag / jnp.sin(angle) ** 2
    )
    return jnp.where(offset == 0, VISCO * OMEGA * OMEGA * (count * count + 2.0) / 12.0, other)


def split_three(values):
    high = lax.reduce_precision(values, exponent_bits=8, mantissa_bits=7)
    rest = values - high
    middle = lax.reduce_precision(rest, exponent_bits=8, mantissa_bits=7)
    low = rest - middle
    return jnp.stack([high, middle, low]).astype(jnp.bfloat16)


def plane_gather(psi, onehot):
    comps, layers, plane = psi.shape
    parts = split_three(psi.reshape(comps * layers, plane))
    picked = jnp.einsum("pra,kba->kprb", parts, onehot,
                        preferred_element_type=jnp.float32)
    picked = (picked[:, 0] + picked[:, 1]) + picked[:, 2]
    return picked.reshape(onehot.shape[0], comps, layers, plane)


def cell_sum(weight, cell, layers, plane):
    by_layer = (cell // plane)[None, :] == jnp.arange(layers, dtype=jnp.int32)[:, None]
    spread = jnp.where(by_layer, weight[None, :], 0.0)
    picks = ((cell % plane)[:, None] == jnp.arange(plane, dtype=jnp.int32)[None, :]).astype(
        jnp.bfloat16
    )
    parts = split_three(spread)
    summed = jnp.einsum("plq,qb->plb", parts, picks, preferred_element_type=jnp.float32)
    return (summed[0] + summed[1]) + summed[2]


def greet(axis, peers):
    greet_all([{axis: peer} for peer in peers])


def greet_all(devices):
    barrier = pltpu.get_barrier_semaphore()
    for device in devices:
        pl.semaphore_signal(barrier, inc=1, device_id=device,
                            device_id_type=pl.DeviceIdType.MESH)
    pl.semaphore_wait(barrier, len(devices))


def coupling_kernel(count, inner, gather, psi_ref, table_ref, *refs):
    if gather:
        (block_ref, out_ref, below_ref, above_ref, stacked_ref, held, outbox, inbox, below, above,
         ring_send, ring_recv, cross_send, cross_recv, edge_send, edge_recv, gheld, gsend,
         grecv) = refs
    else:
        (out_ref, below_ref, above_ref, held, outbox, inbox, below, above, ring_send, ring_recv,
         cross_send, cross_recv, edge_send, edge_recv) = refs
    outer = count // inner
    me = lax.axis_index("inst")
    me_hi, me_lo = me // inner, me % inner
    steps = sorted(range(1, inner), key=lambda d: -min(d, inner - d))
    ring = [me_hi * inner + (me_lo + d) % inner for d in steps]
    ring_from = [me_hi * inner + (me_lo - d) % inner for d in steps]
    partners = [((me_hi + h) % outer) * inner + me_lo for h in range(1, outer)]
    slabs = lax.axis_size("space")
    here = lax.axis_index("space")
    up, down = (here + 1) % slabs, (here + slabs - 1) % slabs
    if gather:
        everyone = [(me + d) % count for d in range(1, count)]
        greet_all([{"inst": p} for p in everyone] + [{"space": up}, {"space": down}])
        gathered = []
        for slot, peer in enumerate(everyone):
            copy = pltpu.make_async_remote_copy(
                src_ref=block_ref.at[peer], dst_ref=gheld.at[me], send_sem=gsend.at[slot],
                recv_sem=grecv.at[slot], device_id={"inst": peer},
                device_id_type=pl.DeviceIdType.MESH)
            copy.start()
            gathered.append(copy)
    else:
        greet_all([{"inst": p} for p in ring + partners] + [{"space": up}, {"space": down}])
    last = psi_ref.shape[1] - 1
    edges = []
    for slot, (peer, layer, land) in enumerate(((up, last, below), (down, 0, above))):
        copy = pltpu.make_async_remote_copy(
            src_ref=psi_ref.at[:, pl.ds(layer, 1), :], dst_ref=land.at[:, pl.ds(layer, 1), :],
            send_sem=edge_send.at[slot], recv_sem=edge_recv.at[slot],
            device_id={"space": peer}, device_id_type=pl.DeviceIdType.MESH)
        copy.start()
        edges.append(copy)

    def coef(row, col):
        return table_ref[(row - col) % count]

    halves = PIECES
    width = psi_ref.shape[2] // halves
    spans = [pl.ds(h * width, width) for h in range(halves)]
    copies = []
    for h, cols in enumerate(spans):
        row = []
        for slot, peer in enumerate(ring):
            at = h * len(ring) + slot
            copy = pltpu.make_async_remote_copy(
                src_ref=psi_ref.at[:, :, cols], dst_ref=held.at[slot, :, :, cols],
                send_sem=ring_send.at[at], recv_sem=ring_recv.at[at],
                device_id={"inst": peer}, device_id_type=pl.DeviceIdType.MESH)
            copy.start()
            row.append(copy)
        copies.append(row)
    cross = []
    for h, cols in enumerate(spans):
        for copy in copies[h]:
            copy.wait()
        for slot, partner in enumerate(partners):
            at = h * len(partners) + slot
            part = coef(partner, me) * psi_ref[:, :, cols]
            for d, source in enumerate(ring_from):
                part = part + coef(partner, source) * held[d, :, :, cols]
            outbox[slot, :, :, cols] = part
            copy = pltpu.make_async_remote_copy(
                src_ref=outbox.at[slot, :, :, cols], dst_ref=inbox.at[slot, :, :, cols],
                send_sem=cross_send.at[at], recv_sem=cross_recv.at[at],
                device_id={"inst": partner}, device_id_type=pl.DeviceIdType.MESH)
            copy.start()
            cross.append((h, slot, copy))
    for h, cols in enumerate(spans):
        total = coef(me, me) * psi_ref[:, :, cols]
        for d, source in enumerate(ring_from):
            total = total + coef(me, source) * held[d, :, :, cols]
        out_ref[:, :, cols] = total
    for h, slot, copy in cross:
        copy.wait()
        out_ref[:, :, spans[h]] = out_ref[:, :, spans[h]] + inbox[slot, :, :, spans[h]]
    for copy in edges:
        copy.wait()
    below_ref[...] = below[:, last:, :]
    above_ref[...] = above[:, :1, :]
    if gather:
        for copy in gathered:
            copy.wait()
        gheld[me] = block_ref[me]
        stacked_ref[...] = gheld[...]


def instance_coupling(psi, table, step, block=None):
    count = lax.axis_size("inst")
    slabs = lax.axis_size("space")
    assert slabs > 2
    gather = block is not None
    inner = 4 if count % 4 == 0 else count
    outer = count // inner
    comps, layers, plane = psi.shape
    edge = jax.ShapeDtypeStruct((comps, 1, plane), psi.dtype)
    extra_out, extra_scratch, operands = (), [], (psi, table)
    if gather:
        extra_out = (jax.ShapeDtypeStruct(block.shape, block.dtype),)
        extra_scratch = [
            pltpu.VMEM(block.shape, block.dtype),
            pltpu.SemaphoreType.DMA((count - 1,)),
            pltpu.SemaphoreType.DMA((count - 1,)),
        ]
        operands = (psi, table, block)
    return pl.pallas_call(
        functools.partial(coupling_kernel, count, inner, gather),
        out_shape=(jax.ShapeDtypeStruct(psi.shape, psi.dtype), edge, edge) + extra_out,
        in_specs=[
            pl.BlockSpec(memory_space=pltpu.VMEM),
            pl.BlockSpec(memory_space=pltpu.SMEM),
        ] + [pl.BlockSpec(memory_space=pltpu.VMEM)] * gather,
        out_specs=[pl.BlockSpec(memory_space=pltpu.VMEM)] * (3 + gather),
        scratch_shapes=[
            pltpu.VMEM((inner - 1, *psi.shape), psi.dtype),
            pltpu.VMEM((max(outer - 1, 1), *psi.shape), psi.dtype),
            pltpu.VMEM((max(outer - 1, 1), *psi.shape), psi.dtype),
            pltpu.VMEM(psi.shape, psi.dtype),
            pltpu.VMEM(psi.shape, psi.dtype),
            pltpu.SemaphoreType.DMA((PIECES * (inner - 1),)),
            pltpu.SemaphoreType.DMA((PIECES * (inner - 1),)),
            pltpu.SemaphoreType.DMA((PIECES * max(outer - 1, 1),)),
            pltpu.SemaphoreType.DMA((PIECES * max(outer - 1, 1),)),
            pltpu.SemaphoreType.DMA((2,)),
            pltpu.SemaphoreType.DMA((2,)),
        ] + extra_scratch,
        compiler_params=pltpu.CompilerParams(collective_id=step, has_side_effects=True),
        name=f"instance_coupling_{step}",
    )(*operands)


def gather_kernel(count, block_ref, out_ref, held, send_sem, recv_sem):
    me = lax.axis_index("space")
    steps = sorted(range(1, count), key=lambda d: -min(d, count - d))
    peers = [(me + d) % count for d in steps]
    greet("space", peers)
    copies = []
    for slot, peer in enumerate(peers):
        copy = pltpu.make_async_remote_copy(
            src_ref=block_ref, dst_ref=held.at[me], send_sem=send_sem.at[slot],
            recv_sem=recv_sem.at[slot], device_id={"space": peer},
            device_id_type=pl.DeviceIdType.MESH)
        copy.start()
        copies.append(copy)
    for copy in copies:
        copy.wait()
    held[me] = block_ref[...]
    out_ref[...] = held[...]


def space_gather(block, collective):
    count = lax.axis_size("space")
    return pl.pallas_call(
        functools.partial(gather_kernel, count),
        out_shape=jax.ShapeDtypeStruct((count, *block.shape), block.dtype),
        in_specs=[pl.BlockSpec(memory_space=pltpu.VMEM)],
        out_specs=pl.BlockSpec(memory_space=pltpu.VMEM),
        scratch_shapes=[
            pltpu.VMEM((count, *block.shape), block.dtype),
            pltpu.SemaphoreType.DMA((count - 1,)),
            pltpu.SemaphoreType.DMA((count - 1,)),
        ],
        compiler_params=pltpu.CompilerParams(collective_id=collective, has_side_effects=True),
        name="space_gather",
    )(block)


def route_kernel(count, rows_ref, out_ref, held, send_sem, recv_sem):
    me = lax.axis_index("inst")
    peers = [(me + d) % count for d in range(1, count)]
    greet("inst", peers)
    copies = []
    for slot, peer in enumerate(peers):
        copy = pltpu.make_async_remote_copy(
            src_ref=rows_ref.at[peer], dst_ref=held.at[me], send_sem=send_sem.at[slot],
            recv_sem=recv_sem.at[slot], device_id={"inst": peer},
            device_id_type=pl.DeviceIdType.MESH)
        copy.start()
        copies.append(copy)
    for copy in copies:
        copy.wait()
    held[me] = rows_ref[me]
    out_ref[...] = held[...]


def inst_route(rows, collective):
    count = lax.axis_size("inst")
    return pl.pallas_call(
        functools.partial(route_kernel, count),
        out_shape=jax.ShapeDtypeStruct(rows.shape, rows.dtype),
        in_specs=[pl.BlockSpec(memory_space=pltpu.VMEM)],
        out_specs=pl.BlockSpec(memory_space=pltpu.VMEM),
        scratch_shapes=[
            pltpu.VMEM(rows.shape, rows.dtype),
            pltpu.SemaphoreType.DMA((count - 1,)),
            pltpu.SemaphoreType.DMA((count - 1,)),
        ],
        compiler_params=pltpu.CompilerParams(collective_id=collective, has_side_effects=True),
        name="inst_route",
    )(rows)


def shards(
    psi_start,
    density,
    velocity,
    pressure,
    obs_pos,
    obs_weight,
    obs_harmonic,
    panel_pos,
    panel_normal,
    panel_cell,
    plane_nbr,
):
    inst_count = lax.axis_size("inst")
    inst_id = lax.axis_index("inst")
    space_id = lax.axis_index("space")
    times = jnp.array([2.0 * math.pi * i / inst_count for i in range(inst_count)], jnp.float32)
    local_obs = jnp.concatenate(
        [obs_pos, obs_weight, obs_harmonic[None].astype(jnp.float32)], axis=0
    )
    rows, per = local_obs.shape
    assert rows <= 8 and per <= 128
    packed = jnp.zeros((8, 128), jnp.float32).at[:rows, :per].set(local_obs)
    psi = psi_start[:, 0]
    row_entry = spectral_coeff(
        jnp.arange(inst_count, dtype=jnp.int32).astype(jnp.float32), float(inst_count)
    )
    stacked = space_gather(packed, ITERS)
    observers = stacked[:, :rows, :per].transpose(1, 0, 2).reshape(rows, -1)
    owned_count = panel_normal.shape[1]
    piece = owned_count // inst_count
    assert piece * inst_count == owned_count and piece % 128 == 0
    mine = lax.dynamic_slice_in_dim(
        panel_pos, space_id * owned_count + inst_id * piece, piece, 1
    )
    normal = lax.dynamic_slice_in_dim(panel_normal, inst_id * piece, piece, 1)
    delta = mine[:, None, :] - observers[:3, :, None]
    dist2 = jnp.sum(delta * delta, axis=0)
    dist = jnp.sqrt(dist2)
    harm = observers[5]
    lag = harm[:, None] * (KWAVE * dist)
    along = jnp.sum(delta * normal[:, None, :], axis=0) * (RADIUS * RADIUS) / (dist2 * dist)
    pairs = jnp.concatenate([along * jnp.cos(lag), along * jnp.sin(lag)], axis=0)
    beat = times[:, None] * harm[None, :]
    cos_beat, sin_beat = jnp.cos(beat), jnp.sin(beat)
    real, imag = observers[3][None, :], observers[4][None, :]
    mixes = jnp.concatenate(
        [real * cos_beat + imag * sin_beat, real * sin_beat - imag * cos_beat], axis=1
    )
    partial = jnp.dot(mixes, pairs, precision=lax.Precision.HIGHEST)
    first = instance_coupling(psi, row_entry, 0, partial.reshape(inst_count, piece // 128, 128))
    routed = first[3]
    weight = routed.reshape(owned_count)
    layers = psi_start.shape[2]
    plane = psi_start.shape[3]
    wall = cell_sum(weight, panel_cell, layers, plane)
    dens = density[0]
    vel = velocity[:, 0]
    state = conserved(dens, vel, pressure[0])
    slope = jnp.concatenate(
        [0.5 * jnp.sum(vel * vel, axis=0)[None], -vel, jnp.ones_like(dens)[None]], axis=0
    ) * (GAMMA - 1.0)
    source = slope * wall[None]
    _, pull = jax.vjp(fluxes, state)
    onehot = (plane_nbr[:, :, None] == jnp.arange(plane, dtype=jnp.int32)[None, None, :]).astype(
        jnp.bfloat16
    )
    for step in range(ITERS):
        if step == 0:
            spectral_operator, below, above = first[:3]
        else:
            spectral_operator, below, above = instance_coupling(psi, row_entry, step)
        minus_a = jnp.concatenate([below, psi[:, :-1]], axis=1)
        plus_a = jnp.concatenate([psi[:, 1:], above], axis=1)
        plus_y, minus_y, plus_z, minus_z = plane_gather(psi, onehot)
        middle_point = pull(
            (0.5 * (minus_a - plus_a), 0.5 * (minus_y - plus_y), 0.5 * (minus_z - plus_z))
        )[0]
        spread = 6.0 * psi - (minus_a + plus_a + plus_y + minus_y + plus_z + minus_z)
        psi = psi - TAU * (middle_point + DISSIP * spread + spectral_operator + source)
    return psi[:, None]


def solution(mesh):
    placed = (
        P(None, "inst", "space", None),
        P("inst", "space", None),
        P(None, "inst", "space", None),
        P("inst", "space", None),
        P(None, "space"),
        P(None, "space"),
        P("space"),
        P(),
        P(None, "space"),
        P("space"),
        P(),
    )
    return jax.shard_map(
        shards,
        mesh=mesh,
        in_specs=placed,
        out_specs=P(None, "inst", "space", None),
        check_vma=False,
    )
```
